32 devices in a mesh: dp: 8 (over y, x, core), tensor: 4 (over z).
Axes of the slice: x: 2, y: 2, z: 4, core: 2. Of those that a mesh axis runs over, the one named last changes fastest.
Arguments:
- x_in: bfloat16 [16384, 1536], P(('dp', 'tensor')), may hold values from -6 to 6
- segment_ids: int32 [16, 1024], P('dp'), may hold values from 0 to 11, never falling along the last dimension, each value on 1 to 512 neighbouring positions
- norm_gain: bfloat16 [1536], P('dp'), may hold values from 0.099609375 to 1.8984375
- w_x: bfloat16 [1536, 3072], P('dp', 'tensor'), may hold values from -0.15625 to 0.15625
- w_z: bfloat16 [1536, 3072], P('dp', 'tensor'), may hold values from -0.15625 to 0.15625
- w_bc: bfloat16 [1536, 256], P('dp'), may hold values from -0.15625 to 0.15625
- w_dt: bfloat16 [1536, 48], P('dp', 'tensor'), may hold values from -0.15625 to 0.15625
- conv_x: float32 [4, 3072], P(None, 'tensor'), may hold values from -3 to 3
- conv_x_bias: float32 [3072], P('tensor'), may hold values from -3 to 3
- conv_bc: float32 [4, 256], replicated, may hold values from -3 to 3
- conv_bc_bias: float32 [256], replicated, may hold values from -3 to 3
- dt_bias: float32 [48], P('tensor'), may hold values from -6 to -2
- a_log: float32 [48], P('tensor'), may hold values from 0 to 2.77
- d_skip: float32 [48], P('tensor'), may hold values from 0.5 to 1.5
- gate_gain: float32 [3072], P('tensor'), may hold values from 0.1 to 1.9
- w_out: bfloat16 [3072, 1536], P('tensor', 'dp'), may hold values from -0.109375 to 0.109375
- cotangent: bfloat16 [16384, 1536], P(('dp', 'tensor')), may hold values from -6 to 6
Outputs:
- block_out: bfloat16 [16384, 1536], P(('dp', 'tensor'))
- x_grad: float32 [16384, 1536], P(('dp', 'tensor'))
- norm_gain_grad: float32 [1536], P('dp')
- w_x_grad: float32 [1536, 3072], P('dp', 'tensor')
- w_z_grad: float32 [1536, 3072], P('dp', 'tensor')
- w_bc_grad: float32 [1536, 256], P('dp')
- w_dt_grad: float32 [1536, 48], P('dp', 'tensor')
- conv_x_grad: float32 [4, 3072], P(None, 'tensor')
- conv_x_bias_grad: float32 [3072], P('tensor')
- conv_bc_grad: float32 [4, 256], replicated
- conv_bc_bias_grad: float32 [256], replicated
- dt_bias_grad: float32 [48], P('tensor')
- a_log_grad: float32 [48], P('tensor')
- d_skip_grad: float32 [48], P('tensor')
- gate_gain_grad: float32 [3072], P('tensor')
- w_out_grad: float32 [3072, 1536], P('tensor', 'dp')
The draws below stay inside these ranges and needn't reach their ends.
Inputs may be any that keep to these rules, and one draw needn't show every extreme that they name: `segment_ids`: within each sequence the document numbers never fall; every document has 1 to 512 tokens and one of each sequence has exactly 512.
All inputs are finite; a program needn't handle non-finite values.
Results may differ from the reference program's by a relative error of at most 0.017.
Values may be sent and summed in bfloat16 or wider, within the bound.
No kernel may reach another device: no remote copies, remote signals or barrier semaphores. Data moves between devices by JAX's collectives and lax.ppermute only.
A program may use at most 256 MiB of HBM per device.

```python
import math
from functools import partial
import jax
import jax.numpy as jnp
import numpy as np
from jax import lax

D = 1536
H = 48
N = 128
K = 4
CH = 256
LEN = 1024
SEQ_DEV = 2
SEGS = 12
SEG_MOST = 512
DI = 3072
NSEQ = 16
TOKENS = 16384


def level_of(key, extent, split, smallest, top_value):
    gain = 1.0
    for axis_at, blocks in split:
        draws = jax.random.uniform(jax.random.fold_in(jax.random.fold_in(key, 6), axis_at), (blocks,), jnp.float32, smallest / len(split), top_value / len(split))
        gain = gain * jnp.repeat(jnp.exp(draws), extent[axis_at] // blocks).reshape((-1,) + (1,) * (len(extent) - 1 - axis_at))
    return gain


def split_up(amount, total, bound, lean):
    portions = [(1 << 20) // math.isqrt(rank ** lean) + 1 for rank in range(2, amount + 1)]
    spare, given = total - bound - (amount - 1), [1] * (amount - 1)
    while spare > 0:
        candidates = [i for i in range(amount - 1) if given[i] < bound]
        pool, remaining = sum([portions[i] for i in candidates]), spare
        for i in candidates:
            extra = min(bound - given[i], max(1, remaining * portions[i] // pool), spare)
            given[i] = given[i] + extra
            spare = spare - extra
    return np.array([bound] + given)


def uneven_parts(rng, number_of, total, most, lean):
    if number_of == 2:
        one = jax.random.randint(rng, (), max(1, total - most), min(most, total - 1) + 1)
        return jnp.stack([one, total - one])
    tallies = jnp.asarray(split_up(number_of, total, most, lean), jnp.int32)
    twos = (number_of - 1) // 2
    donor, sink = tallies[1:1 + 2 * twos:2], tallies[2:2 + 2 * twos:2]
    margin = jnp.minimum(donor - 1, most - sink)
    moved = jax.random.randint(jax.random.fold_in(rng, 1), (twos,), 0, 1 << 20) % (margin + 1)
    tallies = tallies.at[1:1 + 2 * twos:2].set(donor - moved).at[2:2 + 2 * twos:2].set(sink + moved)
    return tallies[jax.random.permutation(jax.random.fold_in(rng, 2), number_of)]


def scatter_about(stream_key, dims, spread, reach, cuts=(), kind=jnp.bfloat16):
    values = jax.random.normal(stream_key, dims, jnp.float32) * spread
    if len(cuts) > 0:
        values = level_of(stream_key, dims, cuts, -0.22, 0.18) * values
    return jnp.clip(values, min=-reach, max=reach).astype(kind)


def setup_inputs(seed: int = 0) -> dict:
    key_of = jax.random.split(jax.random.key(seed), 18)
    return {
        "x_in": scatter_about(key_of[0], (TOKENS, D), 1.0, 6.0, ((0, 32),)),
        "segment_ids": jax.vmap(lambda own: jnp.searchsorted(jnp.cumsum(uneven_parts(own, SEGS, LEN, SEG_MOST, 2)), jnp.arange(LEN), side="right"))(jax.random.split(key_of[1], NSEQ)).reshape((NSEQ, LEN)).astype(jnp.int32),
        "norm_gain": jnp.clip(1.0 + 0.18 * jax.random.normal(key_of[2], (D,), jnp.float32), 0.099609375, 1.8984375).astype(jnp.bfloat16),
        "w_x": scatter_about(key_of[3], (D, DI), D ** -0.5, 0.15625, ((0, 8), (1, 4))),
        "w_z": scatter_about(key_of[4], (D, DI), D ** -0.5, 0.15625, ((0, 8), (1, 4))),
        "w_bc": scatter_about(key_of[5], (D, 2 * N), D ** -0.5, 0.15625, ((0, 8),)),
        "w_dt": scatter_about(key_of[6], (D, H), D ** -0.5, 0.15625, ((0, 8), (1, 4))),
        "conv_x": scatter_about(key_of[7], (K, DI), K ** -0.5, 3.0, ((1, 4),), jnp.float32),
        "conv_x_bias": scatter_about(key_of[8], (DI,), 0.5, 3.0, ((0, 4),), jnp.float32),
        "conv_bc": scatter_about(key_of[9], (K, 2 * N), K ** -0.5, 3.0, (), jnp.float32),
        "conv_bc_bias": scatter_about(key_of[10], (2 * N,), 0.5, 3.0, (), jnp.float32),
        "dt_bias": jnp.clip(-6.0 + 4.0 * jax.random.uniform(key_of[11], (H,), jnp.float32) ** level_of(key_of[11], (H,), ((0, 4),), -0.2, 0.2), -6.0, -2.0),
        "a_log": jnp.clip(2.77 * jax.random.uniform(key_of[12], (H,), jnp.float32) ** level_of(key_of[12], (H,), ((0, 4),), -0.2, 0.2), 0.0, 2.77),
        "d_skip": jnp.clip(0.5 + 1.0 * jax.random.uniform(key_of[13], (H,), jnp.float32) ** level_of(key_of[13], (H,), ((0, 4),), -0.2, 0.2), 0.5, 1.5),
        "gate_gain": jnp.clip(1.0 + 0.18 * jax.random.normal(key_of[14], (DI,), jnp.float32), 0.1, 1.9),
        "w_out": scatter_about(key_of[15], (DI, D), DI ** -0.5, 0.109375, ((0, 4), (1, 8))),
        "cotangent": scatter_about(key_of[16], (TOKENS, D), 1.0, 6.0, ((0, 32),)),
    }


epsilon = 1e-05
highest = lax.Precision.HIGHEST

@jax.custom_vjp
def low(v):
    return lax.optimization_barrier(v.astype(jnp.bfloat16)).astype(jnp.float32)

@jax.custom_vjp
def low_back(v):
    return v

def low_keep(v):
    return (low(v), None)

def low_pass(kept, grad):
    return (grad,)

def back_keep(v):
    return (v, None)

def back_low(kept, grad):
    return (low(grad),)
low.defvjp(low_keep, low_pass)
low_back.defvjp(back_keep, back_low)

def conv_reset(values, segments, weights, biases):
    length = values.shape[1]
    running_sum = biases + weights[0] * values
    for shift_by in range(1, weights.shape[0]):
        shifted = jnp.pad(values, ((0, 0), (shift_by, 0), (0, 0)))[:, :length]
        shifted_ids = jnp.pad(segments, ((0, 0), (shift_by, 0)), constant_values=-1)[:, :length]
        valid_tap = (shifted_ids == segments).astype(values.dtype)
        running_sum = running_sum + weights[shift_by] * shifted * valid_tap[:, :, None]
    return running_sum

def block_step(carry, item):
    state_mat, previous = carry
    values, step_sizes, b_rows, c_rows, doc_ids, decay_rate = item
    log_decay = step_sizes * decay_rate[None, :]
    running = jnp.cumsum(log_decay, axis=0)
    positions = jnp.arange(doc_ids.shape[0])
    same_doc = (doc_ids[:, None] == doc_ids[None, :]) & (positions[:, None] >= positions[None, :])
    log_gaps = running.T[:, :, None] - running.T[:, None, :]
    log_gaps = jnp.where(same_doc[None], log_gaps, 0.0)
    decay_mat = jnp.exp(log_gaps) * same_doc[None].astype(values.dtype)
    scores = jnp.dot(c_rows, b_rows.T, precision=highest, preferred_element_type=jnp.float32)
    mixing = scores[None] * decay_mat * step_sizes.T[:, None, :]
    inner_part = jnp.einsum('hts,shp->thp', mixing, values, precision=highest)
    carried = (doc_ids == previous).astype(values.dtype)
    from_state = jnp.einsum('tn,hpn->thp', c_rows, state_mat, precision=highest)
    outer_part = from_state * (carried[:, None] * jnp.exp(running))[:, :, None]
    final_log = running[-1]
    keep_end = (doc_ids == doc_ids[-1]).astype(values.dtype)
    weights_end = jnp.exp(final_log[None, :] - running) * step_sizes * keep_end[:, None]
    update = jnp.einsum('sh,shp,sn->hpn', weights_end, values, b_rows, precision=highest)
    still_open = (doc_ids[-1] == previous).astype(values.dtype)
    new_state = still_open * jnp.exp(final_log)[:, None, None] * state_mat + update
    return ((new_state, doc_ids[-1]), inner_part + outer_part)

def block_scan(values, step_sizes, decay_rate, b_rows, c_rows, doc_ids, block_len):
    length, head_count, head_size = values.shape
    state_size = b_rows.shape[1]
    block_count = length // block_len
    items = (values.reshape(block_count, block_len, head_count, head_size), step_sizes.reshape(block_count, block_len, head_count), b_rows.reshape(block_count, block_len, state_size), c_rows.reshape(block_count, block_len, state_size), doc_ids.reshape(block_count, block_len))

    def step_with_rate(carry, item):
        return block_step(carry, item + (decay_rate,))
    start_state = (jnp.zeros((head_count, head_size, state_size), values.dtype), jnp.array(-1, dtype=jnp.int32))
    final_carry, pieces = lax.scan(jax.checkpoint(step_with_rate), start_state, items)
    return pieces.reshape(length, head_count, head_size)

def bc_branch(bc_proj, conv_bc, conv_bc_bias, segments):
    seq_count, length = segments.shape
    widths = bc_proj.shape[1]
    bc_seq = conv_reset(bc_proj.reshape(seq_count, length, widths), segments, conv_bc, conv_bc_bias)
    return jax.nn.silu(bc_seq).reshape(seq_count * length, widths)

def mix_heads(x_proj, bc_act, dt_proj, conv_x, conv_x_bias, dt_bias, a_log, d_skip, segments, block_len):
    seq_count, length = segments.shape
    channels = x_proj.shape[1]
    head_count = dt_proj.shape[1]
    head_size = channels // head_count
    state_size = bc_act.shape[1] // 2
    x_act = jax.nn.silu(conv_reset(x_proj.reshape(seq_count, length, channels), segments, conv_x, conv_x_bias))
    values = x_act.reshape(seq_count, length, head_count, head_size)
    step_sizes = jax.nn.softplus(dt_proj + dt_bias).reshape(seq_count, length, head_count)
    decay_rate = -jnp.exp(a_log)
    bc_seq = bc_act.reshape(seq_count, length, 2 * state_size)
    scanner = jax.vmap(partial(block_scan, block_len=block_len), in_axes=(0, 0, None, 0, 0, 0))
    scanned = scanner(values, step_sizes, decay_rate, bc_seq[:, :, :state_size], bc_seq[:, :, state_size:], segments)
    result = scanned + d_skip[None, None, :, None] * values
    return result.reshape(seq_count * length, channels)

def forward(tokens, segments, norm_gain, w_x, w_z, w_bc, w_dt, conv_x, conv_x_bias, conv_bc, conv_bc_bias, dt_bias, a_log, d_skip, gate_gain, w_out):
    inv_rms = lax.rsqrt(lax.optimization_barrier(jnp.mean(tokens * tokens, axis=-1, keepdims=True)) + epsilon)
    normed = low(tokens * inv_rms * norm_gain)
    x_proj = low_back(jnp.dot(normed, w_x, precision=highest, preferred_element_type=jnp.float32))
    gate_in = low_back(jnp.dot(normed, w_z, precision=highest, preferred_element_type=jnp.float32))
    bc_proj = low_back(jnp.dot(normed, w_bc, precision=highest, preferred_element_type=jnp.float32))
    dt_proj = low_back(jnp.dot(normed, w_dt, precision=highest, preferred_element_type=jnp.float32))
    bc_act = bc_branch(bc_proj, conv_bc, conv_bc_bias, segments)
    mixed_y = mix_heads(x_proj, bc_act, dt_proj, conv_x, conv_x_bias, dt_bias, a_log, d_skip, segments, CH)
    gated = mixed_y * jax.nn.silu(gate_in)
    gate_rms = lax.rsqrt(lax.optimization_barrier(jnp.mean(gated * gated, axis=-1, keepdims=True)) + epsilon)
    mixed = low(gated * gate_rms * gate_gain)
    return tokens + jnp.dot(mixed, w_out, precision=highest, preferred_element_type=jnp.float32)

def reference(x_in, segment_ids, norm_gain, w_x, w_z, w_bc, w_dt, conv_x, conv_x_bias, conv_bc, conv_bc_bias, dt_bias, a_log, d_skip, gate_gain, w_out, cotangent):
    params = tuple((item.astype(jnp.float32) for item in (norm_gain, w_x, w_z, w_bc, w_dt, conv_x, conv_x_bias, conv_bc, conv_bc_bias, dt_bias, a_log, d_skip, gate_gain, w_out)))
    group_rows = SEQ_DEV * LEN
    group_count = x_in.shape[0] // group_rows
    inputs = x_in.astype(jnp.float32).reshape(group_count, group_rows, D)
    tangents = cotangent.astype(jnp.float32).reshape(group_count, group_rows, D)
    grouped_ids = segment_ids.reshape(group_count, SEQ_DEV, LEN)

    def group_step(totals, item):
        tokens, segments, tangent = item

        def forward_only(tokens_in, *weights):
            return forward(tokens_in, segments, *weights)
        result, pullback = jax.vjp(forward_only, tokens, *params)
        grads = pullback(tangent)
        totals = tuple((total_now + grad_now for total_now, grad_now in zip(totals, grads[1:])))
        return (totals, (result.astype(jnp.bfloat16), grads[0]))
    zeros_start = tuple((jnp.zeros(item.shape, jnp.float32) for item in params))
    totals, stacked = lax.scan(group_step, zeros_start, (inputs, grouped_ids, tangents))
    outputs, input_grads = stacked
    return (outputs.reshape(group_count * group_rows, D), input_grads.reshape(group_count * group_rows, D), totals[0], totals[1], totals[2], totals[3], totals[4], totals[5], totals[6], totals[7], totals[8], totals[9], totals[10], totals[11], totals[12], totals[13])
```

```python
import jax
import jax.numpy as jnp
from jax import lax
from jax.experimental import pallas as pl
from jax.experimental.pallas import tpu as pltpu
from jax.sharding import PartitionSpec as P

CH = 256
HALO = 16
GROUP = 4
LOG2E = 1.4426950408889634
epsilon = 1e-05
f32 = jnp.float32
bf16 = jnp.bfloat16
highest = lax.Precision.HIGHEST


def mm(a, b):
    return lax.dot_general(a, b, (((1,), (0,)), ((), ())), preferred_element_type=f32)


def mmt(a, b):
    return lax.dot_general(a, b, (((1,), (1,)), ((), ())), preferred_element_type=f32)


def tmm(a, b):
    return lax.dot_general(a, b, (((0,), (0,)), ((), ())), preferred_element_type=f32)


def exact(a, b):
    return lax.dot_general(
        a, b, (((1,), (0,)), ((), ())), precision=highest, preferred_element_type=f32
    )


def head_map(channels, kind):
    return (jnp.arange(channels)[:, None] // 64 == jnp.arange(128)[None, :]).astype(kind)


def spread(cols, first, rows, lane_low):
    parts = []
    for pair in range(GROUP // 2):
        left = jnp.broadcast_to(cols[:, first + 2 * pair : first + 2 * pair + 1], (rows, 128))
        right = jnp.broadcast_to(cols[:, first + 2 * pair + 1 : first + 2 * pair + 2], (rows, 128))
        parts.append(jnp.where(lane_low, left, right))
    return jnp.concatenate(parts, axis=1)


def conv_pre(x_ref, cw_ref, flags, start, rows):
    pre = cw_ref[4:5, :] + cw_ref[0:1, :] * x_ref[0, HALO + start : HALO + start + rows, :]
    for k in range(1, 4):
        shifted = x_ref[0, HALO + start - k : HALO + start - k + rows, :]
        pre = pre + (cw_ref[k : k + 1, :] * shifted) * flags[:, k - 1 : k]
    return pre


def masked_scores(cb_ref, bc_ref, fl_ref, rv_ref, n_chunks, rows):
    for c in range(n_chunks):
        at = slice(c * rows, (c + 1) * rows)
        ids_col = fl_ref[0, at, 3:4]
        ids_row = rv_ref[0, 24:25, at]
        t_at = lax.broadcasted_iota(jnp.int32, (rows, rows), 0)
        s_at = lax.broadcasted_iota(jnp.int32, (rows, rows), 1)
        keep = (ids_col == ids_row) & (t_at >= s_at)
        scores = lax.dot_general(
            bc_ref[0, at, 128:], bc_ref[0, at, :128], (((1,), (1,)), ((), ())),
            precision=highest, preferred_element_type=f32,
        )
        cb_ref[c] = jnp.where(keep, scores, 0.0)


def scan_fwd_body(n_chunks, rows, hv_ref, fl_ref, rv_ref, al_ref, bc_ref, bt_ref, x_ref, cw_ref, y_ref, st_ref, cb_ref):
    group = pl.program_id(1)
    turn = lax.rem(128 - GROUP * group, 128)

    @pl.when(group == 0)
    def _():
        masked_scores(cb_ref, bc_ref, fl_ref, rv_ref, n_chunks, rows)

    lane_low = lax.broadcasted_iota(jnp.int32, (rows, 128), 1) < 64
    state = jnp.zeros((128, GROUP * 64), f32)
    for c in range(n_chunks):
        at = slice(c * rows, (c + 1) * rows)
        cols = pltpu.roll(hv_ref[0, at, :], turn, 1)
        flags = fl_ref[0, at, :]
        pre = conv_pre(x_ref, cw_ref, flags, c * rows, rows)
        act = pre * jax.nn.sigmoid(pre)
        u = act * spread(cols, 32, rows, lane_low)
        ub = u.astype(bf16)
        y = cw_ref[5:6, :] * act
        if c > 0:
            c_rows = bc_ref[0, at, 128:].astype(bf16)
            y = y + mm(c_rows, state.astype(bf16)) * spread(cols, 64, rows, lane_low)
        scores = cb_ref[c]
        parts = []
        for pair in range(GROUP // 2):
            u_pair = ub[:, 128 * pair : 128 * pair + 128]
            outs = []
            for j in (2 * pair, 2 * pair + 1):
                gap = cols[:, j : j + 1] - rv_ref[0, pl.ds(group * GROUP + j, 1), at]
                mix = (scores * jnp.exp2(jnp.minimum(gap, 0.0))).astype(bf16)
                outs.append(mm(mix, u_pair))
            parts.append(jnp.where(lane_low, outs[0], outs[1]))
        y_ref[0, at, :] = y + jnp.concatenate(parts, axis=1)
        wu = (u * spread(cols, 96, rows, lane_low)).astype(bf16)
        state = al_ref[0, c : c + 1, :] * state + mm(bt_ref[0, :128, at], wu)
        st_ref[0, c] = state


def scan_fwd(hv, fl, rv, al, bc, bt, x_ext, cw, rows):
    pieces, length, _ = hv.shape
    n_chunks = length // rows
    width = GROUP * 64
    channels = x_ext.shape[2]
    groups = channels // width
    return pl.pallas_call(
        lambda *refs: scan_fwd_body(n_chunks, rows, *refs),
        grid=(pieces, groups),
        in_specs=[
            pl.BlockSpec((1, length, 128), lambda s, g: (s, 0, 0)),
            pl.BlockSpec((1, length, 8), lambda s, g: (s, 0, 0)),
            pl.BlockSpec((1, 32, length), lambda s, g: (s, 0, 0)),
            pl.BlockSpec((1, 8, width), lambda s, g: (s, 0, g)),
            pl.BlockSpec((1, length, 256), lambda s, g: (s, 0, 0)),
            pl.BlockSpec((1, 256, length), lambda s, g: (s, 0, 0)),
            pl.BlockSpec((1, HALO + length, width), lambda s, g: (s, 0, g)),
            pl.BlockSpec((8, width), lambda s, g: (0, g)),
        ],
        out_specs=[
            pl.BlockSpec((1, length, width), lambda s, g: (s, 0, g)),
            pl.BlockSpec((1, n_chunks, 128, width), lambda s, g: (s, 0, 0, g)),
        ],
        out_shape=[
            jax.ShapeDtypeStruct((pieces, length, channels), f32),
            jax.ShapeDtypeStruct((pieces, n_chunks, 128, channels), f32),
        ],
        scratch_shapes=[pltpu.VMEM((n_chunks, rows, rows), f32)],
        cost_estimate=pl.CostEstimate(
            flops=pieces * groups * GROUP * length * (rows + 256) * 128 * 2,
            transcendentals=pieces * groups * GROUP * length * rows,
            bytes_accessed=pieces * length * channels * 8,
        ),
        name="scan_fwd",
    )(hv, fl, rv, al, bc, bt, x_ext, cw)


def scan_bwd_body(
    n_chunks, rows, hv_ref, fl_ref, rv_ref, al_ref, bc_ref, bt_ref, x_ref, cw_ref, dy_ref, st_ref, sr_ref, rr_ref, seg_ref,
    xl_ref, tail_ref, head_ref, dbc_ref, dcol_ref, drow_ref, dcw_ref, cb_ref, dcb_ref, dpre_ref,
):
    group = pl.program_id(1)
    turn = lax.rem(128 - GROUP * group, 128)
    length = n_chunks * rows
    width = GROUP * 64

    @pl.when(group == 0)
    def _():
        masked_scores(cb_ref, bc_ref, fl_ref, rv_ref, n_chunks, rows)
        dcb_ref[...] = jnp.zeros_like(dcb_ref)
        dbc_ref[...] = jnp.zeros_like(dbc_ref)
        dcol_ref[...] = jnp.zeros_like(dcol_ref)
        drow_ref[...] = jnp.zeros_like(drow_ref)

    lane_low = lax.broadcasted_iota(jnp.int32, (rows, 128), 1) < 64
    lane = lax.broadcasted_iota(jnp.int32, (rows, 128), 1)
    row_at = lax.broadcasted_iota(jnp.int32, (rows, width), 0)
    grad_state = rr_ref[0].astype(f32)
    recv = sr_ref[0].astype(f32)
    states = [recv]
    carry = recv
    for c in range(n_chunks - 1):
        carry = al_ref[0, c : c + 1, :] * carry
        states.append(st_ref[0, c] + carry)
    tap_sums = [jnp.zeros((1, width), f32) for _ in range(6)]
    dpre_ref[length : length + 8, :] = jnp.zeros((8, width), f32)
    for c in reversed(range(n_chunks)):
        at = slice(c * rows, (c + 1) * rows)
        cols = pltpu.roll(hv_ref[0, at, :], turn, 1)
        flags = fl_ref[0, at, :]
        pre = conv_pre(x_ref, cw_ref, flags, c * rows, rows)
        sig = jax.nn.sigmoid(pre)
        act = pre * sig
        step_wide = spread(cols, 32, rows, lane_low)
        end_wide = spread(cols, 96, rows, lane_low)
        u = act * step_wide
        ub = u.astype(bf16)
        dy = dy_ref[0, at, :]
        dyb = dy.astype(bf16)
        b_rows = bc_ref[0, at, :128].astype(bf16)
        c_rows = bc_ref[0, at, 128:].astype(bf16)
        state_b = states[c].astype(bf16)
        dye = dy * spread(cols, 64, rows, lane_low)
        dyeb = dye.astype(bf16)
        gs_b = grad_state.astype(bf16)
        wub = (u * end_wide).astype(bf16)
        dbc_ref[0, at, 128:] += mmt(dyeb, state_b)
        dbc_ref[0, at, :128] += mmt(wub, gs_b)
        du_state = mm(b_rows, gs_b) * end_wide
        u_du = u * du_state
        at_end = jnp.sum(u_du, axis=0, keepdims=True) + al_ref[0, c : c + 1, :] * jnp.sum(
            grad_state * states[c], axis=0, keepdims=True
        )
        log_grad = dye * mm(c_rows, state_b) - u_du
        log_grad = jnp.where(row_at == rows - 1, log_grad + at_end, log_grad)
        grad_state = al_ref[0, c : c + 1, :] * grad_state + mm(bt_ref[0, 128:, at], dyeb)
        scores = cb_ref[c]
        dcb = dcb_ref[c]
        parts = []
        row_sums = jnp.zeros((rows, 128), f32)
        for pair in range(GROUP // 2):
            lanes = slice(128 * pair, 128 * pair + 128)
            u_pair = ub[:, lanes]
            dy_pair = dyb[:, lanes]
            outs = []
            for j in (2 * pair, 2 * pair + 1):
                gap = cols[:, j : j + 1] - rv_ref[0, pl.ds(group * GROUP + j, 1), at]
                decay = jnp.exp2(jnp.minimum(gap, 0.0))
                mix = (scores * decay).astype(bf16)
                own = lane_low if j % 2 == 0 else jnp.logical_not(lane_low)
                prod = mmt(jnp.where(own, dy_pair, jnp.zeros_like(dy_pair)), u_pair) * decay
                dcb = dcb + prod
                full = prod * scores
                row_sums = jnp.where(
                    lane == group * GROUP + j, jnp.sum(full, axis=1, keepdims=True), row_sums
                )
                drow_ref[0, pl.ds(group * GROUP + j, 1), at] = jnp.sum(full, axis=0, keepdims=True)
                outs.append(tmm(mix, dy_pair))
            parts.append(jnp.where(lane_low, outs[0], outs[1]))
        dcb_ref[c] = dcb
        du = jnp.concatenate(parts, axis=1) + du_state
        seg = seg_ref[...]
        dcol_ref[0, at, :128] += row_sums + lax.dot_general(
            log_grad, seg, (((1,), (0,)), ((), ())), precision=highest, preferred_element_type=f32
        )
        dcol_ref[0, at, 128:] += lax.dot_general(
            du * act, seg, (((1,), (0,)), ((), ())), precision=highest, preferred_element_type=f32
        )
        dact = du * step_wide + cw_ref[5:6, :] * dy
        dpre = dact * (sig * (1.0 + pre * (1.0 - sig)))
        dpre_ref[at, :] = dpre
        tap_sums[0] += jnp.sum(dpre * x_ref[0, HALO + c * rows : HALO + (c + 1) * rows, :], axis=0, keepdims=True)
        for k in range(1, 4):
            shifted = x_ref[0, HALO + c * rows - k : HALO + (c + 1) * rows - k, :]
            tap_sums[k] += jnp.sum(dpre * flags[:, k - 1 : k] * shifted, axis=0, keepdims=True)
        tap_sums[4] += jnp.sum(dpre, axis=0, keepdims=True)
        tap_sums[5] += jnp.sum(dy * act, axis=0, keepdims=True)
        xg = cw_ref[0:1, :] * dpre
        for k in range(1, 4):
            xg = xg + (cw_ref[k : k + 1, :] * dpre_ref[c * rows + k : (c + 1) * rows + k, :]) * flags[:, 3 + k : 4 + k]
        xl_ref[0, at, :] = xg.astype(bf16)
        if c == n_chunks - 1:
            tail_ref[0] = xg[rows - 16 :, :]
        if c == 0:
            head_ref[0] = dpre[:8, :]
    dcw_ref[0] = jnp.concatenate(tap_sums + [jnp.zeros((2, width), f32)], axis=0)

    @pl.when(group == pl.num_programs(1) - 1)
    def _():
        for c in range(n_chunks):
            at = slice(c * rows, (c + 1) * rows)
            ids_col = fl_ref[0, at, 3:4]
            ids_row = rv_ref[0, 24:25, at]
            t_at = lax.broadcasted_iota(jnp.int32, (rows, rows), 0)
            s_at = lax.broadcasted_iota(jnp.int32, (rows, rows), 1)
            keep = (ids_col == ids_row) & (t_at >= s_at)
            grad = jnp.where(keep, dcb_ref[c], 0.0).astype(bf16)
            dbc_ref[0, at, 128:] += mm(grad, bc_ref[0, at, :128].astype(bf16))
            dbc_ref[0, at, :128] += tmm(grad, bc_ref[0, at, 128:].astype(bf16))


def scan_bwd(hv, fl, rv, al, bc, bt, x_ext, cw, dy, states, s_recv, r_recv, rows):
    pieces, length, _ = hv.shape
    n_chunks = length // rows
    width = GROUP * 64
    channels = x_ext.shape[2]
    groups = channels // width
    seg = head_map(channels, f32)
    return pl.pallas_call(
        lambda *refs: scan_bwd_body(n_chunks, rows, *refs),
        grid=(pieces, groups),
        in_specs=[
            pl.BlockSpec((1, length, 128), lambda s, g: (s, 0, 0)),
            pl.BlockSpec((1, length, 8), lambda s, g: (s, 0, 0)),
            pl.BlockSpec((1, 32, length), lambda s, g: (s, 0, 0)),
            pl.BlockSpec((1, 8, width), lambda s, g: (s, 0, g)),
            pl.BlockSpec((1, length, 256), lambda s, g: (s, 0, 0)),
            pl.BlockSpec((1, 256, length), lambda s, g: (s, 0, 0)),
            pl.BlockSpec((1, HALO + length, width), lambda s, g: (s, 0, g)),
            pl.BlockSpec((8, width), lambda s, g: (0, g)),
            pl.BlockSpec((1, length, width), lambda s, g: (s, 0, g)),
            pl.BlockSpec((1, n_chunks, 128, width), lambda s, g: (s, 0, 0, g)),
            pl.BlockSpec((1, 128, width), lambda s, g: (s, 0, g)),
            pl.BlockSpec((1, 128, width), lambda s, g: (s, 0, g)),
            pl.BlockSpec((width, 128), lambda s, g: (g, 0)),
        ],
        out_specs=[
            pl.BlockSpec((1, length, width), lambda s, g: (s, 0, g)),
            pl.BlockSpec((1, 16, width), lambda s, g: (s, 0, g)),
            pl.BlockSpec((1, 8, width), lambda s, g: (s, 0, g)),
            pl.BlockSpec((1, length, 256), lambda s, g: (s, 0, 0)),
            pl.BlockSpec((1, length, 256), lambda s, g: (s, 0, 0)),
            pl.BlockSpec((1, 32, length), lambda s, g: (s, 0, 0)),
            pl.BlockSpec((1, 8, width), lambda s, g: (s, 0, g)),
        ],
        out_shape=[
            jax.ShapeDtypeStruct((pieces, length, channels), bf16),
            jax.ShapeDtypeStruct((pieces, 16, channels), f32),
            jax.ShapeDtypeStruct((pieces, 8, channels), f32),
            jax.ShapeDtypeStruct((pieces, length, 256), f32),
            jax.ShapeDtypeStruct((pieces, length, 256), f32),
            jax.ShapeDtypeStruct((pieces, 32, length), f32),
            jax.ShapeDtypeStruct((pieces, 8, channels), f32),
        ],
        scratch_shapes=[
            pltpu.VMEM((n_chunks, rows, rows), f32),
            pltpu.VMEM((n_chunks, rows, rows), f32),
            pltpu.VMEM((length + 8, width), f32),
        ],
        cost_estimate=pl.CostEstimate(
            flops=pieces * groups * GROUP * length * (rows + 256) * 128 * 6,
            transcendentals=pieces * groups * GROUP * length * rows,
            bytes_accessed=pieces * length * channels * 12,
        ),
        name="scan_bwd",
    )(hv, fl, rv, al, bc, bt, x_ext, cw, dy, states, s_recv, r_recv, seg)


def swap(value):
    size = lax.axis_size("dp")
    return lax.ppermute(value, "dp", [(i, i ^ 1) for i in range(size)])


def across(value, bit):
    size = lax.axis_size("dp")
    return lax.ppermute(value, "dp", [(i, i ^ (1 << bit)) for i in range(size)])


def around(value, by):
    size = lax.axis_size("tensor")
    return lax.ppermute(value, "tensor", [(i, (i + by) % size) for i in range(size)])


def along_sequence(value, pieces, forward):
    size = lax.axis_size("tensor")
    pairs = [(i, i + 1) for i in range(size - 1) if (i + 1) % pieces]
    if not forward:
        pairs = [(b, a) for a, b in pairs]
    return lax.ppermute(value, "tensor", pairs)


class Place:
    def __init__(self):
        dp = lax.axis_index("dp")
        self.core = dp % 2
        self.slots = lax.axis_size("tensor")
        self.slot = lax.axis_index("tensor")
        self.bits = [b for b in range(1, lax.axis_size("dp").bit_length() - 1)]
        self.side = {b: (dp >> b) % 2 for b in range(lax.axis_size("dp").bit_length() - 1)}

    def gather_slots(self, block):
        blocks = [block] + [around(block, d) for d in range(1, self.slots)]
        shape = (block.shape[0], self.slots, block.shape[1])
        index = lax.broadcasted_iota(jnp.int32, shape, 1)
        out = jnp.broadcast_to(block[:, None, :], shape)
        for d in range(1, self.slots):
            from_slot = (self.slot - d) % self.slots
            out = jnp.where(index == from_slot, blocks[d][:, None, :], out)
        return out

    def scatter_slots(self, blocks):
        def block(at):
            return lax.dynamic_index_in_dim(blocks, at % self.slots, 1, keepdims=False)

        total = block(self.slot).astype(f32)
        for d in range(1, self.slots):
            total = total + around(block(self.slot + d), d).astype(f32)
        return total

    def ordered(self, bit, mine, other, axis):
        mine, other = jnp.expand_dims(mine, axis), jnp.expand_dims(other, axis)
        low = self.side[bit] == 0
        return jnp.where(
            low,
            jnp.concatenate([mine, other], axis=axis),
            jnp.concatenate([other, mine], axis=axis),
        )

    def gather_rows(self, block, upward):
        done = block
        for bit in self.bits if upward else self.bits[::-1]:
            axis = 0 if upward else len(done.shape) - 2
            done = self.ordered(bit, done, across(done, bit), axis)
        return done.reshape((-1, block.shape[1]))

    def scatter_rows(self, whole, upward, low_bit=1):
        bits = [b for b in self.bits if b >= low_bit]
        if low_bit == 0:
            bits = [0] + bits
        count = len(bits)
        rows = whole.shape[0] >> count
        left = sorted(bits, reverse=True)
        now = whole.reshape((2,) * count + (rows, whole.shape[1]))
        for bit in bits if upward else bits[::-1]:
            axis = left.index(bit)
            left.remove(bit)
            side = self.side[bit]
            keep = lax.dynamic_index_in_dim(now, side, axis, keepdims=False)
            give = lax.dynamic_index_in_dim(now, 1 - side, axis, keepdims=False)
            now = (keep.astype(f32) + across(give, bit).astype(f32)).astype(whole.dtype)
        return now

    def gather_weight(self, mine, other):
        both = self.ordered(0, mine, other, 0).reshape((-1, mine.shape[1]))
        blocks = self.gather_slots(both)
        half = self.slots // 2
        first = blocks[:, :half].reshape((both.shape[0], -1))
        second = blocks[:, half:].reshape((both.shape[0], -1))
        return jnp.concatenate(
            [self.gather_rows(first, True), self.gather_rows(second, False)], axis=1
        )

    def scatter_weight(self, part):
        columns = part.shape[1] // 2
        half = self.slots // 2
        first = self.scatter_rows(part[:, :columns], False)
        second = self.scatter_rows(part[:, columns:], True)
        rows = first.shape[0]
        blocks = jnp.concatenate(
            [first.reshape((rows, half, -1)), second.reshape((rows, half, -1))], axis=1
        )
        mine = self.scatter_slots(blocks).reshape((2, rows // 2, -1))
        keep = lax.dynamic_index_in_dim(mine, self.core, 0, keepdims=False)
        give = lax.dynamic_index_in_dim(mine, 1 - self.core, 0, keepdims=False)
        out = self.ordered(0, keep, swap(give), 1)
        return out.reshape((rows // 2, -1))

    def sum_chips(self, value):
        for bit in self.bits:
            value = value + across(value, bit)
        return value

    def sum_slots(self, value):
        total = value.astype(f32)
        for d in range(1, self.slots):
            total = total + around(value, d).astype(f32)
        return total


def on_device(
    x_in,
    segment_ids,
    norm_gain,
    w_x,
    w_z,
    w_bc,
    w_dt,
    conv_x,
    conv_x_bias,
    conv_bc,
    conv_bc_bias,
    dt_bias,
    a_log,
    d_skip,
    gate_gain,
    w_out,
    cotangent,
):
    place = Place()
    core, slots, slot = place.core, place.slots, place.slot
    length, features = x_in.shape
    sequences, whole_length = segment_ids.shape
    pieces = whole_length // length
    own_rows = w_x.shape[0]
    slot_channels = w_x.shape[1]
    slot_heads = w_dt.shape[1]
    half_channels = slot_channels // 2
    half_heads = slot_heads // 2
    channels = half_channels * slots
    heads = half_heads * slots
    all_channels = 2 * channels
    all_heads = 2 * heads
    bc_width = w_bc.shape[1]
    n_chunks = length // CH

    def split(weight):
        return weight.reshape((own_rows, 2, half_channels))

    stacked = jnp.stack([split(w_x), split(w_z), split(w_out.T)])
    mine = lax.dynamic_index_in_dim(stacked, core, 2, keepdims=False)
    other = swap(lax.dynamic_index_in_dim(stacked, 1 - core, 2, keepdims=False))
    wx = place.gather_weight(mine[0], other[0])
    dt_slots = place.gather_slots(w_dt).reshape((own_rows, all_heads))
    thin = jnp.concatenate([w_bc, dt_slots, norm_gain[:, None]], axis=1)
    thin = jnp.pad(thin, ((0, 0), (0, bc_width + 128 - thin.shape[1])))
    thin = place.ordered(0, thin, swap(thin), 0).reshape((2 * own_rows, -1))
    thin = place.gather_rows(thin, True)
    wz = place.gather_weight(mine[1], other[1])
    wo = place.gather_weight(mine[2], other[2])

    rows = jnp.concatenate(
        [
            conv_x,
            conv_x_bias[None],
            gate_gain[None],
            jnp.pad(jnp.concatenate([dt_bias, a_log, d_skip])[None], ((0, 0), (0, slot_channels - 3 * slot_heads))),
            jnp.zeros((1, slot_channels), f32),
        ],
        axis=0,
    )
    rows = place.gather_slots(rows)
    own = lax.dynamic_index_in_dim(
        rows.reshape((8, slots, 2, half_channels)), core, 2, keepdims=False
    ).reshape((8, channels))
    gain_row = own[5:6]
    lane = jnp.arange(128)
    head_at = lane % 32
    global_head = (head_at // half_heads) * slot_heads + core * half_heads + head_at % half_heads
    pick = ((lane[:, None] == global_head[None, :]) & (head_at < heads)[None, :]).astype(f32)
    small = rows[6, :, : 3 * slot_heads].reshape((slots, 3, slot_heads)).transpose(1, 0, 2)
    small = jnp.pad(small.reshape((3, all_heads)), ((0, 5), (0, 128 - all_heads)))
    small = exact(small, pick)
    bias_lanes = small[0]
    rate_lanes = jnp.where(head_at < heads, -jnp.exp(small[1]), 0.0)
    to_heads = head_map(channels, f32)
    skip_row = exact(small[2:3] * (lane < 32), to_heads.T)
    cw = jnp.concatenate([own[:5], skip_row, jnp.zeros((2, channels), f32)], axis=0)

    padded = jnp.pad(segment_ids, ((0, 0), (HALO, HALO)), constant_values=-1)
    ids_own = lax.dynamic_slice(
        padded, (slot // pieces, (slot % pieces) * length), (1, length + 2 * HALO)
    )
    ids_all = jnp.concatenate([ids_own, swap(ids_own)], axis=0)
    ids = ids_all[:, HALO : HALO + length]
    before = ids_all[:, HALO - 1]

    def near(k):
        return ids_all[:, HALO + k : HALO + k + length] == ids

    flags = [near(-1), near(-2), near(-3), ids, near(1), near(2), near(3), jnp.zeros_like(ids)]
    flags = jnp.stack([v.astype(f32) for v in flags], axis=-1)

    x_rows = jnp.concatenate([along_sequence(x_in[-HALO:], pieces, True), x_in], axis=0)
    tokens_ext = x_rows.astype(f32)
    inv_ext = lax.rsqrt(jnp.mean(tokens_ext * tokens_ext, axis=-1, keepdims=True) + epsilon)
    gain = thin[:, bc_width + all_heads].astype(f32)[None, :]
    normed_own = (tokens_ext * inv_ext * gain).astype(bf16)
    normed_other = swap(normed_own)
    normed_ext = jnp.concatenate([normed_own, normed_other], axis=0)
    normed = jnp.concatenate([normed_own[HALO:], normed_other[HALO:]], axis=0)
    tokens, inv_rms = tokens_ext[HALO:], inv_ext[HALO:]
    cot = jnp.concatenate([cotangent, swap(cotangent)], axis=0)

    dt_pick = jnp.dot(thin[:, bc_width:], pick.astype(bf16), preferred_element_type=f32).astype(bf16)
    thin_proj = mm(normed_ext, jnp.concatenate([thin[:, :bc_width], dt_pick], axis=1))
    thin_proj = thin_proj.reshape((2, HALO + length, -1))
    bc_ext = thin_proj[:, :, :bc_width]
    dt_in = thin_proj[:, HALO:, bc_width:] + bias_lanes
    x_ext = mm(normed_ext, wx).reshape((2, HALO + length, channels))

    bc_pre = conv_bc_bias + conv_bc[0] * bc_ext[:, HALO:]
    for k in range(1, conv_bc.shape[0]):
        shifted = bc_ext[:, HALO - k : HALO - k + length]
        bc_pre = bc_pre + conv_bc[k] * shifted * flags[:, :, k - 1 : k]
    bc_act = jax.nn.silu(bc_pre)
    bc_turned = bc_act.astype(bf16).transpose(0, 2, 1)
    c_low = bc_act[:, :, bc_width // 2 :].astype(bf16)

    step = jax.nn.softplus(dt_in)
    log_step = (step * rate_lanes).reshape((2 * n_chunks, CH, 128))
    tri = (jnp.arange(CH)[:, None] >= jnp.arange(CH)[None, :]).astype(f32)
    running = jnp.einsum("ts,csh->cth", tri, log_step, precision=highest)
    running = running.reshape((2, n_chunks, CH, 128))
    last = running[:, :, -1:, :]
    ids_chunks = ids.reshape((2, n_chunks, CH, 1))
    chunk_end = ids_chunks[:, :, -1:, :]
    chunk_before = jnp.concatenate(
        [before[:, None, None, None], chunk_end[:, :-1]], axis=1
    )
    still = (chunk_end == chunk_before).astype(f32)
    alpha = still * jnp.exp(last)
    lead = jnp.cumsum(last, axis=1) - last
    since_piece = (ids_chunks == before[:, None, None, None]).astype(f32) * jnp.exp(running + lead)
    since_piece = since_piece.reshape((2 * length, 128))
    group_lane = lane // 32
    hv = jnp.where(
        group_lane == 0,
        running * LOG2E,
        jnp.where(
            group_lane == 1,
            step.reshape((2, n_chunks, CH, 128)),
            jnp.where(
                group_lane == 2,
                (ids_chunks == chunk_before).astype(f32) * jnp.exp(running),
                (ids_chunks == chunk_end).astype(f32) * jnp.exp(last - running),
            ),
        ),
    ).reshape((2, length, 128))
    rv = jnp.concatenate(
        [
            hv[:, :, :24].transpose(0, 2, 1),
            ids.astype(f32)[:, None, :],
            jnp.zeros((2, 7, length), f32),
        ],
        axis=1,
    )
    first_lanes = (lane < 32).astype(f32)
    al = exact((alpha * first_lanes).reshape((2 * n_chunks, 128)), to_heads.T)
    al = al.reshape((2, n_chunks, channels))
    whole_alpha = jnp.prod(al, axis=1, keepdims=True)
    al = jnp.pad(al, ((0, 0), (0, 8 - n_chunks), (0, 0)))
    wide_since = mm((since_piece * first_lanes).astype(bf16), to_heads.T.astype(bf16))
    wide_since = wide_since.reshape((2, length, channels))

    def hand_on(local, forward):
        low = local.astype(bf16)
        for _ in range(pieces - 2):
            came = along_sequence(low, pieces, forward)
            low = (local + whole_alpha * came.astype(f32)).astype(bf16)
        return along_sequence(low, pieces, forward)

    y_here, states = scan_fwd(hv, flags, rv, al, bc_act, bc_turned, x_ext, cw, CH)
    state_in = hand_on(states[:, -1], True)
    y = y_here + wide_since * lax.dot_general(
        c_low, state_in, (((2,), (1,)), ((0,), (0,))), preferred_element_type=f32
    )

    gate_in = mm(normed, wz)
    mixed_grad = mm(cot, wo)
    y = y.reshape((2 * length, channels))
    sig = jax.nn.sigmoid(gate_in)
    act = gate_in * sig
    gated = y * act
    scaled = mixed_grad * gain_row
    sums = jnp.stack([jnp.sum(gated * gated, axis=1), jnp.sum(scaled * gated, axis=1)])
    sums = sums.reshape((2, 2, length))
    sums = (sums + swap(sums)[:, ::-1]).reshape((2, 2 * length))
    gate_rms = lax.rsqrt(sums[0] / all_channels + epsilon)[:, None]
    mixed = (gated * gate_rms * gain_row).astype(bf16)
    gate_gain_part = jnp.sum(mixed_grad * gated * gate_rms, axis=0)
    gated_grad = gate_rms * scaled - gated * gate_rms**3 * (sums[1] / all_channels)[:, None]
    y_grad = (gated_grad * act).reshape((2, length, channels))
    gate_grad = (gated_grad * y * sig * (1.0 + gate_in * (1.0 - sig))).astype(bf16)

    state_grad = lax.dot_general(
        c_low, (y_grad * wide_since).astype(bf16), (((1,), (1,)), ((0,), (0,))), preferred_element_type=f32
    )
    state_grad = hand_on(state_grad, False)
    wo_part = tmm(cot, mixed).astype(bf16)
    w_out_grad = place.scatter_weight(wo_part).T
    branch = mmt(mixed, wo)
    block_out = (tokens + branch[:length] + swap(branch[length:].astype(bf16)).astype(f32)).astype(bf16)
    wz_part = tmm(normed, gate_grad).astype(bf16)
    w_z_grad = place.scatter_weight(wz_part)

    x_low, tail, head, dbc, dcol, drow, dcw = scan_bwd(
        hv, flags, rv, al, bc_act, bc_turned, x_ext, cw, y_grad, states, state_in, state_grad, CH
    )

    head = along_sequence(head, pieces, False)

    def past_end(begin, taps):
        total = jnp.zeros((begin.shape[0], HALO, begin.shape[2]), f32)
        for k in range(1, taps.shape[0]):
            moved = jnp.pad(begin[:, :k], ((0, 0), (HALO - k, 0), (0, 0)))
            total = total + taps[k] * moved * flags[: begin.shape[0], length - HALO :, 3 + k : 4 + k]
        return total

    fixed = (tail + past_end(head, own[:4])).astype(bf16)
    x_low = lax.dynamic_update_slice(x_low, fixed, (0, length - HALO, 0)).reshape((2 * length, channels))

    bc_grad = dbc[0] + swap(dbc[1])
    pre = bc_pre[0]
    sig_bc = jax.nn.sigmoid(pre)
    bc_dpre = bc_grad * (sig_bc * (1.0 + pre * (1.0 - sig_bc)))
    bc_head = along_sequence(bc_dpre[:8], pieces, False)
    bc_raw = conv_bc[0] * bc_dpre
    bc_taps = [jnp.sum(bc_dpre * bc_ext[0, HALO:], axis=0)]
    longer = jnp.concatenate([bc_dpre, bc_head], axis=0)
    for k in range(1, conv_bc.shape[0]):
        bc_raw = bc_raw + conv_bc[k] * longer[k : k + length] * flags[0, :, 3 + k : 4 + k]
        shifted = bc_ext[0, HALO - k : HALO - k + length]
        bc_taps.append(jnp.sum(bc_dpre * shifted * flags[0, :, k - 1 : k], axis=0))
    bc_low = bc_raw.astype(bf16)
    bc_small = jnp.stack(bc_taps + [jnp.sum(bc_dpre, axis=0)] + [jnp.zeros((bc_width,), f32)] * 3)
    bc_small = place.sum_chips(bc_small + swap(bc_small))
    bc_small = place.sum_slots(bc_small)

    dcum = dcol[:, :, :128] - jnp.pad(drow.transpose(0, 2, 1), ((0, 0), (0, 0), (0, 96)))
    dlog = jnp.einsum("ts,csh->cth", tri.T, dcum.reshape((2 * n_chunks, CH, 128)), precision=highest)
    dstep = dcol[:, :, 128:] + dlog.reshape((2, length, 128)) * rate_lanes
    dt_raw = (dstep * jax.nn.sigmoid(dt_in)).reshape((2 * length, 128))
    rate_part = jnp.sum(dlog * log_step, axis=(0, 1))
    place_back = (pick * first_lanes).T.astype(bf16)
    dt_low = mm(dt_raw.astype(bf16), place_back).astype(bf16)

    dcw = jnp.sum(dcw, axis=0)
    head_rows = jnp.stack([jnp.sum(dt_raw, axis=0), rate_part]) * first_lanes
    head_rows = exact(head_rows, to_heads.T)
    packed = jnp.concatenate(
        [dcw[:5], gate_gain_part[None], dcw[5:6], head_rows, jnp.zeros((7, channels), f32)], axis=0
    )
    packed = place.sum_chips(packed).reshape((16, slots, half_channels))
    packed = place.scatter_slots(packed)
    packed = place.ordered(0, packed, swap(packed), 1).reshape((16, slot_channels))
    by_head = packed[6:9].reshape((3, slot_heads, 64))

    wx_part = tmm(normed, x_low).astype(bf16)
    w_x_grad = place.scatter_weight(wx_part)
    thin_low = jnp.concatenate(
        [jnp.concatenate([bc_low, jnp.zeros_like(bc_low)], axis=0), dt_low], axis=1
    )
    thin_part = tmm(normed, thin_low).astype(bf16)
    thin_grad = place.scatter_rows(thin_part, True, low_bit=0)
    thin_grad = place.sum_slots(thin_grad)
    w_bc_grad = thin_grad[:, :bc_width]
    w_dt_grad = lax.dynamic_slice_in_dim(thin_grad, bc_width + slot * slot_heads, slot_heads, 1)

    normed_grad = mmt(x_low, wx) + mmt(gate_grad, wz) + mmt(thin_low, thin)
    normed_grad = normed_grad[:length] + swap(normed_grad[length:].astype(bf16)).astype(f32)
    gain_part = jnp.sum(normed_grad * tokens * inv_rms, axis=0)
    pushed = normed_grad * gain
    x_grad = (
        cotangent.astype(f32)
        + inv_rms * pushed
        - tokens * inv_rms**3 * jnp.mean(pushed * tokens, axis=-1, keepdims=True)
    )
    gain_rows = gain_part.reshape((features // own_rows * 2, own_rows // 2))
    gain_rows = place.scatter_rows(gain_rows, True, low_bit=0)
    norm_gain_grad = place.sum_slots(gain_rows).reshape((own_rows,))
    return (
        block_out,
        x_grad,
        norm_gain_grad,
        w_x_grad,
        w_z_grad,
        w_bc_grad,
        w_dt_grad,
        packed[:4],
        packed[4],
        bc_small[:4],
        bc_small[4],
        by_head[1, :, 0],
        by_head[2, :, 0],
        jnp.sum(by_head[0], axis=1),
        packed[5],
        w_out_grad,
    )


def solution(mesh):
    rows = P(("dp", "tensor"), None)
    both = P("dp", "tensor")
    heads = P("tensor")
    in_specs = (
        rows, P("dp", None), P("dp"), both, both, P("dp", None), both, P(None, "tensor"), heads,
        P(), P(), heads, heads, heads, heads, P("tensor", "dp"), rows,
    )
    out_specs = (
        rows, rows, P("dp"), both, both, P("dp", None), both, P(None, "tensor"), heads,
        P(), P(), heads, heads, heads, heads, P("tensor", "dp"),
    )
    return jax.shard_map(
        on_device, mesh=mesh, in_specs=in_specs, out_specs=out_specs, check_vma=False
    )
```

```python
import jax
import jax.numpy as jnp
from jax import lax
from jax.experimental import pallas as pl
from jax.experimental.pallas import tpu as pltpu
from jax.sharding import PartitionSpec as P

CH = 256
HALO = 16
GROUP = 4
LOG2E = 1.4426950408889634
epsilon = 1e-05
f32 = jnp.float32
bf16 = jnp.bfloat16
highest = lax.Precision.HIGHEST


def mm(a, b):
    return lax.dot_general(a, b, (((1,), (0,)), ((), ())), preferred_element_type=f32)


def mmt(a, b):
    return lax.dot_general(a, b, (((1,), (1,)), ((), ())), preferred_element_type=f32)


def tmm(a, b):
    return lax.dot_general(a, b, (((0,), (0,)), ((), ())), preferred_element_type=f32)


def exact(a, b):
    return lax.dot_general(
        a, b, (((1,), (0,)), ((), ())), precision=highest, preferred_element_type=f32
    )


def head_map(channels, kind):
    return (jnp.arange(channels)[:, None] // 64 == jnp.arange(128)[None, :]).astype(kind)


def spread(cols, first, rows, lane_low):
    parts = []
    for pair in range(GROUP // 2):
        left = jnp.broadcast_to(cols[:, first + 2 * pair : first + 2 * pair + 1], (rows, 128))
        right = jnp.broadcast_to(cols[:, first + 2 * pair + 1 : first + 2 * pair + 2], (rows, 128))
        parts.append(jnp.where(lane_low, left, right))
    return jnp.concatenate(parts, axis=1)


def conv_pre(x_ref, cw_ref, flags, start, rows):
    pre = cw_ref[4:5, :] + cw_ref[0:1, :] * x_ref[0, HALO + start : HALO + start + rows, :]
    for k in range(1, 4):
        shifted = x_ref[0, HALO + start - k : HALO + start - k + rows, :]
        pre = pre + (cw_ref[k : k + 1, :] * shifted) * flags[:, k - 1 : k]
    return pre


def masked_scores(cb_ref, bc_ref, fl_ref, rv_ref, n_chunks, rows):
    for c in range(n_chunks):
        at = slice(c * rows, (c + 1) * rows)
        ids_col = fl_ref[0, at, 3:4]
        ids_row = rv_ref[0, 24:25, at]
        t_at = lax.broadcasted_iota(jnp.int32, (rows, rows), 0)
        s_at = lax.broadcasted_iota(jnp.int32, (rows, rows), 1)
        keep = (ids_col == ids_row) & (t_at >= s_at)
        scores = lax.dot_general(
            bc_ref[0, at, 128:], bc_ref[0, at, :128], (((1,), (1,)), ((), ())),
            precision=highest, preferred_element_type=f32,
        )
        cb_ref[c] = jnp.where(keep, scores, 0.0)


def scan_fwd_body(n_chunks, rows, hv_ref, fl_ref, rv_ref, al_ref, bc_ref, bt_ref, x_ref, cw_ref, y_ref, st_ref, cb_ref):
    group = pl.program_id(1)
    turn = lax.rem(128 - GROUP * group, 128)

    @pl.when(group == 0)
    def _():
        masked_scores(cb_ref, bc_ref, fl_ref, rv_ref, n_chunks, rows)

    lane_low = lax.broadcasted_iota(jnp.int32, (rows, 128), 1) < 64
    state = jnp.zeros((128, GROUP * 64), f32)
    for c in range(n_chunks):
        at = slice(c * rows, (c + 1) * rows)
        cols = pltpu.roll(hv_ref[0, at, :], turn, 1)
        flags = fl_ref[0, at, :]
        pre = conv_pre(x_ref, cw_ref, flags, c * rows, rows)
        act = pre * jax.nn.sigmoid(pre)
        u = act * spread(cols, 32, rows, lane_low)
        ub = u.astype(bf16)
        y = cw_ref[5:6, :] * act
        if c > 0:
            c_rows = bc_ref[0, at, 128:].astype(bf16)
            y = y + mm(c_rows, state.astype(bf16)) * spread(cols, 64, rows, lane_low)
        scores = cb_ref[c]
        parts = []
        for pair in range(GROUP // 2):
            u_pair = ub[:, 128 * pair : 128 * pair + 128]
            outs = []
            for j in (2 * pair, 2 * pair + 1):
                gap = cols[:, j : j + 1] - rv_ref[0, pl.ds(group * GROUP + j, 1), at]
                mix = (scores * jnp.exp2(jnp.minimum(gap, 0.0))).astype(bf16)
                outs.append(mm(mix, u_pair))
            parts.append(jnp.where(lane_low, outs[0], outs[1]))
        y_ref[0, at, :] = y + jnp.concatenate(parts, axis=1)
        wu = (u * spread(cols, 96, rows, lane_low)).astype(bf16)
        state = al_ref[0, c : c + 1, :] * state + mm(bt_ref[0, :128, at], wu)
        st_ref[0, c] = state


def scan_fwd(hv, fl, rv, al, bc, bt, x_ext, cw, rows, first=0, count=2):
    length = hv.shape[1]
    n_chunks = length // rows
    width = GROUP * 64
    channels = x_ext.shape[2]
    groups = channels // width
    return pl.pallas_call(
        lambda *refs: scan_fwd_body(n_chunks, rows, *refs),
        grid=(count, groups),
        in_specs=[
            pl.BlockSpec((1, length, 128), lambda s, g: (first + s, 0, 0)),
            pl.BlockSpec((1, length, 8), lambda s, g: (first + s, 0, 0)),
            pl.BlockSpec((1, 32, length), lambda s, g: (first + s, 0, 0)),
            pl.BlockSpec((1, 8, width), lambda s, g: (first + s, 0, g)),
            pl.BlockSpec((1, length, 256), lambda s, g: (first + s, 0, 0)),
            pl.BlockSpec((1, 256, length), lambda s, g: (first + s, 0, 0)),
            pl.BlockSpec((1, HALO + length, width), lambda s, g: (first + s, 0, g)),
            pl.BlockSpec((8, width), lambda s, g: (0, g)),
        ],
        out_specs=[
            pl.BlockSpec((1, length, width), lambda s, g: (s, 0, g)),
            pl.BlockSpec((1, n_chunks, 128, width), lambda s, g: (s, 0, 0, g)),
        ],
        out_shape=[
            jax.ShapeDtypeStruct((count, length, channels), f32),
            jax.ShapeDtypeStruct((count, n_chunks, 128, channels), f32),
        ],
        scratch_shapes=[pltpu.VMEM((n_chunks, rows, rows), f32)],
        cost_estimate=pl.CostEstimate(
            flops=count * groups * GROUP * length * (rows + 256) * 128 * 2,
            transcendentals=count * groups * GROUP * length * rows,
            bytes_accessed=count * length * channels * 8,
        ),
        name="scan_fwd",
    )(hv, fl, rv, al, bc, bt, x_ext, cw)


def scan_bwd_body(
    n_chunks, rows, hv_ref, fl_ref, rv_ref, al_ref, bc_ref, bt_ref, x_ref, cw_ref, dy_ref, st_ref, sr_ref, rr_ref, seg_ref,
    xl_ref, tail_ref, head_ref, dbc_ref, dcol_ref, drow_ref, dcw_ref, cb_ref, dcb_ref, dpre_ref,
):
    group = pl.program_id(1)
    turn = lax.rem(128 - GROUP * group, 128)
    length = n_chunks * rows
    width = GROUP * 64

    @pl.when(group == 0)
    def _():
        masked_scores(cb_ref, bc_ref, fl_ref, rv_ref, n_chunks, rows)
        dcb_ref[...] = jnp.zeros_like(dcb_ref)
        dbc_ref[...] = jnp.zeros_like(dbc_ref)
        dcol_ref[...] = jnp.zeros_like(dcol_ref)
        drow_ref[...] = jnp.zeros_like(drow_ref)

    lane_low = lax.broadcasted_iota(jnp.int32, (rows, 128), 1) < 64
    lane = lax.broadcasted_iota(jnp.int32, (rows, 128), 1)
    row_at = lax.broadcasted_iota(jnp.int32, (rows, width), 0)
    grad_state = rr_ref[0].astype(f32)
    recv = sr_ref[0].astype(f32)
    states = [recv]
    carry = recv
    for c in range(n_chunks - 1):
        carry = al_ref[0, c : c + 1, :] * carry
        states.append(st_ref[0, c] + carry)
    tap_sums = [jnp.zeros((1, width), f32) for _ in range(6)]
    dpre_ref[length : length + 8, :] = jnp.zeros((8, width), f32)
    for c in reversed(range(n_chunks)):
        at = slice(c * rows, (c + 1) * rows)
        cols = pltpu.roll(hv_ref[0, at, :], turn, 1)
        flags = fl_ref[0, at, :]
        pre = conv_pre(x_ref, cw_ref, flags, c * rows, rows)
        sig = jax.nn.sigmoid(pre)
        act = pre * sig
        step_wide = spread(cols, 32, rows, lane_low)
        end_wide = spread(cols, 96, rows, lane_low)
        u = act * step_wide
        ub = u.astype(bf16)
        dy = dy_ref[0, at, :]
        dyb = dy.astype(bf16)
        b_rows = bc_ref[0, at, :128].astype(bf16)
        c_rows = bc_ref[0, at, 128:].astype(bf16)
        state_b = states[c].astype(bf16)
        dye = dy * spread(cols, 64, rows, lane_low)
        dyeb = dye.astype(bf16)
        gs_b = grad_state.astype(bf16)
        wub = (u * end_wide).astype(bf16)
        dbc_ref[0, at, 128:] += mmt(dyeb, state_b)
        dbc_ref[0, at, :128] += mmt(wub, gs_b)
        du_state = mm(b_rows, gs_b) * end_wide
        u_du = u * du_state
        at_end = jnp.sum(u_du, axis=0, keepdims=True) + al_ref[0, c : c + 1, :] * jnp.sum(
            grad_state * states[c], axis=0, keepdims=True
        )
        log_grad = dye * mm(c_rows, state_b) - u_du
        log_grad = jnp.where(row_at == rows - 1, log_grad + at_end, log_grad)
        grad_state = al_ref[0, c : c + 1, :] * grad_state + mm(bt_ref[0, 128:, at], dyeb)
        scores = cb_ref[c]
        dcb = dcb_ref[c]
        parts = []
        row_sums = jnp.zeros((rows, 128), f32)
        for pair in range(GROUP // 2):
            lanes = slice(128 * pair, 128 * pair + 128)
            u_pair = ub[:, lanes]
            dy_pair = dyb[:, lanes]
            outs = []
            for j in (2 * pair, 2 * pair + 1):
                gap = cols[:, j : j + 1] - rv_ref[0, pl.ds(group * GROUP + j, 1), at]
                decay = jnp.exp2(jnp.minimum(gap, 0.0))
                mix = (scores * decay).astype(bf16)
                own = lane_low if j % 2 == 0 else jnp.logical_not(lane_low)
                prod = mmt(jnp.where(own, dy_pair, jnp.zeros_like(dy_pair)), u_pair) * decay
                dcb = dcb + prod
                full = prod * scores
                row_sums = jnp.where(
                    lane == group * GROUP + j, jnp.sum(full, axis=1, keepdims=True), row_sums
                )
                drow_ref[0, pl.ds(group * GROUP + j, 1), at] = jnp.sum(full, axis=0, keepdims=True)
                outs.append(tmm(mix, dy_pair))
            parts.append(jnp.where(lane_low, outs[0], outs[1]))
        dcb_ref[c] = dcb
        du = jnp.concatenate(parts, axis=1) + du_state
        seg = seg_ref[...]
        dcol_ref[0, at, :128] += row_sums + lax.dot_general(
            log_grad, seg, (((1,), (0,)), ((), ())), precision=highest, preferred_element_type=f32
        )
        dcol_ref[0, at, 128:] += lax.dot_general(
            du * act, seg, (((1,), (0,)), ((), ())), precision=highest, preferred_element_type=f32
        )
        dact = du * step_wide + cw_ref[5:6, :] * dy
        dpre = dact * (sig * (1.0 + pre * (1.0 - sig)))
        dpre_ref[at, :] = dpre
        tap_sums[0] += jnp.sum(dpre * x_ref[0, HALO + c * rows : HALO + (c + 1) * rows, :], axis=0, keepdims=True)
        for k in range(1, 4):
            shifted = x_ref[0, HALO + c * rows - k : HALO + (c + 1) * rows - k, :]
            tap_sums[k] += jnp.sum(dpre * flags[:, k - 1 : k] * shifted, axis=0, keepdims=True)
        tap_sums[4] += jnp.sum(dpre, axis=0, keepdims=True)
        tap_sums[5] += jnp.sum(dy * act, axis=0, keepdims=True)
        xg = cw_ref[0:1, :] * dpre
        for k in range(1, 4):
            xg = xg + (cw_ref[k : k + 1, :] * dpre_ref[c * rows + k : (c + 1) * rows + k, :]) * flags[:, 3 + k : 4 + k]
        xl_ref[0, at, :] = xg.astype(bf16)
        if c == n_chunks - 1:
            tail_ref[0] = xg[rows - 16 :, :]
        if c == 0:
            head_ref[0] = dpre[:8, :]
    dcw_ref[0] = jnp.concatenate(tap_sums + [jnp.zeros((2, width), f32)], axis=0)

    @pl.when(group == pl.num_programs(1) - 1)
    def _():
        for c in range(n_chunks):
            at = slice(c * rows, (c + 1) * rows)
            ids_col = fl_ref[0, at, 3:4]
            ids_row = rv_ref[0, 24:25, at]
            t_at = lax.broadcasted_iota(jnp.int32, (rows, rows), 0)
            s_at = lax.broadcasted_iota(jnp.int32, (rows, rows), 1)
            keep = (ids_col == ids_row) & (t_at >= s_at)
            grad = jnp.where(keep, dcb_ref[c], 0.0).astype(bf16)
            dbc_ref[0, at, 128:] += mm(grad, bc_ref[0, at, :128].astype(bf16))
            dbc_ref[0, at, :128] += tmm(grad, bc_ref[0, at, 128:].astype(bf16))


def scan_bwd(hv, fl, rv, al, bc, bt, x_ext, cw, dy, states, s_recv, r_recv, rows, first=0, count=2):
    length = hv.shape[1]
    n_chunks = length // rows
    width = GROUP * 64
    channels = x_ext.shape[2]
    groups = channels // width
    seg = head_map(channels, f32)
    return pl.pallas_call(
        lambda *refs: scan_bwd_body(n_chunks, rows, *refs),
        grid=(count, groups),
        in_specs=[
            pl.BlockSpec((1, length, 128), lambda s, g: (first + s, 0, 0)),
            pl.BlockSpec((1, length, 8), lambda s, g: (first + s, 0, 0)),
            pl.BlockSpec((1, 32, length), lambda s, g: (first + s, 0, 0)),
            pl.BlockSpec((1, 8, width), lambda s, g: (first + s, 0, g)),
            pl.BlockSpec((1, length, 256), lambda s, g: (first + s, 0, 0)),
            pl.BlockSpec((1, 256, length), lambda s, g: (first + s, 0, 0)),
            pl.BlockSpec((1, HALO + length, width), lambda s, g: (first + s, 0, g)),
            pl.BlockSpec((8, width), lambda s, g: (0, g)),
            pl.BlockSpec((1, length, width), lambda s, g: (first + s, 0, g)),
            pl.BlockSpec((1, n_chunks, 128, width), lambda s, g: (first + s, 0, 0, g)),
            pl.BlockSpec((1, 128, width), lambda s, g: (first + s, 0, g)),
            pl.BlockSpec((1, 128, width), lambda s, g: (first + s, 0, g)),
            pl.BlockSpec((width, 128), lambda s, g: (g, 0)),
        ],
        out_specs=[
            pl.BlockSpec((1, length, width), lambda s, g: (s, 0, g)),
            pl.BlockSpec((1, 16, width), lambda s, g: (s, 0, g)),
            pl.BlockSpec((1, 8, width), lambda s, g: (s, 0, g)),
            pl.BlockSpec((1, length, 256), lambda s, g: (s, 0, 0)),
            pl.BlockSpec((1, length, 256), lambda s, g: (s, 0, 0)),
            pl.BlockSpec((1, 32, length), lambda s, g: (s, 0, 0)),
            pl.BlockSpec((1, 8, width), lambda s, g: (s, 0, g)),
        ],
        out_shape=[
            jax.ShapeDtypeStruct((count, length, channels), bf16),
            jax.ShapeDtypeStruct((count, 16, channels), f32),
            jax.ShapeDtypeStruct((count, 8, channels), f32),
            jax.ShapeDtypeStruct((count, length, 256), f32),
            jax.ShapeDtypeStruct((count, length, 256), f32),
            jax.ShapeDtypeStruct((count, 32, length), f32),
            jax.ShapeDtypeStruct((count, 8, channels), f32),
        ],
        scratch_shapes=[
            pltpu.VMEM((n_chunks, rows, rows), f32),
            pltpu.VMEM((n_chunks, rows, rows), f32),
            pltpu.VMEM((length + 8, width), f32),
        ],
        cost_estimate=pl.CostEstimate(
            flops=count * groups * GROUP * length * (rows + 256) * 128 * 6,
            transcendentals=count * groups * GROUP * length * rows,
            bytes_accessed=count * length * channels * 12,
        ),
        name="scan_bwd",
    )(hv, fl, rv, al, bc, bt, x_ext, cw, dy, states, s_recv, r_recv, seg)


def project_body(places, at_ref, act_ref, *refs):
    blocks, out_ref, full_ref = refs[:-2], refs[-2], refs[-1]

    @pl.when(pl.program_id(0) == 0)
    def _():
        for ref, (d, k) in zip(blocks, places):
            rows, columns = ref.shape[1:]
            row = pl.multiple_of(at_ref[k], rows)
            column = pl.multiple_of(at_ref[4 + d], columns)
            full_ref[pl.ds(row, rows), pl.ds(column, columns)] = ref[0]

    out_ref[...] = mm(act_ref[...], full_ref[...])


def project(act, at, items, weight, channels):
    rows, features = act.shape
    tile = rows // 3 if rows % 48 == 0 else rows // 4
    blocks = [item[0] for item in items]
    places = [item[1:] for item in items]
    return pl.pallas_call(
        lambda *refs: project_body(places, *refs),
        grid_spec=pltpu.PrefetchScalarGridSpec(
            num_scalar_prefetch=1,
            grid=(rows // tile,),
            in_specs=[pl.BlockSpec((tile, features), lambda i, at: (i, 0))]
            + [
                pl.BlockSpec((1,) + b.shape[1:], lambda i, at: (weight, 0, 0), pipeline_mode=pl.Buffered(1))
                for b in blocks
            ],
            out_specs=[
                pl.BlockSpec((tile, channels), lambda i, at: (i, 0)),
                pl.BlockSpec((features, channels), lambda i, at: (0, 0), pipeline_mode=pl.Buffered(1)),
            ],
        ),
        out_shape=[
            jax.ShapeDtypeStruct((rows, channels), f32),
            jax.ShapeDtypeStruct((features, channels), bf16),
        ],
        cost_estimate=pl.CostEstimate(
            flops=2 * rows * features * channels,
            transcendentals=0,
            bytes_accessed=rows * features * 2 + rows * channels * 4 + features * channels * 4,
        ),
        name="project",
    )(at, act, *blocks)


def weight_parts_body(count, group, flip, at_ref, *refs):
    keep_ref, give_ref = refs[-2:]
    rows, columns = keep_ref.shape[3:]
    per = (len(refs) - 2 - count) // count
    for w in range(count):
        left_ref, right_refs = refs[w], refs[count + w * per : count + (w + 1) * per]

        @pl.when(pl.program_id(0) == w)
        def _():
            rights = [
                jnp.concatenate(
                    [ref[:, pl.ds(pl.multiple_of(at_ref[4 + d], columns), columns)] for d in group], axis=1
                )
                for ref in right_refs
            ]
            tokens = right_refs[0].shape[0]
            for k in range(4):
                left = pl.ds(pl.multiple_of(at_ref[k], rows), rows)
                part = mm(left_ref[left, :tokens], rights[0])
                for i in range(1, per):
                    part = part + mm(left_ref[left, i * tokens : (i + 1) * tokens], rights[i])
                part = part.astype(bf16)
                away, place = (k // 2, k % 2) if flip == 0 else (k % 2, k // 2)
                target = give_ref if away else keep_ref
                for i in range(len(group)):
                    target[0, i, place] = part[:, i * columns : (i + 1) * columns]


def weight_parts(at, lefts, rights, group, own_rows, columns, flip):
    rights = [piece for right in rights for piece in right]
    count = len(lefts)
    shape = (count, len(group), 2, 2 * own_rows, columns)
    whole = lambda v: pl.BlockSpec(v.shape, lambda w, at: (0, 0), pipeline_mode=pl.Buffered(1))
    tokens = lefts[0].shape[1]
    return pl.pallas_call(
        lambda *refs: weight_parts_body(count, group, flip, *refs),
        grid_spec=pltpu.PrefetchScalarGridSpec(
            num_scalar_prefetch=1,
            grid=(count,),
            in_specs=[whole(v) for v in lefts] + [whole(v) for v in rights],
            out_specs=[pl.BlockSpec((1,) + shape[1:], lambda w, at: (w, 0, 0, 0, 0))] * 2,
        ),
        out_shape=[jax.ShapeDtypeStruct(shape, bf16)] * 2,
        cost_estimate=pl.CostEstimate(
            flops=2 * count * tokens * 8 * own_rows * columns * len(group),
            transcendentals=0,
            bytes_accessed=count * tokens * (8 * own_rows + columns * len(group)) * 2,
        ),
        name="weight_parts",
    )(at, *lefts, *rights)


def swap(value):
    size = lax.axis_size("dp")
    return lax.ppermute(value, "dp", [(i, i ^ 1) for i in range(size)])


def across(value, bit):
    size = lax.axis_size("dp")
    return lax.ppermute(value, "dp", [(i, i ^ (1 << bit)) for i in range(size)])


def around(value, by):
    size = lax.axis_size("tensor")
    by = by % size
    return lax.ppermute(value, "tensor", [(i, (i + by) % size) for i in range(size)])


def along_sequence(value, pieces, forward):
    size = lax.axis_size("tensor")
    pairs = [(i, i + 1) for i in range(size - 1) if (i + 1) % pieces]
    if not forward:
        pairs = [(b, a) for a, b in pairs]
    return lax.ppermute(value, "tensor", pairs)


class Place:
    def __init__(self):
        dp = lax.axis_index("dp")
        self.core = dp % 2
        self.slots = lax.axis_size("tensor")
        self.slot = lax.axis_index("tensor")
        self.bits = [b for b in range(1, lax.axis_size("dp").bit_length() - 1)]
        self.side = {b: (dp >> b) % 2 for b in range(lax.axis_size("dp").bit_length() - 1)}

    def gather_slots(self, block):
        blocks = [block] + [around(block, d) for d in range(1, self.slots)]
        shape = (block.shape[0], self.slots, block.shape[1])
        index = lax.broadcasted_iota(jnp.int32, shape, 1)
        out = jnp.broadcast_to(block[:, None, :], shape)
        for d in range(1, self.slots):
            from_slot = (self.slot - d) % self.slots
            out = jnp.where(index == from_slot, blocks[d][:, None, :], out)
        return out

    def scatter_slots(self, blocks):
        def block(at):
            return lax.dynamic_index_in_dim(blocks, at % self.slots, 1, keepdims=False)

        total = block(self.slot).astype(f32)
        for d in range(1, self.slots):
            total = total + around(block(self.slot + d), d).astype(f32)
        return total

    def ordered(self, bit, mine, other, axis):
        mine, other = jnp.expand_dims(mine, axis), jnp.expand_dims(other, axis)
        low = self.side[bit] == 0
        return jnp.where(
            low,
            jnp.concatenate([mine, other], axis=axis),
            jnp.concatenate([other, mine], axis=axis),
        )

    def gather_rows(self, block, upward):
        done = block
        for bit in self.bits if upward else self.bits[::-1]:
            axis = 0 if upward else len(done.shape) - 2
            done = self.ordered(bit, done, across(done, bit), axis)
        return done.reshape((-1, block.shape[1]))

    def scatter_rows(self, whole, upward, low_bit=1):
        bits = [b for b in self.bits if b >= low_bit]
        if low_bit == 0:
            bits = [0] + bits
        count = len(bits)
        rows = whole.shape[0] >> count
        left = sorted(bits, reverse=True)
        now = whole.reshape((2,) * count + (rows, whole.shape[1]))
        for bit in bits if upward else bits[::-1]:
            axis = left.index(bit)
            left.remove(bit)
            side = self.side[bit]
            keep = lax.dynamic_index_in_dim(now, side, axis, keepdims=False)
            give = lax.dynamic_index_in_dim(now, 1 - side, axis, keepdims=False)
            now = (keep.astype(f32) + across(give, bit).astype(f32)).astype(whole.dtype)
        return now

    def gather_weight(self, mine, other):
        both = self.ordered(0, mine, other, 0).reshape((-1, mine.shape[1]))
        blocks = self.gather_slots(both)
        half = self.slots // 2
        first = blocks[:, :half].reshape((both.shape[0], -1))
        second = blocks[:, half:].reshape((both.shape[0], -1))
        return jnp.concatenate(
            [self.gather_rows(first, True), self.gather_rows(second, False)], axis=1
        )

    def scatter_weight(self, part):
        columns = part.shape[1] // 2
        half = self.slots // 2
        first = self.scatter_rows(part[:, :columns], False)
        second = self.scatter_rows(part[:, columns:], True)
        rows = first.shape[0]
        blocks = jnp.concatenate(
            [first.reshape((rows, half, -1)), second.reshape((rows, half, -1))], axis=1
        )
        mine = self.scatter_slots(blocks).reshape((2, rows // 2, -1))
        keep = lax.dynamic_index_in_dim(mine, self.core, 0, keepdims=False)
        give = lax.dynamic_index_in_dim(mine, 1 - self.core, 0, keepdims=False)
        out = self.ordered(0, keep, swap(give), 1)
        return out.reshape((rows // 2, -1))

    def fast(self, half_channels):
        return len(self.bits) == 2 and half_channels % 128 == 0

    def offsets(self, own_rows, half_channels):
        chip = lax.axis_index("dp") // 2
        rows = [(chip ^ k) * 2 * own_rows for k in range(4)]
        columns = [(self.slot - d) % self.slots * half_channels for d in range(self.slots)]
        return jnp.stack(rows + columns).astype(jnp.int32)

    def unit(self, d, block):
        first, second = self.bits if d % 2 == 0 else self.bits[::-1]
        return across(block, first), across(block, second)

    def forward(self, d, one):
        return across(one, self.bits[1] if d % 2 == 0 else self.bits[0])

    def items(self, d, here, one, two, both):
        order = (here, one, two, both) if d % 2 == 0 else (here, two, one, both)
        return [(block, d, k) for k, block in enumerate(order)]

    def first_exchange(self, at, give):
        return across(give, self.bits[1 - at])

    def second_term(self, keep, came):
        return (keep[:, :, 1].astype(f32) + came[:, :, 1].astype(f32)).astype(bf16)

    def second_exchange(self, at, term):
        return across(term, self.bits[at])

    def slot_sum(self, keeps, cames, lasts, groups):
        own = {}
        for group, keep, came, last in zip(groups, keeps, cames, lasts):
            total = keep[:, :, 0].astype(f32) + came[:, :, 0].astype(f32) + last.astype(f32)
            for i, d in enumerate(group):
                own[d] = total[:, i]
        return own[0], [around(own[d].astype(bf16), -d) for d in range(1, self.slots)]

    def to_owner(self, own, others):
        total = own
        for other in others:
            total = total + other.astype(f32)
        weights, rows, columns = total.shape
        total = total.reshape((weights, 2, rows // 2, columns))
        keep = lax.dynamic_index_in_dim(total, self.core, 1, keepdims=False)
        give = lax.dynamic_index_in_dim(total, 1 - self.core, 1, keepdims=False)
        out = self.ordered(0, keep, swap(give), 2)
        return out.reshape((weights, rows // 2, 2 * columns))

    def sum_chips(self, value):
        for bit in self.bits:
            value = value + across(value, bit)
        return value

    def sum_slots(self, value):
        total = value.astype(f32)
        for d in range(1, self.slots):
            total = total + around(value, d).astype(f32)
        return total


def on_device_general(
    x_in,
    segment_ids,
    norm_gain,
    w_x,
    w_z,
    w_bc,
    w_dt,
    conv_x,
    conv_x_bias,
    conv_bc,
    conv_bc_bias,
    dt_bias,
    a_log,
    d_skip,
    gate_gain,
    w_out,
    cotangent,
):
    place = Place()
    core, slots, slot = place.core, place.slots, place.slot
    length, features = x_in.shape
    sequences, whole_length = segment_ids.shape
    pieces = whole_length // length
    own_rows = w_x.shape[0]
    slot_channels = w_x.shape[1]
    slot_heads = w_dt.shape[1]
    half_channels = slot_channels // 2
    half_heads = slot_heads // 2
    channels = half_channels * slots
    heads = half_heads * slots
    all_channels = 2 * channels
    all_heads = 2 * heads
    bc_width = w_bc.shape[1]
    n_chunks = length // CH

    def split(weight):
        return weight.reshape((own_rows, 2, half_channels))

    stacked = jnp.stack([split(w_x), split(w_z), split(w_out.T)])
    mine = lax.dynamic_index_in_dim(stacked, core, 2, keepdims=False)
    other = swap(lax.dynamic_index_in_dim(stacked, 1 - core, 2, keepdims=False))
    wx = place.gather_weight(mine[0], other[0])
    dt_slots = place.gather_slots(w_dt).reshape((own_rows, all_heads))
    thin = jnp.concatenate([w_bc, dt_slots, norm_gain[:, None]], axis=1)
    thin = jnp.pad(thin, ((0, 0), (0, bc_width + 128 - thin.shape[1])))
    thin = place.ordered(0, thin, swap(thin), 0).reshape((2 * own_rows, -1))
    thin = place.gather_rows(thin, True)
    wz = place.gather_weight(mine[1], other[1])
    wo = place.gather_weight(mine[2], other[2])

    rows = jnp.concatenate(
        [
            conv_x,
            conv_x_bias[None],
            gate_gain[None],
            jnp.pad(jnp.concatenate([dt_bias, a_log, d_skip])[None], ((0, 0), (0, slot_channels - 3 * slot_heads))),
            jnp.zeros((1, slot_channels), f32),
        ],
        axis=0,
    )
    rows = place.gather_slots(rows)
    own = lax.dynamic_index_in_dim(
        rows.reshape((8, slots, 2, half_channels)), core, 2, keepdims=False
    ).reshape((8, channels))
    gain_row = own[5:6]
    lane = jnp.arange(128)
    head_at = lane % 32
    global_head = (head_at // half_heads) * slot_heads + core * half_heads + head_at % half_heads
    pick = ((lane[:, None] == global_head[None, :]) & (head_at < heads)[None, :]).astype(f32)
    small = rows[6, :, : 3 * slot_heads].reshape((slots, 3, slot_heads)).transpose(1, 0, 2)
    small = jnp.pad(small.reshape((3, all_heads)), ((0, 5), (0, 128 - all_heads)))
    small = exact(small, pick)
    bias_lanes = small[0]
    rate_lanes = jnp.where(head_at < heads, -jnp.exp(small[1]), 0.0)
    to_heads = head_map(channels, f32)
    skip_row = exact(small[2:3] * (lane < 32), to_heads.T)
    cw = jnp.concatenate([own[:5], skip_row, jnp.zeros((2, channels), f32)], axis=0)

    padded = jnp.pad(segment_ids, ((0, 0), (HALO, HALO)), constant_values=-1)
    ids_own = lax.dynamic_slice(
        padded, (slot // pieces, (slot % pieces) * length), (1, length + 2 * HALO)
    )
    ids_all = jnp.concatenate([ids_own, swap(ids_own)], axis=0)
    ids = ids_all[:, HALO : HALO + length]
    before = ids_all[:, HALO - 1]

    def near(k):
        return ids_all[:, HALO + k : HALO + k + length] == ids

    flags = [near(-1), near(-2), near(-3), ids, near(1), near(2), near(3), jnp.zeros_like(ids)]
    flags = jnp.stack([v.astype(f32) for v in flags], axis=-1)

    x_rows = jnp.concatenate([along_sequence(x_in[-HALO:], pieces, True), x_in], axis=0)
    tokens_ext = x_rows.astype(f32)
    inv_ext = lax.rsqrt(jnp.mean(tokens_ext * tokens_ext, axis=-1, keepdims=True) + epsilon)
    gain = thin[:, bc_width + all_heads].astype(f32)[None, :]
    normed_own = (tokens_ext * inv_ext * gain).astype(bf16)
    normed_other = swap(normed_own)
    normed_ext = jnp.concatenate([normed_own, normed_other], axis=0)
    normed = jnp.concatenate([normed_own[HALO:], normed_other[HALO:]], axis=0)
    tokens, inv_rms = tokens_ext[HALO:], inv_ext[HALO:]
    cot = jnp.concatenate([cotangent, swap(cotangent)], axis=0)

    dt_pick = jnp.dot(thin[:, bc_width:], pick.astype(bf16), preferred_element_type=f32).astype(bf16)
    thin_proj = mm(normed_ext, jnp.concatenate([thin[:, :bc_width], dt_pick], axis=1))
    thin_proj = thin_proj.reshape((2, HALO + length, -1))
    bc_ext = thin_proj[:, :, :bc_width]
    dt_in = thin_proj[:, HALO:, bc_width:] + bias_lanes
    x_ext = mm(normed_ext, wx).reshape((2, HALO + length, channels))

    bc_pre = conv_bc_bias + conv_bc[0] * bc_ext[:, HALO:]
    for k in range(1, conv_bc.shape[0]):
        shifted = bc_ext[:, HALO - k : HALO - k + length]
        bc_pre = bc_pre + conv_bc[k] * shifted * flags[:, :, k - 1 : k]
    bc_act = jax.nn.silu(bc_pre)
    bc_turned = bc_act.astype(bf16).transpose(0, 2, 1)
    c_low = bc_act[:, :, bc_width // 2 :].astype(bf16)

    step = jax.nn.softplus(dt_in)
    log_step = (step * rate_lanes).reshape((2 * n_chunks, CH, 128))
    tri = (jnp.arange(CH)[:, None] >= jnp.arange(CH)[None, :]).astype(f32)
    running = jnp.einsum("ts,csh->cth", tri, log_step, precision=highest)
    running = running.reshape((2, n_chunks, CH, 128))
    last = running[:, :, -1:, :]
    ids_chunks = ids.reshape((2, n_chunks, CH, 1))
    chunk_end = ids_chunks[:, :, -1:, :]
    chunk_before = jnp.concatenate(
        [before[:, None, None, None], chunk_end[:, :-1]], axis=1
    )
    still = (chunk_end == chunk_before).astype(f32)
    alpha = still * jnp.exp(last)
    lead = jnp.cumsum(last, axis=1) - last
    since_piece = (ids_chunks == before[:, None, None, None]).astype(f32) * jnp.exp(running + lead)
    since_piece = since_piece.reshape((2 * length, 128))
    group_lane = lane // 32
    hv = jnp.where(
        group_lane == 0,
        running * LOG2E,
        jnp.where(
            group_lane == 1,
            step.reshape((2, n_chunks, CH, 128)),
            jnp.where(
                group_lane == 2,
                (ids_chunks == chunk_before).astype(f32) * jnp.exp(running),
                (ids_chunks == chunk_end).astype(f32) * jnp.exp(last - running),
            ),
        ),
    ).reshape((2, length, 128))
    rv = jnp.concatenate(
        [
            hv[:, :, :24].transpose(0, 2, 1),
            ids.astype(f32)[:, None, :],
            jnp.zeros((2, 7, length), f32),
        ],
        axis=1,
    )
    first_lanes = (lane < 32).astype(f32)
    al = exact((alpha * first_lanes).reshape((2 * n_chunks, 128)), to_heads.T)
    al = al.reshape((2, n_chunks, channels))
    whole_alpha = jnp.prod(al, axis=1, keepdims=True)
    al = jnp.pad(al, ((0, 0), (0, 8 - n_chunks), (0, 0)))
    wide_since = mm((since_piece * first_lanes).astype(bf16), to_heads.T.astype(bf16))
    wide_since = wide_since.reshape((2, length, channels))

    def hand_on(local, forward):
        low = local.astype(bf16)
        for _ in range(pieces - 2):
            came = along_sequence(low, pieces, forward)
            low = (local + whole_alpha * came.astype(f32)).astype(bf16)
        return along_sequence(low, pieces, forward)

    y_here, states = scan_fwd(hv, flags, rv, al, bc_act, bc_turned, x_ext, cw, CH)
    state_in = hand_on(states[:, -1], True)
    y = y_here + wide_since * lax.dot_general(
        c_low, state_in, (((2,), (1,)), ((0,), (0,))), preferred_element_type=f32
    )

    gate_in = mm(normed, wz)
    mixed_grad = mm(cot, wo)
    y = y.reshape((2 * length, channels))
    sig = jax.nn.sigmoid(gate_in)
    act = gate_in * sig
    gated = y * act
    scaled = mixed_grad * gain_row
    sums = jnp.stack([jnp.sum(gated * gated, axis=1), jnp.sum(scaled * gated, axis=1)])
    sums = sums.reshape((2, 2, length))
    sums = (sums + swap(sums)[:, ::-1]).reshape((2, 2 * length))
    gate_rms = lax.rsqrt(sums[0] / all_channels + epsilon)[:, None]
    mixed = (gated * gate_rms * gain_row).astype(bf16)
    gate_gain_part = jnp.sum(mixed_grad * gated * gate_rms, axis=0)
    gated_grad = gate_rms * scaled - gated * gate_rms**3 * (sums[1] / all_channels)[:, None]
    y_grad = (gated_grad * act).reshape((2, length, channels))
    gate_grad = (gated_grad * y * sig * (1.0 + gate_in * (1.0 - sig))).astype(bf16)

    state_grad = lax.dot_general(
        c_low, (y_grad * wide_since).astype(bf16), (((1,), (1,)), ((0,), (0,))), preferred_element_type=f32
    )
    state_grad = hand_on(state_grad, False)
    wo_part = tmm(cot, mixed).astype(bf16)
    w_out_grad = place.scatter_weight(wo_part).T
    branch = mmt(mixed, wo)
    block_out = (tokens + branch[:length] + swap(branch[length:].astype(bf16)).astype(f32)).astype(bf16)
    wz_part = tmm(normed, gate_grad).astype(bf16)
    w_z_grad = place.scatter_weight(wz_part)

    x_low, tail, head, dbc, dcol, drow, dcw = scan_bwd(
        hv, flags, rv, al, bc_act, bc_turned, x_ext, cw, y_grad, states, state_in, state_grad, CH
    )

    head = along_sequence(head, pieces, False)

    def past_end(begin, taps):
        total = jnp.zeros((begin.shape[0], HALO, begin.shape[2]), f32)
        for k in range(1, taps.shape[0]):
            moved = jnp.pad(begin[:, :k], ((0, 0), (HALO - k, 0), (0, 0)))
            total = total + taps[k] * moved * flags[: begin.shape[0], length - HALO :, 3 + k : 4 + k]
        return total

    fixed = (tail + past_end(head, own[:4])).astype(bf16)
    x_low = lax.dynamic_update_slice(x_low, fixed, (0, length - HALO, 0)).reshape((2 * length, channels))

    bc_grad = dbc[0] + swap(dbc[1])
    pre = bc_pre[0]
    sig_bc = jax.nn.sigmoid(pre)
    bc_dpre = bc_grad * (sig_bc * (1.0 + pre * (1.0 - sig_bc)))
    bc_head = along_sequence(bc_dpre[:8], pieces, False)
    bc_raw = conv_bc[0] * bc_dpre
    bc_taps = [jnp.sum(bc_dpre * bc_ext[0, HALO:], axis=0)]
    longer = jnp.concatenate([bc_dpre, bc_head], axis=0)
    for k in range(1, conv_bc.shape[0]):
        bc_raw = bc_raw + conv_bc[k] * longer[k : k + length] * flags[0, :, 3 + k : 4 + k]
        shifted = bc_ext[0, HALO - k : HALO - k + length]
        bc_taps.append(jnp.sum(bc_dpre * shifted * flags[0, :, k - 1 : k], axis=0))
    bc_low = bc_raw.astype(bf16)
    bc_small = jnp.stack(bc_taps + [jnp.sum(bc_dpre, axis=0)] + [jnp.zeros((bc_width,), f32)] * 3)
    bc_small = place.sum_chips(bc_small + swap(bc_small))
    bc_small = place.sum_slots(bc_small)

    dcum = dcol[:, :, :128] - jnp.pad(drow.transpose(0, 2, 1), ((0, 0), (0, 0), (0, 96)))
    dlog = jnp.einsum("ts,csh->cth", tri.T, dcum.reshape((2 * n_chunks, CH, 128)), precision=highest)
    dstep = dcol[:, :, 128:] + dlog.reshape((2, length, 128)) * rate_lanes
    dt_raw = (dstep * jax.nn.sigmoid(dt_in)).reshape((2 * length, 128))
    rate_part = jnp.sum(dlog * log_step, axis=(0, 1))
    place_back = (pick * first_lanes).T.astype(bf16)
    dt_low = mm(dt_raw.astype(bf16), place_back).astype(bf16)

    dcw = jnp.sum(dcw, axis=0)
    head_rows = jnp.stack([jnp.sum(dt_raw, axis=0), rate_part]) * first_lanes
    head_rows = exact(head_rows, to_heads.T)
    packed = jnp.concatenate(
        [dcw[:5], gate_gain_part[None], dcw[5:6], head_rows, jnp.zeros((7, channels), f32)], axis=0
    )
    packed = place.sum_chips(packed).reshape((16, slots, half_channels))
    packed = place.scatter_slots(packed)
    packed = place.ordered(0, packed, swap(packed), 1).reshape((16, slot_channels))
    by_head = packed[6:9].reshape((3, slot_heads, 64))

    wx_part = tmm(normed, x_low).astype(bf16)
    w_x_grad = place.scatter_weight(wx_part)
    thin_low = jnp.concatenate(
        [jnp.concatenate([bc_low, jnp.zeros_like(bc_low)], axis=0), dt_low], axis=1
    )
    thin_part = tmm(normed, thin_low).astype(bf16)
    thin_grad = place.scatter_rows(thin_part, True, low_bit=0)
    thin_grad = place.sum_slots(thin_grad)
    w_bc_grad = thin_grad[:, :bc_width]
    w_dt_grad = lax.dynamic_slice_in_dim(thin_grad, bc_width + slot * slot_heads, slot_heads, 1)

    normed_grad = mmt(x_low, wx) + mmt(gate_grad, wz) + mmt(thin_low, thin)
    normed_grad = normed_grad[:length] + swap(normed_grad[length:].astype(bf16)).astype(f32)
    gain_part = jnp.sum(normed_grad * tokens * inv_rms, axis=0)
    pushed = normed_grad * gain
    x_grad = (
        cotangent.astype(f32)
        + inv_rms * pushed
        - tokens * inv_rms**3 * jnp.mean(pushed * tokens, axis=-1, keepdims=True)
    )
    gain_rows = gain_part.reshape((features // own_rows * 2, own_rows // 2))
    gain_rows = place.scatter_rows(gain_rows, True, low_bit=0)
    norm_gain_grad = place.sum_slots(gain_rows).reshape((own_rows,))
    return (
        block_out,
        x_grad,
        norm_gain_grad,
        w_x_grad,
        w_z_grad,
        w_bc_grad,
        w_dt_grad,
        packed[:4],
        packed[4],
        bc_small[:4],
        bc_small[4],
        by_head[1, :, 0],
        by_head[2, :, 0],
        jnp.sum(by_head[0], axis=1),
        packed[5],
        w_out_grad,
    )


def tie(*values):
    return lax.optimization_barrier(values)


def on_device(*args):
    if Place().fast(args[3].shape[1] // 2):
        return on_device_fast(*args)
    return on_device_general(*args)


def on_device_fast(
    x_in,
    segment_ids,
    norm_gain,
    w_x,
    w_z,
    w_bc,
    w_dt,
    conv_x,
    conv_x_bias,
    conv_bc,
    conv_bc_bias,
    dt_bias,
    a_log,
    d_skip,
    gate_gain,
    w_out,
    cotangent,
):
    place = Place()
    core, slots, slot = place.core, place.slots, place.slot
    length, features = x_in.shape
    sequences, whole_length = segment_ids.shape
    pieces = whole_length // length
    own_rows = w_x.shape[0]
    slot_channels = w_x.shape[1]
    slot_heads = w_dt.shape[1]
    half_channels = slot_channels // 2
    half_heads = slot_heads // 2
    channels = half_channels * slots
    heads = half_heads * slots
    all_channels = 2 * channels
    all_heads = 2 * heads
    bc_width = w_bc.shape[1]
    n_chunks = length // CH
    groups = [tuple(range(0, slots, 2)), tuple(range(1, slots, 2))]
    at = place.offsets(own_rows, half_channels)

    def split(weight):
        return weight.reshape((own_rows, 2, half_channels))

    stacked = jnp.stack([split(w_x), split(w_z), split(w_out.T)])
    mine = lax.dynamic_index_in_dim(stacked, core, 2, keepdims=False)
    other = swap(lax.dynamic_index_in_dim(stacked, 1 - core, 2, keepdims=False))
    both = place.ordered(0, mine, other, 1).reshape((3, 2 * own_rows, half_channels))
    (
        both, x_in, segment_ids, norm_gain, w_bc, w_dt, conv_x, conv_x_bias, dt_bias, a_log, d_skip, gate_gain, cotangent,
    ) = tie(both, x_in, segment_ids, norm_gain, w_bc, w_dt, conv_x, conv_x_bias, dt_bias, a_log, d_skip, gate_gain, cotangent)

    wx_here = [both[:1]] + [around(both[:1], d) for d in range(1, slots)]
    wx_items = []
    for d in range(slots):
        one, two = place.unit(d, wx_here[d])
        wx_items += place.items(d, wx_here[d], one, two, place.forward(d, one))
    pair, _ = tie(both[1:], wx_here[1:])
    pair_here = [pair] + [around(pair, d) for d in range(1, slots)]

    rows = jnp.concatenate(
        [
            conv_x,
            conv_x_bias[None],
            gate_gain[None],
            jnp.pad(
                jnp.concatenate([dt_bias, a_log, d_skip])[None], ((0, 0), (0, slot_channels - 3 * slot_heads))
            ),
            jnp.zeros((1, slot_channels), f32),
            jnp.pad(w_dt.T.astype(f32), ((0, 0), (0, slot_channels - own_rows))),
        ],
        axis=0,
    )
    rows = place.gather_slots(rows)
    dt_slots = rows[8:, :, :own_rows].transpose(2, 1, 0).reshape((own_rows, all_heads)).astype(bf16)
    thin = jnp.concatenate([w_bc, dt_slots, norm_gain[:, None]], axis=1)
    thin = jnp.pad(thin, ((0, 0), (0, bc_width + 128 - thin.shape[1])))
    thin = place.ordered(0, thin, swap(thin), 0).reshape((2 * own_rows, -1))
    thin = place.gather_rows(thin, True)
    own = lax.dynamic_index_in_dim(
        rows[:8].reshape((8, slots, 2, half_channels)), core, 2, keepdims=False
    ).reshape((8, channels))
    gain_row = own[5:6]
    lane = jnp.arange(128)
    head_at = lane % 32
    global_head = (head_at // half_heads) * slot_heads + core * half_heads + head_at % half_heads
    pick = ((lane[:, None] == global_head[None, :]) & (head_at < heads)[None, :]).astype(f32)
    small = rows[6, :, : 3 * slot_heads].reshape((slots, 3, slot_heads)).transpose(1, 0, 2)
    small = jnp.pad(small.reshape((3, all_heads)), ((0, 5), (0, 128 - all_heads)))
    small = exact(small, pick)
    bias_lanes = small[0]
    rate_lanes = jnp.where(head_at < heads, -jnp.exp(small[1]), 0.0)
    to_heads = head_map(channels, f32)
    skip_row = exact(small[2:3] * (lane < 32), to_heads.T)
    cw = jnp.concatenate([own[:5], skip_row, jnp.zeros((2, channels), f32)], axis=0)

    padded = jnp.pad(segment_ids, ((0, 0), (HALO, HALO)), constant_values=-1)
    ids_own = lax.dynamic_slice(
        padded, (slot // pieces, (slot % pieces) * length), (1, length + 2 * HALO)
    )
    ids_all = jnp.concatenate([ids_own, swap(ids_own)], axis=0)
    ids = ids_all[:, HALO : HALO + length]
    before = ids_all[:, HALO - 1]

    def near(k):
        return ids_all[:, HALO + k : HALO + k + length] == ids

    flags = [near(-1), near(-2), near(-3), ids, near(1), near(2), near(3), jnp.zeros_like(ids)]
    flags = jnp.stack([v.astype(f32) for v in flags], axis=-1)

    x_rows = jnp.concatenate([along_sequence(x_in[-HALO:], pieces, True), x_in], axis=0)
    tokens_ext = x_rows.astype(f32)
    inv_ext = lax.rsqrt(jnp.mean(tokens_ext * tokens_ext, axis=-1, keepdims=True) + epsilon)
    gain = thin[:, bc_width + all_heads].astype(f32)[None, :]
    normed_own = (tokens_ext * inv_ext * gain).astype(bf16)
    normed_other = swap(normed_own)
    normed_ext = jnp.concatenate([normed_own, normed_other], axis=0)
    normed = jnp.concatenate([normed_own[HALO:], normed_other[HALO:]], axis=0)
    tokens, inv_rms = tokens_ext[HALO:], inv_ext[HALO:]
    cot = jnp.concatenate([cotangent, swap(cotangent)], axis=0)
    normed_turned, cot_turned = normed.T, cot.T

    dt_pick = jnp.dot(thin[:, bc_width:], pick.astype(bf16), preferred_element_type=f32).astype(bf16)
    thin_proj = mm(normed_ext, jnp.concatenate([thin[:, :bc_width], dt_pick], axis=1))
    thin_proj = thin_proj.reshape((2, HALO + length, -1))
    bc_ext = thin_proj[:, :, :bc_width]
    dt_in = thin_proj[:, HALO:, bc_width:] + bias_lanes

    bc_pre = conv_bc_bias + conv_bc[0] * bc_ext[:, HALO:]
    for k in range(1, conv_bc.shape[0]):
        shifted = bc_ext[:, HALO - k : HALO - k + length]
        bc_pre = bc_pre + conv_bc[k] * shifted * flags[:, :, k - 1 : k]
    bc_act = jax.nn.silu(bc_pre)
    bc_turned = bc_act.astype(bf16).transpose(0, 2, 1)
    c_low = bc_act[:, :, bc_width // 2 :].astype(bf16)

    step = jax.nn.softplus(dt_in)
    log_step = (step * rate_lanes).reshape((2 * n_chunks, CH, 128))
    tri = (jnp.arange(CH)[:, None] >= jnp.arange(CH)[None, :]).astype(f32)
    running = jnp.einsum("ts,csh->cth", tri, log_step, precision=highest)
    running = running.reshape((2, n_chunks, CH, 128))
    last = running[:, :, -1:, :]
    ids_chunks = ids.reshape((2, n_chunks, CH, 1))
    chunk_end = ids_chunks[:, :, -1:, :]
    chunk_before = jnp.concatenate([before[:, None, None, None], chunk_end[:, :-1]], axis=1)
    still = (chunk_end == chunk_before).astype(f32)
    alpha = still * jnp.exp(last)
    lead = jnp.cumsum(last, axis=1) - last
    since_piece = (ids_chunks == before[:, None, None, None]).astype(f32) * jnp.exp(running + lead)
    since_piece = since_piece.reshape((2 * length, 128))
    group_lane = lane // 32
    hv = jnp.where(
        group_lane == 0,
        running * LOG2E,
        jnp.where(
            group_lane == 1,
            step.reshape((2, n_chunks, CH, 128)),
            jnp.where(
                group_lane == 2,
                (ids_chunks == chunk_before).astype(f32) * jnp.exp(running),
                (ids_chunks == chunk_end).astype(f32) * jnp.exp(last - running),
            ),
        ),
    ).reshape((2, length, 128))
    rv = jnp.concatenate(
        [
            hv[:, :, :24].transpose(0, 2, 1),
            ids.astype(f32)[:, None, :],
            jnp.zeros((2, 7, length), f32),
        ],
        axis=1,
    )
    first_lanes = (lane < 32).astype(f32)
    al = exact((alpha * first_lanes).reshape((2 * n_chunks, 128)), to_heads.T)
    al = al.reshape((2, n_chunks, channels))
    whole_alpha = jnp.prod(al, axis=1, keepdims=True)
    al = jnp.pad(al, ((0, 0), (0, 8 - n_chunks), (0, 0)))
    wide_since = mm((since_piece * first_lanes).astype(bf16), to_heads.T.astype(bf16))
    wide_since = wide_since.reshape((2, length, channels))

    def hand_on(local, forward):
        low = local.astype(bf16)
        for _ in range(pieces - 2):
            came = along_sequence(low, pieces, forward)
            low = (local + whole_alpha * came.astype(f32)).astype(bf16)
        return along_sequence(low, pieces, forward)

    (wx_blocks, pair_here[0], pair_here[1], normed_ext, hv, rv, al, bc_act, bc_turned, cw, wide_since, c_low, normed,
     normed_turned, cot, cot_turned) = tie(
        [item[0] for item in wx_items], pair_here[0], pair_here[1], normed_ext, hv, rv, al, bc_act, bc_turned, cw,
        wide_since, c_low, normed, normed_turned, cot, cot_turned)
    wx_items = [(block,) + item[1:] for block, item in zip(wx_blocks, wx_items)]
    one, two, both_k = {}, {}, {}
    one[0], two[0] = place.unit(0, pair_here[0])
    one[1], two[1] = place.unit(1, pair_here[1])
    x_ext, wx = project(normed_ext, at, wx_items, 0, channels)
    x_ext = x_ext.reshape((2, HALO + length, channels))

    x_ext, one[0], two[0], one[1], two[1], pair_here[2], pair_here[3] = tie(
        x_ext, one[0], two[0], one[1], two[1], pair_here[2], pair_here[3])
    both_k[0], both_k[1] = place.forward(0, one[0]), place.forward(1, one[1])
    one[2], one[3] = across(pair_here[2], place.bits[0]), across(pair_here[3], place.bits[1])
    y_here, states = scan_fwd(hv, flags, rv, al, bc_act, bc_turned, x_ext, cw, CH)

    y_here, states, both_k[0], both_k[1], one[2], one[3] = tie(y_here, states, both_k[0], both_k[1], one[2], one[3])
    two[2], two[3] = across(pair_here[2], place.bits[1]), across(pair_here[3], place.bits[0])
    both_k[2], both_k[3] = place.forward(2, one[2]), place.forward(3, one[3])
    pair_items = []
    for d in range(slots):
        pair_items += place.items(d, pair_here[d], one[d], two[d], both_k[d])
    state_in = hand_on(states[:, -1], True)
    y = y_here + wide_since * lax.dot_general(
        c_low, state_in, (((2,), (1,)), ((0,), (0,))), preferred_element_type=f32
    )

    gate_in, wz = project(normed, at, pair_items, 0, channels)
    mixed_grad, wo = project(cot, at, pair_items, 1, channels)
    y = y.reshape((2 * length, channels))
    sig = jax.nn.sigmoid(gate_in)
    act = gate_in * sig
    gated = y * act
    scaled = mixed_grad * gain_row
    sums = jnp.stack([jnp.sum(gated * gated, axis=1), jnp.sum(scaled * gated, axis=1)])
    sums = sums.reshape((2, 2, length))
    sums = (sums + swap(sums)[:, ::-1]).reshape((2, 2 * length))
    gate_rms = lax.rsqrt(sums[0] / all_channels + epsilon)[:, None]
    mixed = (gated * gate_rms * gain_row).astype(bf16)
    gate_gain_part = jnp.sum(mixed_grad * gated * gate_rms, axis=0)
    gated_grad = gate_rms * scaled - gated * gate_rms**3 * (sums[1] / all_channels)[:, None]
    y_grad = (gated_grad * act).reshape((2, length, channels))
    gate_grad = (gated_grad * y * sig * (1.0 + gate_in * (1.0 - sig))).astype(bf16)
    state_grad = lax.dot_general(
        c_low, (y_grad * wide_since).astype(bf16), (((1,), (1,)), ((0,), (0,))), preferred_element_type=f32
    )
    state_grad = hand_on(state_grad, False)
    parts = [
        weight_parts(at, [normed_turned, cot_turned], [[gate_grad], [mixed]], group, own_rows, half_channels, flip)
        for flip, group in enumerate(groups)
    ]
    parts, y_grad, mixed, gate_grad = tie(parts, y_grad, mixed, gate_grad)
    pair_came = [place.first_exchange(i, parts[i][1]) for i in range(2)]

    branch_other = swap(mmt(mixed[length:], wo).astype(bf16))
    branch = mmt(mixed[:length], wo)
    block_out = (tokens + branch + branch_other.astype(f32)).astype(bf16)
    normed_grad_other = mmt(gate_grad[length:], wz)
    normed_grad = mmt(gate_grad[:length], wz)

    def backward(piece):
        return scan_bwd(
            hv, flags, rv, al, bc_act, bc_turned, x_ext, cw, y_grad, states, state_in, state_grad, CH, piece, 1
        )

    back_other = backward(1)
    pair_came, back_other, y_grad, block_out, normed_grad, normed_grad_other = tie(
        pair_came, back_other, y_grad, block_out, normed_grad, normed_grad_other)
    terms = [place.second_term(parts[i][0], pair_came[i]) for i in range(2)]
    pair_last = [place.second_exchange(i, terms[i]) for i in range(2)]
    back_own = backward(0)
    dbc_other = swap(back_other[3][0])
    pair_last, back_own, dbc_other, normed_grad, normed_grad_other = tie(
        pair_last, back_own, dbc_other, normed_grad, normed_grad_other)
    pair_own, pair_others = place.slot_sum([p[0] for p in parts], pair_came, pair_last, groups)

    head = along_sequence(jnp.concatenate([back_own[2], back_other[2]]), pieces, False)

    def past_end(begin, taps):
        total = jnp.zeros((begin.shape[0], HALO, begin.shape[2]), f32)
        for k in range(1, taps.shape[0]):
            moved = jnp.pad(begin[:, :k], ((0, 0), (HALO - k, 0), (0, 0)))
            total = total + taps[k] * moved * flags[: begin.shape[0], length - HALO :, 3 + k : 4 + k]
        return total

    fix = past_end(head, own[:4])
    x_low = [
        lax.dynamic_update_slice(back[0][0], (back[1][0] + fix[i]).astype(bf16), (length - HALO, 0))
        for i, back in enumerate((back_own, back_other))
    ]
    x_parts = [
        weight_parts(at, [normed_turned], [x_low], group, own_rows, half_channels, flip)
        for flip, group in enumerate(groups)
    ]
    x_came = [place.first_exchange(i, x_parts[i][1]) for i in range(2)]

    bc_grad = back_own[3][0] + dbc_other
    pre = bc_pre[0]
    sig_bc = jax.nn.sigmoid(pre)
    bc_dpre = bc_grad * (sig_bc * (1.0 + pre * (1.0 - sig_bc)))
    bc_head = along_sequence(bc_dpre[:8], pieces, False)
    bc_raw = conv_bc[0] * bc_dpre
    bc_taps = [jnp.sum(bc_dpre * bc_ext[0, HALO:], axis=0)]
    longer = jnp.concatenate([bc_dpre, bc_head], axis=0)
    for k in range(1, conv_bc.shape[0]):
        bc_raw = bc_raw + conv_bc[k] * longer[k : k + length] * flags[0, :, 3 + k : 4 + k]
        shifted = bc_ext[0, HALO - k : HALO - k + length]
        bc_taps.append(jnp.sum(bc_dpre * shifted * flags[0, :, k - 1 : k], axis=0))
    bc_low = bc_raw.astype(bf16)
    bc_small = jnp.stack(bc_taps + [jnp.sum(bc_dpre, axis=0)] + [jnp.zeros((bc_width,), f32)] * 11)
    bc_small = bc_small + swap(bc_small)

    dcol = jnp.concatenate([back_own[4], back_other[4]])
    drow = jnp.concatenate([back_own[5], back_other[5]])
    dcum = dcol[:, :, :128] - jnp.pad(drow.transpose(0, 2, 1), ((0, 0), (0, 0), (0, 96)))
    dlog = jnp.einsum("ts,csh->cth", tri.T, dcum.reshape((2 * n_chunks, CH, 128)), precision=highest)
    dstep = dcol[:, :, 128:] + dlog.reshape((2, length, 128)) * rate_lanes
    dt_raw = (dstep * jax.nn.sigmoid(dt_in)).reshape((2 * length, 128))
    rate_part = jnp.sum(dlog * log_step, axis=(0, 1))
    place_back = (pick * first_lanes).T.astype(bf16)
    dt_low = mm(dt_raw.astype(bf16), place_back).astype(bf16)
    thin_low = jnp.concatenate(
        [jnp.concatenate([bc_low, jnp.zeros_like(bc_low)], axis=0), dt_low], axis=1
    )
    thin_part = mm(normed_turned, thin_low).astype(bf16)

    dcw = back_own[6][0] + back_other[6][0]
    head_rows = jnp.stack([jnp.sum(dt_raw, axis=0), rate_part]) * first_lanes
    head_rows = exact(head_rows, to_heads.T)
    packed = jnp.concatenate(
        [dcw[:5], gate_gain_part[None], dcw[5:6], head_rows, jnp.zeros((7, channels), f32)], axis=0
    )
    packed = place.sum_chips(jnp.concatenate([packed, bc_small], axis=1))

    normed_grad_other = normed_grad_other + mmt(x_low[1], wx) + mmt(thin_low[length:], thin)
    normed_grad_other = swap(normed_grad_other.astype(bf16))
    normed_grad = normed_grad + mmt(x_low[0], wx) + mmt(thin_low[:length], thin)
    thin_grad = place.scatter_rows(thin_part, True, low_bit=0)

    x_came, packed, thin_grad, normed_grad_other, normed_grad, pair_own, pair_others = tie(
        x_came, packed, thin_grad, normed_grad_other, normed_grad, pair_own, pair_others)
    x_terms = [place.second_term(x_parts[i][0], x_came[i]) for i in range(2)]
    x_last = [place.second_exchange(i, x_terms[i]) for i in range(2)]

    bc_small = packed[:, channels:]
    packed = packed[:, :channels].reshape((16, slots, half_channels))

    def block(index):
        return lax.dynamic_index_in_dim(packed, index % slots, 1, keepdims=False)

    own_sums = jnp.concatenate([block(slot), bc_small], axis=1)
    for d in range(1, slots):
        own_sums = own_sums + around(jnp.concatenate([block(slot + d), bc_small], axis=1), d)
    packed = own_sums[:, :half_channels]
    bc_small = own_sums[:, half_channels:]
    packed = place.ordered(0, packed, swap(packed), 1).reshape((16, slot_channels))
    by_head = packed[6:9].reshape((3, slot_heads, 64))

    normed_grad = normed_grad + normed_grad_other.astype(f32)
    gain_part = jnp.sum(normed_grad * tokens * inv_rms, axis=0)
    pushed = normed_grad * gain
    x_grad = (
        cotangent.astype(f32)
        + inv_rms * pushed
        - tokens * inv_rms**3 * jnp.mean(pushed * tokens, axis=-1, keepdims=True)
    )
    gain_rows = gain_part.reshape((features // own_rows * 2, own_rows // 2))
    gain_rows = place.scatter_rows(gain_rows, True, low_bit=0)
    w_z_grad, w_out_grad = place.to_owner(pair_own, pair_others)

    x_last, gain_rows, x_grad = tie(x_last, gain_rows, x_grad)
    x_own, x_others = place.slot_sum([p[0] for p in x_parts], x_came, x_last, groups)
    thin_grad = place.sum_slots(thin_grad)
    w_bc_grad = thin_grad[:, :bc_width]
    w_dt_grad = lax.dynamic_slice_in_dim(thin_grad, bc_width + slot * slot_heads, slot_heads, 1)
    norm_gain_grad = place.sum_slots(gain_rows).reshape((own_rows,))
    w_x_grad = place.to_owner(x_own, x_others)[0]
    return (
        block_out,
        x_grad,
        norm_gain_grad,
        w_x_grad,
        w_z_grad,
        w_bc_grad,
        w_dt_grad,
        packed[:4],
        packed[4],
        bc_small[:4],
        bc_small[4],
        by_head[1, :, 0],
        by_head[2, :, 0],
        jnp.sum(by_head[0], axis=1),
        packed[5],
        w_out_grad.T,
    )


def solution(mesh):
    rows = P(("dp", "tensor"), None)
    both = P("dp", "tensor")
    heads = P("tensor")
    in_specs = (
        rows, P("dp", None), P("dp"), both, both, P("dp", None), both, P(None, "tensor"), heads,
        P(), P(), heads, heads, heads, heads, P("tensor", "dp"), rows,
    )
    out_specs = (
        rows, rows, P("dp"), both, both, P("dp", None), both, P(None, "tensor"), heads,
        P(), P(), heads, heads, heads, heads, P("tensor", "dp"),
    )
    return jax.shard_map(
        on_device, mesh=mesh, in_specs=in_specs, out_specs=out_specs, check_vma=False
    )
```

```python
import jax
import jax.numpy as jnp
from jax import lax
from jax.experimental import pallas as pl
from jax.experimental.pallas import tpu as pltpu
from jax.sharding import PartitionSpec as P

CH = 256
HALO = 16
GROUP = 4
LOG2E = 1.4426950408889634
epsilon = 1e-05
f32 = jnp.float32
bf16 = jnp.bfloat16
highest = lax.Precision.HIGHEST


def mm(a, b):
    return lax.dot_general(a, b, (((1,), (0,)), ((), ())), preferred_element_type=f32)


def mmt(a, b):
    return lax.dot_general(a, b, (((1,), (1,)), ((), ())), preferred_element_type=f32)


def tmm(a, b):
    return lax.dot_general(a, b, (((0,), (0,)), ((), ())), preferred_element_type=f32)


def exact(a, b):
    return lax.dot_general(
        a, b, (((1,), (0,)), ((), ())), precision=highest, preferred_element_type=f32
    )


def head_map(channels, kind):
    return (jnp.arange(channels)[:, None] // 64 == jnp.arange(128)[None, :]).astype(kind)


def spread(cols, first, rows, lane_low):
    parts = []
    for pair in range(GROUP // 2):
        left = jnp.broadcast_to(cols[:, first + 2 * pair : first + 2 * pair + 1], (rows, 128))
        right = jnp.broadcast_to(cols[:, first + 2 * pair + 1 : first + 2 * pair + 2], (rows, 128))
        parts.append(jnp.where(lane_low, left, right))
    return jnp.concatenate(parts, axis=1)


def conv_pre(x_ref, cw_ref, flags, start, rows):
    pre = cw_ref[4:5, :] + cw_ref[0:1, :] * x_ref[0, HALO + start : HALO + start + rows, :]
    for k in range(1, 4):
        shifted = x_ref[0, HALO + start - k : HALO + start - k + rows, :]
        pre = pre + (cw_ref[k : k + 1, :] * shifted) * flags[:, k - 1 : k]
    return pre


def masked_scores(cb_ref, bc_ref, fl_ref, rv_ref, n_chunks, rows):
    for c in range(n_chunks):
        at = slice(c * rows, (c + 1) * rows)
        ids_col = fl_ref[0, at, 3:4]
        ids_row = rv_ref[0, 24:25, at]
        t_at = lax.broadcasted_iota(jnp.int32, (rows, rows), 0)
        s_at = lax.broadcasted_iota(jnp.int32, (rows, rows), 1)
        keep = (ids_col == ids_row) & (t_at >= s_at)
        scores = lax.dot_general(
            bc_ref[0, at, 128:], bc_ref[0, at, :128], (((1,), (1,)), ((), ())),
            precision=highest, preferred_element_type=f32,
        )
        cb_ref[c] = jnp.where(keep, scores, 0.0)


def scan_fwd_body(n_chunks, rows, hv_ref, fl_ref, rv_ref, al_ref, bc_ref, bt_ref, x_ref, cw_ref, y_ref, st_ref, cb_ref):
    group = pl.program_id(1)
    turn = lax.rem(128 - GROUP * group, 128)

    @pl.when(group == 0)
    def _():
        masked_scores(cb_ref, bc_ref, fl_ref, rv_ref, n_chunks, rows)

    lane_low = lax.broadcasted_iota(jnp.int32, (rows, 128), 1) < 64
    state = jnp.zeros((128, GROUP * 64), f32)
    for c in range(n_chunks):
        at = slice(c * rows, (c + 1) * rows)
        cols = pltpu.roll(hv_ref[0, at, :], turn, 1)
        flags = fl_ref[0, at, :]
        pre = conv_pre(x_ref, cw_ref, flags, c * rows, rows)
        act = pre * jax.nn.sigmoid(pre)
        u = act * spread(cols, 32, rows, lane_low)
        ub = u.astype(bf16)
        y = cw_ref[5:6, :] * act
        if c > 0:
            c_rows = bc_ref[0, at, 128:].astype(bf16)
            y = y + mm(c_rows, state.astype(bf16)) * spread(cols, 64, rows, lane_low)
        scores = cb_ref[c]
        parts = []
        for pair in range(GROUP // 2):
            u_pair = ub[:, 128 * pair : 128 * pair + 128]
            outs = []
            for j in (2 * pair, 2 * pair + 1):
                gap = cols[:, j : j + 1] - rv_ref[0, pl.ds(group * GROUP + j, 1), at]
                mix = (scores * jnp.exp2(jnp.minimum(gap, 0.0))).astype(bf16)
                outs.append(mm(mix, u_pair))
            parts.append(jnp.where(lane_low, outs[0], outs[1]))
        y_ref[0, at, :] = y + jnp.concatenate(parts, axis=1)
        wu = (u * spread(cols, 96, rows, lane_low)).astype(bf16)
        state = al_ref[0, c : c + 1, :] * state + mm(bt_ref[0, :128, at], wu)
        st_ref[0, c] = state


def scan_fwd(hv, fl, rv, al, bc, bt, x_ext, cw, rows, first=0, count=2):
    length = hv.shape[1]
    n_chunks = length // rows
    width = GROUP * 64
    channels = x_ext.shape[2]
    groups = channels // width
    return pl.pallas_call(
        lambda *refs: scan_fwd_body(n_chunks, rows, *refs),
        grid=(count, groups),
        in_specs=[
            pl.BlockSpec((1, length, 128), lambda s, g: (first + s, 0, 0)),
            pl.BlockSpec((1, length, 8), lambda s, g: (first + s, 0, 0)),
            pl.BlockSpec((1, 32, length), lambda s, g: (first + s, 0, 0)),
            pl.BlockSpec((1, 8, width), lambda s, g: (first + s, 0, g)),
            pl.BlockSpec((1, length, 256), lambda s, g: (first + s, 0, 0)),
            pl.BlockSpec((1, 256, length), lambda s, g: (first + s, 0, 0)),
            pl.BlockSpec((1, HALO + length, width), lambda s, g: (first + s, 0, g)),
            pl.BlockSpec((8, width), lambda s, g: (0, g)),
        ],
        out_specs=[
            pl.BlockSpec((1, length, width), lambda s, g: (s, 0, g)),
            pl.BlockSpec((1, n_chunks, 128, width), lambda s, g: (s, 0, 0, g)),
        ],
        out_shape=[
            jax.ShapeDtypeStruct((count, length, channels), f32),
            jax.ShapeDtypeStruct((count, n_chunks, 128, channels), f32),
        ],
        scratch_shapes=[pltpu.VMEM((n_chunks, rows, rows), f32)],
        cost_estimate=pl.CostEstimate(
            flops=count * groups * GROUP * length * (rows + 256) * 128 * 2,
            transcendentals=count * groups * GROUP * length * rows,
            bytes_accessed=count * length * channels * 8,
        ),
        name="scan_fwd",
    )(hv, fl, rv, al, bc, bt, x_ext, cw)


def scan_bwd_body(
    n_chunks, rows, hv_ref, fl_ref, rv_ref, al_ref, bc_ref, bt_ref, x_ref, cw_ref, dy_ref, st_ref, sr_ref, rr_ref, seg_ref,
    xl_ref, tail_ref, head_ref, dbc_ref, dcol_ref, drow_ref, dcw_ref, cb_ref, dcb_ref, dpre_ref,
):
    group = pl.program_id(1)
    turn = lax.rem(128 - GROUP * group, 128)
    length = n_chunks * rows
    width = GROUP * 64

    @pl.when(group == 0)
    def _():
        masked_scores(cb_ref, bc_ref, fl_ref, rv_ref, n_chunks, rows)
        dcb_ref[...] = jnp.zeros_like(dcb_ref)
        dbc_ref[...] = jnp.zeros_like(dbc_ref)
        dcol_ref[...] = jnp.zeros_like(dcol_ref)
        drow_ref[...] = jnp.zeros_like(drow_ref)

    lane_low = lax.broadcasted_iota(jnp.int32, (rows, 128), 1) < 64
    lane = lax.broadcasted_iota(jnp.int32, (rows, 128), 1)
    row_at = lax.broadcasted_iota(jnp.int32, (rows, width), 0)
    grad_state = rr_ref[0].astype(f32)
    recv = sr_ref[0].astype(f32)
    states = [recv]
    carry = recv
    for c in range(n_chunks - 1):
        carry = al_ref[0, c : c + 1, :] * carry
        states.append(st_ref[0, c] + carry)
    tap_sums = [jnp.zeros((1, width), f32) for _ in range(6)]
    dpre_ref[length : length + 8, :] = jnp.zeros((8, width), f32)
    for c in reversed(range(n_chunks)):
        at = slice(c * rows, (c + 1) * rows)
        cols = pltpu.roll(hv_ref[0, at, :], turn, 1)
        flags = fl_ref[0, at, :]
        pre = conv_pre(x_ref, cw_ref, flags, c * rows, rows)
        sig = jax.nn.sigmoid(pre)
        act = pre * sig
        step_wide = spread(cols, 32, rows, lane_low)
        end_wide = spread(cols, 96, rows, lane_low)
        u = act * step_wide
        ub = u.astype(bf16)
        dy = dy_ref[0, at, :]
        dyb = dy.astype(bf16)
        b_rows = bc_ref[0, at, :128].astype(bf16)
        c_rows = bc_ref[0, at, 128:].astype(bf16)
        state_b = states[c].astype(bf16)
        dye = dy * spread(cols, 64, rows, lane_low)
        dyeb = dye.astype(bf16)
        gs_b = grad_state.astype(bf16)
        wub = (u * end_wide).astype(bf16)
        dbc_ref[0, at, 128:] += mmt(dyeb, state_b)
        dbc_ref[0, at, :128] += mmt(wub, gs_b)
        du_state = mm(b_rows, gs_b) * end_wide
        u_du = u * du_state
        at_end = jnp.sum(u_du, axis=0, keepdims=True) + al_ref[0, c : c + 1, :] * jnp.sum(
            grad_state * states[c], axis=0, keepdims=True
        )
        log_grad = dye * mm(c_rows, state_b) - u_du
        log_grad = jnp.where(row_at == rows - 1, log_grad + at_end, log_grad)
        grad_state = al_ref[0, c : c + 1, :] * grad_state + mm(bt_ref[0, 128:, at], dyeb)
        scores = cb_ref[c]
        dcb = dcb_ref[c]
        parts = []
        row_sums = jnp.zeros((rows, 128), f32)
        for pair in range(GROUP // 2):
            lanes = slice(128 * pair, 128 * pair + 128)
            u_pair = ub[:, lanes]
            dy_pair = dyb[:, lanes]
            outs = []
            for j in (2 * pair, 2 * pair + 1):
                gap = cols[:, j : j + 1] - rv_ref[0, pl.ds(group * GROUP + j, 1), at]
                decay = jnp.exp2(jnp.minimum(gap, 0.0))
                mix = (scores * decay).astype(bf16)
                own = lane_low if j % 2 == 0 else jnp.logical_not(lane_low)
                prod = mmt(jnp.where(own, dy_pair, jnp.zeros_like(dy_pair)), u_pair) * decay
                dcb = dcb + prod
                full = prod * scores
                row_sums = jnp.where(
                    lane == group * GROUP + j, jnp.sum(full, axis=1, keepdims=True), row_sums
                )
                drow_ref[0, pl.ds(group * GROUP + j, 1), at] = jnp.sum(full, axis=0, keepdims=True)
                outs.append(tmm(mix, dy_pair))
            parts.append(jnp.where(lane_low, outs[0], outs[1]))
        dcb_ref[c] = dcb
        du = jnp.concatenate(parts, axis=1) + du_state
        seg = seg_ref[...]
        dcol_ref[0, at, :128] += row_sums + lax.dot_general(
            log_grad, seg, (((1,), (0,)), ((), ())), precision=highest, preferred_element_type=f32
        )
        dcol_ref[0, at, 128:] += lax.dot_general(
            du * act, seg, (((1,), (0,)), ((), ())), precision=highest, preferred_element_type=f32
        )
        dact = du * step_wide + cw_ref[5:6, :] * dy
        dpre = dact * (sig * (1.0 + pre * (1.0 - sig)))
        dpre_ref[at, :] = dpre
        tap_sums[0] += jnp.sum(dpre * x_ref[0, HALO + c * rows : HALO + (c + 1) * rows, :], axis=0, keepdims=True)
        for k in range(1, 4):
            shifted = x_ref[0, HALO + c * rows - k : HALO + (c + 1) * rows - k, :]
            tap_sums[k] += jnp.sum(dpre * flags[:, k - 1 : k] * shifted, axis=0, keepdims=True)
        tap_sums[4] += jnp.sum(dpre, axis=0, keepdims=True)
        tap_sums[5] += jnp.sum(dy * act, axis=0, keepdims=True)
        xg = cw_ref[0:1, :] * dpre
        for k in range(1, 4):
            xg = xg + (cw_ref[k : k + 1, :] * dpre_ref[c * rows + k : (c + 1) * rows + k, :]) * flags[:, 3 + k : 4 + k]
        xl_ref[0, at, :] = xg.astype(bf16)
        if c == n_chunks - 1:
            tail_ref[0] = xg[rows - 16 :, :]
        if c == 0:
            head_ref[0] = dpre[:8, :]
    dcw_ref[0] = jnp.concatenate(tap_sums + [jnp.zeros((2, width), f32)], axis=0)

    @pl.when(group == pl.num_programs(1) - 1)
    def _():
        for c in range(n_chunks):
            at = slice(c * rows, (c + 1) * rows)
            ids_col = fl_ref[0, at, 3:4]
            ids_row = rv_ref[0, 24:25, at]
            t_at = lax.broadcasted_iota(jnp.int32, (rows, rows), 0)
            s_at = lax.broadcasted_iota(jnp.int32, (rows, rows), 1)
            keep = (ids_col == ids_row) & (t_at >= s_at)
            grad = jnp.where(keep, dcb_ref[c], 0.0).astype(bf16)
            dbc_ref[0, at, 128:] += mm(grad, bc_ref[0, at, :128].astype(bf16))
            dbc_ref[0, at, :128] += tmm(grad, bc_ref[0, at, 128:].astype(bf16))


def scan_bwd(hv, fl, rv, al, bc, bt, x_ext, cw, dy, states, s_recv, r_recv, rows, first=0, count=2):
    length = hv.shape[1]
    n_chunks = length // rows
    width = GROUP * 64
    channels = x_ext.shape[2]
    groups = channels // width
    seg = head_map(channels, f32)
    return pl.pallas_call(
        lambda *refs: scan_bwd_body(n_chunks, rows, *refs),
        grid=(count, groups),
        in_specs=[
            pl.BlockSpec((1, length, 128), lambda s, g: (first + s, 0, 0)),
            pl.BlockSpec((1, length, 8), lambda s, g: (first + s, 0, 0)),
            pl.BlockSpec((1, 32, length), lambda s, g: (first + s, 0, 0)),
            pl.BlockSpec((1, 8, width), lambda s, g: (first + s, 0, g)),
            pl.BlockSpec((1, length, 256), lambda s, g: (first + s, 0, 0)),
            pl.BlockSpec((1, 256, length), lambda s, g: (first + s, 0, 0)),
            pl.BlockSpec((1, HALO + length, width), lambda s, g: (first + s, 0, g)),
            pl.BlockSpec((8, width), lambda s, g: (0, g)),
            pl.BlockSpec((1, length, width), lambda s, g: (first + s, 0, g)),
            pl.BlockSpec((1, n_chunks, 128, width), lambda s, g: (first + s, 0, 0, g)),
            pl.BlockSpec((1, 128, width), lambda s, g: (first + s, 0, g)),
            pl.BlockSpec((1, 128, width), lambda s, g: (first + s, 0, g)),
            pl.BlockSpec((width, 128), lambda s, g: (g, 0)),
        ],
        out_specs=[
            pl.BlockSpec((1, length, width), lambda s, g: (s, 0, g)),
            pl.BlockSpec((1, 16, width), lambda s, g: (s, 0, g)),
            pl.BlockSpec((1, 8, width), lambda s, g: (s, 0, g)),
            pl.BlockSpec((1, length, 256), lambda s, g: (s, 0, 0)),
            pl.BlockSpec((1, length, 256), lambda s, g: (s, 0, 0)),
            pl.BlockSpec((1, 32, length), lambda s, g: (s, 0, 0)),
            pl.BlockSpec((1, 8, width), lambda s, g: (s, 0, g)),
        ],
        out_shape=[
            jax.ShapeDtypeStruct((count, length, channels), bf16),
            jax.ShapeDtypeStruct((count, 16, channels), f32),
            jax.ShapeDtypeStruct((count, 8, channels), f32),
            jax.ShapeDtypeStruct((count, length, 256), f32),
            jax.ShapeDtypeStruct((count, length, 256), f32),
            jax.ShapeDtypeStruct((count, 32, length), f32),
            jax.ShapeDtypeStruct((count, 8, channels), f32),
        ],
        scratch_shapes=[
            pltpu.VMEM((n_chunks, rows, rows), f32),
            pltpu.VMEM((n_chunks, rows, rows), f32),
            pltpu.VMEM((length + 8, width), f32),
        ],
        cost_estimate=pl.CostEstimate(
            flops=count * groups * GROUP * length * (rows + 256) * 128 * 6,
            transcendentals=count * groups * GROUP * length * rows,
            bytes_accessed=count * length * channels * 12,
        ),
        name="scan_bwd",
    )(hv, fl, rv, al, bc, bt, x_ext, cw, dy, states, s_recv, r_recv, seg)


def project_body(places, skip, at_ref, *refs):
    left_ref, right_ref, blocks, out_ref, full_ref = refs[0], refs[1], refs[2:-2], refs[-2], refs[-1]

    @pl.when(pl.program_id(0) == 0)
    def _():
        for ref, (d, k) in zip(blocks, places):
            rows, columns = ref.shape[1:]
            row = pl.multiple_of(at_ref[k], rows)
            column = pl.multiple_of(at_ref[4 + d], columns)
            full_ref[pl.ds(row, rows), pl.ds(column, columns)] = ref[0]
        out_ref[...] = mm(left_ref[skip:, :], full_ref[...])

    @pl.when(pl.program_id(0) == 1)
    def _():
        out_ref[...] = mm(right_ref[skip:, :], full_ref[...])


def project(acts, skip, at, items, weight, channels):
    rows, features = acts[0].shape
    rows = rows - skip
    blocks = [item[0] for item in items]
    places = [item[1:] for item in items]
    return pl.pallas_call(
        lambda *refs: project_body(places, skip, *refs),
        grid_spec=pltpu.PrefetchScalarGridSpec(
            num_scalar_prefetch=1,
            grid=(2,),
            in_specs=[pl.BlockSpec(v.shape, lambda i, at: (0, 0), pipeline_mode=pl.Buffered(1)) for v in acts]
            + [
                pl.BlockSpec((1,) + b.shape[1:], lambda i, at: (weight, 0, 0), pipeline_mode=pl.Buffered(1))
                for b in blocks
            ],
            out_specs=[
                pl.BlockSpec((rows, channels), lambda i, at: (i, 0)),
                pl.BlockSpec((features, channels), lambda i, at: (0, 0), pipeline_mode=pl.Buffered(1)),
            ],
        ),
        out_shape=[
            jax.ShapeDtypeStruct((2 * rows, channels), f32),
            jax.ShapeDtypeStruct((features, channels), bf16),
        ],
        cost_estimate=pl.CostEstimate(
            flops=4 * rows * features * channels,
            transcendentals=0,
            bytes_accessed=rows * features * 4 + rows * channels * 8 + features * channels * 4,
        ),
        name="project",
    )(at, *acts, *blocks)


def turn_body(x_ref, out_ref):
    out_ref[...] = x_ref[...].T


def turn(x):
    rows, columns = x.shape
    return pl.pallas_call(
        turn_body, out_shape=jax.ShapeDtypeStruct((columns, rows), x.dtype), name="turn", cost_estimate=pl.CostEstimate(flops=1, transcendentals=0, bytes_accessed=1)
    )(x)


def norm_body(x_ref, halo_ref, gain_ref, out_ref, turned_ref):
    def normed(ref, at):
        x = ref[at, :].astype(f32)
        inv = lax.rsqrt(jnp.mean(x * x, axis=-1, keepdims=True) + epsilon)
        return (x * inv * gain_ref[...]).astype(bf16)

    out_ref[:HALO, :] = normed(halo_ref, slice(0, HALO))
    for r in range(x_ref.shape[0] // 128):
        rows = normed(x_ref, slice(128 * r, 128 * r + 128))
        out_ref[HALO + 128 * r : HALO + 128 * r + 128, :] = rows
        turned_ref[:, 128 * r : 128 * r + 128] = rows.T


def norm(x, halo, gain):
    rows, features = x.shape
    return pl.pallas_call(
        norm_body,
        out_shape=[
            jax.ShapeDtypeStruct((HALO + rows, features), bf16),
            jax.ShapeDtypeStruct((features, rows), bf16),
        ],
        cost_estimate=pl.CostEstimate(flops=1, transcendentals=0, bytes_accessed=1),
        name="norm",
    )(x, halo, gain)


def prepare_body(
    own_ref, other_ref, thin_ref, pick_ref, lanes_ref, cbc_ref, ids_ref, row_ref,
    bcx_ref, pre_ref, act_ref, turned_ref, low_ref, dt_ref, log_ref, hv_ref, rv_ref, al_ref, since_ref, flags_ref,
    scr_ref,
):
    length = act_ref.shape[1]
    n_chunks = length // CH
    width = pre_ref.shape[2]
    channels = al_ref.shape[2]
    picked = mm(thin_ref[:, width:], pick_ref[...]).astype(bf16)
    weights = jnp.concatenate([thin_ref[:, :width], picked], axis=1)

    @pl.when(pl.program_id(0) == 0)
    def _():
        scr_ref[...] = mm(own_ref[...], weights)

    @pl.when(pl.program_id(0) == 1)
    def _():
        scr_ref[...] = mm(other_ref[...], weights)

    columns = ids_ref[0].T
    at = slice(HALO, HALO + length)
    ids = columns[at, :1]
    before = columns[HALO - 1 : HALO, :1]
    eight = lax.broadcasted_iota(jnp.int32, (length, 8), 1)
    flags = jnp.where(eight == 3, ids, 0.0)
    near = {}
    for j, k in enumerate((-1, -2, -3, 0, 1, 2, 3)):
        if k != 0:
            near[k] = (columns[HALO + k : HALO + k + length, :1] == ids).astype(f32)
            flags = jnp.where(eight == j, near[k], flags)
    flags_ref[0] = flags

    bcx_ref[0] = scr_ref[:, :width]
    pre = cbc_ref[4:5, :] + cbc_ref[0:1, :] * scr_ref[at, :width]
    for k in range(1, 4):
        pre = pre + cbc_ref[k : k + 1, :] * scr_ref[HALO - k : HALO - k + length, :width] * near[-k]
    act = pre * jax.nn.sigmoid(pre)
    pre_ref[0] = pre
    act_ref[0] = act
    turned_ref[0] = act.T.astype(bf16)
    low_ref[0] = act[:, width // 2 :].astype(bf16)

    dt_in = scr_ref[at, width:] + lanes_ref[0:1, :]
    dt_ref[0] = dt_in
    step = jnp.maximum(dt_in, 0.0) + jnp.log1p(jnp.exp(-jnp.abs(dt_in)))
    log_step = step * lanes_ref[1:2, :]
    log_ref[0] = log_step
    tri = (
        lax.broadcasted_iota(jnp.int32, (CH, CH), 0) >= lax.broadcasted_iota(jnp.int32, (CH, CH), 1)
    ).astype(f32)
    quarter = lax.broadcasted_iota(jnp.int32, (CH, 128), 1) // 32
    low_lanes = lax.broadcasted_iota(jnp.int32, (CH, 128), 1) < 32
    row_at = lax.broadcasted_iota(jnp.int32, (32, CH), 0)
    to_wide = (
        lax.broadcasted_iota(jnp.int32, (128, channels), 1) // 64 == lax.broadcasted_iota(jnp.int32, (128, channels), 0)
    ).astype(f32)
    eight_rows = lax.broadcasted_iota(jnp.int32, (8, 128), 0)
    alphas = jnp.zeros((8, 128), f32)
    lead = jnp.zeros((1, 128), f32)
    chunk_before = before
    for c in range(n_chunks):
        rows = slice(c * CH, (c + 1) * CH)
        running = exact(tri, log_step[rows])
        last = running[CH - 1 : CH, :]
        ids_c = ids[rows]
        chunk_end = ids_c[CH - 1 : CH, :]
        still = (chunk_end == chunk_before).astype(f32)
        alphas = jnp.where(eight_rows == c, still * jnp.exp(last), alphas)
        since = (ids_c == before).astype(f32) * jnp.exp(running + lead)
        since = jnp.where(low_lanes, since, 0.0).astype(bf16)
        since_ref[0, rows, :] = mm(since, to_wide.astype(bf16)).astype(bf16)
        hv = jnp.where(
            quarter == 0,
            running * LOG2E,
            jnp.where(
                quarter == 1,
                step[rows],
                jnp.where(
                    quarter == 2,
                    (ids_c == chunk_before).astype(f32) * jnp.exp(running),
                    (ids_c == chunk_end).astype(f32) * jnp.exp(last - running),
                ),
            ),
        )
        hv_ref[0, rows, :] = hv
        turned = hv.T[:32, :]
        rv_ref[0, :, rows] = jnp.where(
            row_at < 24, turned, jnp.where(row_at == 24, row_ref[0, 0:1, rows], 0.0)
        )
        lead = lead + last
        chunk_before = chunk_end
    first = lax.broadcasted_iota(jnp.int32, (8, 128), 1) < 32
    al_ref[0] = exact(jnp.where(first, alphas, 0.0), to_wide)


def prepare(own, other, thin, pick, lanes, cbc, ids_all, ids_rows, channels):
    length = own.shape[0] - HALO
    width = cbc.shape[1]
    whole = lambda v: pl.BlockSpec(v.shape, lambda s: (0,) * len(v.shape), pipeline_mode=pl.Buffered(1))
    piece = lambda shape: pl.BlockSpec((1,) + shape, lambda s: (s, 0, 0))
    outs = [
        ((HALO + length, width), f32), ((length, width), f32), ((length, width), f32), ((width, length), bf16),
        ((length, width // 2), bf16), ((length, 128), f32), ((length, 128), f32), ((length, 128), f32),
        ((32, length), f32), ((8, channels), f32), ((length, channels), bf16), ((length, 8), f32),
    ]
    return pl.pallas_call(
        prepare_body,
        grid=(2,),
        in_specs=[whole(v) for v in (own, other, thin, pick, lanes, cbc)]
        + [piece(ids_all.shape[1:]), piece(ids_rows.shape[1:])],
        out_specs=[piece(shape) for shape, _ in outs],
        out_shape=[jax.ShapeDtypeStruct((2,) + shape, kind) for shape, kind in outs],
        scratch_shapes=[pltpu.VMEM((HALO + length, width + 128), f32)],
        cost_estimate=pl.CostEstimate(flops=1, transcendentals=0, bytes_accessed=1),
        name="prepare",
    )(own, other, thin, pick, lanes, cbc, ids_all, ids_rows)


def gate_sums_body(here_ref, since_ref, low_ref, state_ref, gate_ref, grad_ref, gain_ref, y_ref, sums_ref):
    y = here_ref[...] + since_ref[...].astype(f32) * mm(low_ref[...], state_ref[0])
    y_ref[...] = y
    gate = gate_ref[...]
    gated = y * (gate * jax.nn.sigmoid(gate))
    scaled = grad_ref[...] * gain_ref[...]
    lane = lax.broadcasted_iota(jnp.int32, sums_ref.shape, 1)
    sums_ref[...] = jnp.where(
        lane == 0,
        jnp.sum(gated * gated, axis=1, keepdims=True),
        jnp.where(lane == 1, jnp.sum(scaled * gated, axis=1, keepdims=True), 0.0),
    )


def gate_sums(here, since, low, state, gate, grad, gain):
    tokens, channels = here.shape
    tile = 128
    per = tokens // tile // 2
    token = lambda width: pl.BlockSpec((tile, width), lambda i: (i, 0))
    return pl.pallas_call(
        gate_sums_body,
        grid=(tokens // tile,),
        in_specs=[
            token(channels), token(channels), token(low.shape[1]),
            pl.BlockSpec((1,) + state.shape[1:], lambda i: (i // per, 0, 0)),
            token(channels), token(channels), pl.BlockSpec((1, channels), lambda i: (0, 0)),
        ],
        out_specs=[token(channels), token(128)],
        out_shape=[jax.ShapeDtypeStruct((tokens, channels), f32), jax.ShapeDtypeStruct((tokens, 128), f32)],
        cost_estimate=pl.CostEstimate(flops=1, transcendentals=0, bytes_accessed=1),
        name="gate_sums",
    )(here, since, low, state, gate, grad, gain)


def gate_grads_body(
    all_channels, per, y_ref, since_ref, low_ref, gate_ref, grad_ref, gain_ref, sums_ref, came_ref,
    mixed_ref, gate_grad_ref, y_grad_ref, gain_grad_ref, state_ref,
):
    at = pl.program_id(0)
    y = y_ref[...]
    gate = gate_ref[...]
    grad = grad_ref[...]
    sums = sums_ref[...] + came_ref[...]
    gate_rms = lax.rsqrt(sums[:, 0:1] / all_channels + epsilon)
    inner = gate_rms * gate_rms * gate_rms * (sums[:, 1:2] / all_channels)
    sig = jax.nn.sigmoid(gate)
    act = gate * sig
    gated = y * act
    hat = gated * gate_rms
    mixed_ref[...] = (hat * gain_ref[...]).astype(bf16)
    gated_grad = gate_rms * (grad * gain_ref[...]) - gated * inner
    y_grad = gated_grad * act
    y_grad_ref[...] = y_grad
    gate_grad_ref[...] = (gated_grad * y * sig * (1.0 + gate * (1.0 - sig))).astype(bf16)
    part = jnp.sum((grad * hat).reshape((y.shape[0] // 8, 8, y.shape[1])), axis=0)
    pushed = tmm(low_ref[...], (y_grad * since_ref[...].astype(f32)).astype(bf16))

    @pl.when(at == 0)
    def _():
        gain_grad_ref[...] = part

    @pl.when(at > 0)
    def _():
        gain_grad_ref[...] += part

    @pl.when(lax.rem(at, per) == 0)
    def _():
        state_ref[0] = pushed

    @pl.when(lax.rem(at, per) > 0)
    def _():
        state_ref[0] += pushed


def gate_grads(y, since, low, gate, grad, gain, sums, came, all_channels):
    tokens, channels = y.shape
    tile = 128
    count = tokens // tile
    per = count // 2
    token = lambda width: pl.BlockSpec((tile, width), lambda i: (i, 0))
    turned = pl.BlockSpec((tile, 128), lambda i: (lax.rem(i + per, count), 0))
    return pl.pallas_call(
        lambda *refs: gate_grads_body(all_channels, per, *refs),
        grid=(count,),
        in_specs=[
            token(channels), token(channels), token(low.shape[1]), token(channels), token(channels),
            pl.BlockSpec((1, channels), lambda i: (0, 0)), token(128), turned,
        ],
        out_specs=[
            token(channels), token(channels), token(channels), pl.BlockSpec((8, channels), lambda i: (0, 0)),
            pl.BlockSpec((1, low.shape[1], channels), lambda i: (i // per, 0, 0)),
        ],
        out_shape=[
            jax.ShapeDtypeStruct((tokens, channels), bf16),
            jax.ShapeDtypeStruct((tokens, channels), bf16),
            jax.ShapeDtypeStruct((tokens, channels), f32),
            jax.ShapeDtypeStruct((8, channels), f32),
            jax.ShapeDtypeStruct((2, low.shape[1], channels), f32),
        ],
        cost_estimate=pl.CostEstimate(flops=1, transcendentals=0, bytes_accessed=1),
        name="gate_grads",
    )(y, since, low, gate, grad, gain, sums, came)


def small_grads_body(
    dbc_ref, came_ref, pre_ref, bcx_ref, flags_ref, own_col_ref, other_col_ref, own_row_ref, other_row_ref,
    log_ref, dt_ref, lanes_ref, back_ref, own_sums_ref, other_sums_ref, gain_ref, dpre_ref, dt_low_ref, taps_ref,
    packed_ref,
):
    length = dpre_ref.shape[0]
    width = dpre_ref.shape[1]
    channels = packed_ref.shape[1]
    pre = pre_ref[0]
    sig = jax.nn.sigmoid(pre)
    dpre = (dbc_ref[0] + came_ref[...]) * (sig * (1.0 + pre * (1.0 - sig)))
    dpre_ref[...] = dpre
    sums = [jnp.sum(dpre * bcx_ref[0, HALO:, :], axis=0, keepdims=True)]
    for k in range(1, 4):
        shifted = bcx_ref[0, HALO - k : HALO - k + length, :]
        sums.append(jnp.sum(dpre * shifted * flags_ref[0, :, k - 1 : k], axis=0, keepdims=True))
    sums.append(jnp.sum(dpre, axis=0, keepdims=True))
    taps_ref[...] = jnp.concatenate(sums + [jnp.zeros((11, width), f32)], axis=0)

    tri = (
        lax.broadcasted_iota(jnp.int32, (CH, CH), 1) >= lax.broadcasted_iota(jnp.int32, (CH, CH), 0)
    ).astype(f32)
    raw_sum = jnp.zeros((1, 128), f32)
    rate_sum = jnp.zeros((1, 128), f32)
    for p, (col_ref, row_ref) in enumerate(((own_col_ref, own_row_ref), (other_col_ref, other_row_ref))):
        for c in range(length // CH):
            rows = slice(c * CH, (c + 1) * CH)
            by_row = jnp.concatenate([row_ref[0, :, rows], jnp.zeros((96, CH), f32)], axis=0).T
            dlog = exact(tri, col_ref[0, rows, :128] - by_row)
            dstep = col_ref[0, rows, 128:] + dlog * lanes_ref[1:2, :]
            raw = dstep * jax.nn.sigmoid(dt_ref[p, rows, :])
            rate_sum += jnp.sum(dlog * log_ref[p, rows, :], axis=0, keepdims=True)
            raw_sum += jnp.sum(raw, axis=0, keepdims=True)
            dt_low_ref[p, rows, :] = mm(raw.astype(bf16), back_ref[...]).astype(bf16)
    to_wide = (
        lax.broadcasted_iota(jnp.int32, (128, channels), 1) // 64 == lax.broadcasted_iota(jnp.int32, (128, channels), 0)
    ).astype(f32)
    both = jnp.concatenate([raw_sum, rate_sum, jnp.zeros((6, 128), f32)], axis=0)
    first = lax.broadcasted_iota(jnp.int32, (8, 128), 1) < 32
    wide = exact(jnp.where(first, both, 0.0), to_wide)
    sums = own_sums_ref[0] + other_sums_ref[0]
    gain = jnp.sum(gain_ref[...], axis=0, keepdims=True)
    packed_ref[...] = jnp.concatenate(
        [sums[:5], gain, sums[5:6], wide[:2], jnp.zeros((7, channels), f32)], axis=0
    )


def small_grads(dbc, came, pre, *rest):
    length, width = came.shape
    channels = rest[-1].shape[1]
    return pl.pallas_call(
        small_grads_body,
        out_shape=[
            jax.ShapeDtypeStruct((length, width), f32),
            jax.ShapeDtypeStruct((2, length, 128), bf16),
            jax.ShapeDtypeStruct((16, width), f32),
            jax.ShapeDtypeStruct((16, channels), f32),
        ],
        cost_estimate=pl.CostEstimate(flops=1, transcendentals=0, bytes_accessed=1),
        name="small_grads",
    )(dbc, came, pre, *rest)


def normed_grads_body(
    dpre_ref, head_ref, flags_ref, cbc_ref, dt_low_ref, own_turned_ref, other_turned_ref, own_ref, other_ref, gate_ref,
    wx_ref, wz_ref, thin_ref, own_out_ref, other_out_ref, part_ref, low_ref, scr_ref,
):
    length, width = dpre_ref.shape

    @pl.when((pl.program_id(0) == 0) & (pl.program_id(1) == 0))
    def _():
        scr_ref[:length, :] = dpre_ref[...]
        scr_ref[length:, :] = head_ref[...]
        raw = cbc_ref[0:1, :] * dpre_ref[...]
        for k in range(1, 4):
            raw = raw + cbc_ref[k : k + 1, :] * scr_ref[k : k + length, :] * flags_ref[0, :, 3 + k : 4 + k]
        own = jnp.concatenate([raw.astype(bf16), dt_low_ref[0]], axis=1)
        other = jnp.concatenate([jnp.zeros((length, width), bf16), dt_low_ref[1]], axis=1)
        low_ref[:length, :] = own
        low_ref[length:, :] = other
        part_ref[...] = (mm(own_turned_ref[...], own) + mm(other_turned_ref[...], other)).astype(bf16)

    def total(ref, rows):
        return (
            mmt(ref[...], wx_ref[...]) + mmt(gate_ref[rows, :], wz_ref[...]) + mmt(low_ref[rows, :], thin_ref[...])
        )

    @pl.when(pl.program_id(0) == 0)
    def _():
        other_out_ref[...] = total(other_ref, slice(length, 2 * length)).astype(bf16)

    @pl.when(pl.program_id(0) == 1)
    def _():
        own_out_ref[...] = total(own_ref, slice(0, length))


def normed_grads(dpre, head, flags, cbc, dt_low, turned, x_low, gate_grad, wx, wz, thin):
    length, width = dpre.shape
    features = wx.shape[0]
    tile = features // 3
    last = features // tile - 1
    whole = lambda v: pl.BlockSpec(v.shape, lambda p, j: (0,) * len(v.shape), pipeline_mode=pl.Buffered(1))
    weight = lambda v: pl.BlockSpec((tile, v.shape[1]), lambda p, j: (j, 0))
    return pl.pallas_call(
        normed_grads_body,
        grid=(2, features // tile),
        in_specs=[whole(v) for v in (dpre, head, flags, cbc, dt_low, *turned, *x_low, gate_grad)]
        + [weight(v) for v in (wx, wz, thin)],
        out_specs=[
            pl.BlockSpec((length, tile), lambda p, j: (0, j * p)),
            pl.BlockSpec((length, tile), lambda p, j: (0, j * (1 - p) + last * p)),
            pl.BlockSpec((features, width + 128), lambda p, j: (0, 0), pipeline_mode=pl.Buffered(1)),
        ],
        out_shape=[
            jax.ShapeDtypeStruct((length, features), f32),
            jax.ShapeDtypeStruct((length, features), bf16),
            jax.ShapeDtypeStruct((features, width + 128), bf16),
        ],
        scratch_shapes=[pltpu.VMEM((2 * length, width + 128), bf16), pltpu.VMEM((length + 8, width), f32)],
        cost_estimate=pl.CostEstimate(
            flops=8 * length * features * features, transcendentals=0, bytes_accessed=8 * features * features
        ),
        name="normed_grads",
    )(dpre, head, flags, cbc, dt_low, *turned, *x_low, gate_grad, wx, wz, thin)


def x_grads_body(own_ref, came_ref, x_ref, cot_ref, gain_ref, out_ref, gain_grad_ref):
    grad = own_ref[...] + came_ref[...].astype(f32)
    x = x_ref[...].astype(f32)
    inv = lax.rsqrt(jnp.mean(x * x, axis=-1, keepdims=True) + epsilon)
    hat = x * inv
    part = jnp.sum((grad * hat).reshape((x.shape[0] // 8, 8, x.shape[1])), axis=0)
    pushed = grad * gain_ref[...]
    inner = jnp.mean(pushed * x, axis=-1, keepdims=True)
    out_ref[...] = cot_ref[...].astype(f32) + inv * pushed - hat * (inv * inv * inner)

    @pl.when(pl.program_id(0) == 0)
    def _():
        gain_grad_ref[...] = part

    @pl.when(pl.program_id(0) > 0)
    def _():
        gain_grad_ref[...] += part


def x_grads(own, came, x, cot, gain):
    tokens, features = own.shape
    tile = 128
    token = pl.BlockSpec((tile, features), lambda i: (i, 0))
    return pl.pallas_call(
        x_grads_body,
        grid=(tokens // tile,),
        in_specs=[token] * 4 + [pl.BlockSpec((1, features), lambda i: (0, 0))],
        out_specs=[token, pl.BlockSpec((8, features), lambda i: (0, 0))],
        out_shape=[jax.ShapeDtypeStruct((tokens, features), f32), jax.ShapeDtypeStruct((8, features), f32)],
        cost_estimate=pl.CostEstimate(flops=1, transcendentals=0, bytes_accessed=1),
        name="x_grads",
    )(own, came, x, cot, gain)


def weight_parts_body(count, group, flip, at_ref, *refs):
    keep_ref, give_ref = refs[-2:]
    rows, columns = keep_ref.shape[3:]
    rights_per = (len(refs) - 2) // count - 2
    for w in range(count):
        lefts = refs[2 * w : 2 * w + 2]
        rights = refs[2 * count + w * rights_per : 2 * count + (w + 1) * rights_per]
        tokens = lefts[0].shape[1]

        @pl.when(pl.program_id(0) == w)
        def _():
            def right(i):
                ref, start = (rights[0], i * tokens) if rights_per == 1 else (rights[i], 0)
                return jnp.concatenate(
                    [
                        ref[start : start + tokens, pl.ds(pl.multiple_of(at_ref[4 + d], columns), columns)]
                        for d in group
                    ],
                    axis=1,
                )

            values = [right(0), right(1)]
            for k in range(4):
                left = pl.ds(pl.multiple_of(at_ref[k], rows), rows)
                part = mm(lefts[0][left, :], values[0]) + mm(lefts[1][left, :], values[1])
                part = part.astype(bf16)
                away, place = (k // 2, k % 2) if flip == 0 else (k % 2, k // 2)
                target = give_ref if away else keep_ref
                for i in range(len(group)):
                    target[0, i, place] = part[:, i * columns : (i + 1) * columns]


def weight_parts(at, lefts, rights, group, own_rows, columns, flip):
    count = len(lefts)
    tokens = 2 * lefts[0][0].shape[1]
    lefts = [piece for left in lefts for piece in left]
    rights = [piece for right in rights for piece in right]
    shape = (count, len(group), 2, 2 * own_rows, columns)
    whole = lambda v: pl.BlockSpec(v.shape, lambda w, at: (0, 0), pipeline_mode=pl.Buffered(1))
    return pl.pallas_call(
        lambda *refs: weight_parts_body(count, group, flip, *refs),
        grid_spec=pltpu.PrefetchScalarGridSpec(
            num_scalar_prefetch=1,
            grid=(count,),
            in_specs=[whole(v) for v in lefts] + [whole(v) for v in rights],
            out_specs=[pl.BlockSpec((1,) + shape[1:], lambda w, at: (w, 0, 0, 0, 0))] * 2,
        ),
        out_shape=[jax.ShapeDtypeStruct(shape, bf16)] * 2,
        cost_estimate=pl.CostEstimate(
            flops=2 * count * tokens * 8 * own_rows * columns * len(group),
            transcendentals=0,
            bytes_accessed=count * tokens * (8 * own_rows + columns * len(group)) * 2,
        ),
        name="weight_parts",
    )(at, *lefts, *rights)


def swap(value):
    size = lax.axis_size("dp")
    return lax.ppermute(value, "dp", [(i, i ^ 1) for i in range(size)])


def across(value, bit):
    size = lax.axis_size("dp")
    return lax.ppermute(value, "dp", [(i, i ^ (1 << bit)) for i in range(size)])


def around(value, by):
    size = lax.axis_size("tensor")
    by = by % size
    return lax.ppermute(value, "tensor", [(i, (i + by) % size) for i in range(size)])


def along_sequence(value, pieces, forward):
    size = lax.axis_size("tensor")
    pairs = [(i, i + 1) for i in range(size - 1) if (i + 1) % pieces]
    if not forward:
        pairs = [(b, a) for a, b in pairs]
    return lax.ppermute(value, "tensor", pairs)


class Place:
    def __init__(self):
        dp = lax.axis_index("dp")
        self.core = dp % 2
        self.slots = lax.axis_size("tensor")
        self.slot = lax.axis_index("tensor")
        self.bits = [b for b in range(1, lax.axis_size("dp").bit_length() - 1)]
        self.side = {b: (dp >> b) % 2 for b in range(lax.axis_size("dp").bit_length() - 1)}

    def gather_slots(self, block):
        blocks = [block] + [around(block, d) for d in range(1, self.slots)]
        shape = (block.shape[0], self.slots, block.shape[1])
        index = lax.broadcasted_iota(jnp.int32, shape, 1)
        out = jnp.broadcast_to(block[:, None, :], shape)
        for d in range(1, self.slots):
            from_slot = (self.slot - d) % self.slots
            out = jnp.where(index == from_slot, blocks[d][:, None, :], out)
        return out

    def scatter_slots(self, blocks):
        def block(at):
            return lax.dynamic_index_in_dim(blocks, at % self.slots, 1, keepdims=False)

        total = block(self.slot).astype(f32)
        for d in range(1, self.slots):
            total = total + around(block(self.slot + d), d).astype(f32)
        return total

    def ordered(self, bit, mine, other, axis):
        mine, other = jnp.expand_dims(mine, axis), jnp.expand_dims(other, axis)
        low = self.side[bit] == 0
        return jnp.where(
            low,
            jnp.concatenate([mine, other], axis=axis),
            jnp.concatenate([other, mine], axis=axis),
        )

    def gather_rows(self, block, upward):
        done = block
        for bit in self.bits if upward else self.bits[::-1]:
            axis = 0 if upward else len(done.shape) - 2
            done = self.ordered(bit, done, across(done, bit), axis)
        return done.reshape((-1, block.shape[1]))

    def scatter_rows(self, whole, upward, low_bit=1):
        bits = [b for b in self.bits if b >= low_bit]
        if low_bit == 0:
            bits = [0] + bits
        count = len(bits)
        rows = whole.shape[0] >> count
        left = sorted(bits, reverse=True)
        now = whole.reshape((2,) * count + (rows, whole.shape[1]))
        for bit in bits if upward else bits[::-1]:
            axis = left.index(bit)
            left.remove(bit)
            side = self.side[bit]
            keep = lax.dynamic_index_in_dim(now, side, axis, keepdims=False)
            give = lax.dynamic_index_in_dim(now, 1 - side, axis, keepdims=False)
            now = (keep.astype(f32) + across(give, bit).astype(f32)).astype(whole.dtype)
        return now

    def half_rows(self, whole, bit):
        keep = lax.dynamic_index_in_dim(whole, self.side[bit], whole.ndim - 3, keepdims=False)
        give = lax.dynamic_index_in_dim(whole, 1 - self.side[bit], whole.ndim - 3, keepdims=False)
        return (keep.astype(f32) + across(give, bit).astype(f32)).astype(whole.dtype)

    def ordered_sum(self, part):
        return self.half_rows(part.reshape((2, 2, 2, -1, part.shape[1])), 0)

    def gather_weight(self, mine, other):
        both = self.ordered(0, mine, other, 0).reshape((-1, mine.shape[1]))
        blocks = self.gather_slots(both)
        half = self.slots // 2
        first = blocks[:, :half].reshape((both.shape[0], -1))
        second = blocks[:, half:].reshape((both.shape[0], -1))
        return jnp.concatenate(
            [self.gather_rows(first, True), self.gather_rows(second, False)], axis=1
        )

    def scatter_weight(self, part):
        columns = part.shape[1] // 2
        half = self.slots // 2
        first = self.scatter_rows(part[:, :columns], False)
        second = self.scatter_rows(part[:, columns:], True)
        rows = first.shape[0]
        blocks = jnp.concatenate(
            [first.reshape((rows, half, -1)), second.reshape((rows, half, -1))], axis=1
        )
        mine = self.scatter_slots(blocks).reshape((2, rows // 2, -1))
        keep = lax.dynamic_index_in_dim(mine, self.core, 0, keepdims=False)
        give = lax.dynamic_index_in_dim(mine, 1 - self.core, 0, keepdims=False)
        out = self.ordered(0, keep, swap(give), 1)
        return out.reshape((rows // 2, -1))

    def fast(self, half_channels):
        return len(self.bits) == 2 and self.slots == 4 and half_channels % 128 == 0

    def offsets(self, own_rows, half_channels):
        chip = lax.axis_index("dp") // 2
        rows = [(chip ^ k) * 2 * own_rows for k in range(4)]
        columns = [(self.slot - d) % self.slots * half_channels for d in range(self.slots)]
        return jnp.stack(rows + columns).astype(jnp.int32)

    def unit(self, d, block):
        first, second = self.bits if d % 2 == 0 else self.bits[::-1]
        return across(block, first), across(block, second)

    def forward(self, d, one):
        return across(one, self.bits[1] if d % 2 == 0 else self.bits[0])

    def items(self, d, here, one, two, both):
        order = (here, one, two, both) if d % 2 == 0 else (here, two, one, both)
        return [(block, d, k) for k, block in enumerate(order)]

    def first_exchange(self, at, give):
        return across(give, self.bits[1 - at])

    def second_term(self, keep, came):
        return (keep[:, :, 1].astype(f32) + came[:, :, 1].astype(f32)).astype(bf16)

    def second_exchange(self, at, term):
        return across(term, self.bits[at])

    def slot_parts(self, keeps, cames, lasts, groups):
        own = {}
        for group, keep, came, last in zip(groups, keeps, cames, lasts):
            total = keep[:, :, 0].astype(f32) + came[:, :, 0].astype(f32) + last.astype(f32)
            for i, d in enumerate(group):
                own[d] = total[:, i]
        return own

    def slot_sum(self, keeps, cames, lasts, groups):
        own = self.slot_parts(keeps, cames, lasts, groups)
        return own[0], [around(own[d].astype(bf16), -d) for d in range(1, self.slots)]

    def to_owner(self, own, others):
        total = own
        for other in others:
            total = total + other.astype(f32)
        weights, rows, columns = total.shape
        total = total.reshape((weights, 2, rows // 2, columns))
        keep = lax.dynamic_index_in_dim(total, self.core, 1, keepdims=False)
        give = lax.dynamic_index_in_dim(total, 1 - self.core, 1, keepdims=False)
        out = self.ordered(0, keep, swap(give), 2)
        return out.reshape((weights, rows // 2, 2 * columns))

    def sum_chips(self, value):
        for bit in self.bits:
            value = value + across(value, bit)
        return value

    def sum_slots(self, value):
        total = value.astype(f32)
        for d in range(1, self.slots):
            total = total + around(value, d).astype(f32)
        return total


def on_device_general(
    x_in,
    segment_ids,
    norm_gain,
    w_x,
    w_z,
    w_bc,
    w_dt,
    conv_x,
    conv_x_bias,
    conv_bc,
    conv_bc_bias,
    dt_bias,
    a_log,
    d_skip,
    gate_gain,
    w_out,
    cotangent,
):
    place = Place()
    core, slots, slot = place.core, place.slots, place.slot
    length, features = x_in.shape
    sequences, whole_length = segment_ids.shape
    pieces = whole_length // length
    own_rows = w_x.shape[0]
    slot_channels = w_x.shape[1]
    slot_heads = w_dt.shape[1]
    half_channels = slot_channels // 2
    half_heads = slot_heads // 2
    channels = half_channels * slots
    heads = half_heads * slots
    all_channels = 2 * channels
    all_heads = 2 * heads
    bc_width = w_bc.shape[1]
    n_chunks = length // CH

    def split(weight):
        return weight.reshape((own_rows, 2, half_channels))

    stacked = jnp.stack([split(w_x), split(w_z), split(w_out.T)])
    mine = lax.dynamic_index_in_dim(stacked, core, 2, keepdims=False)
    other = swap(lax.dynamic_index_in_dim(stacked, 1 - core, 2, keepdims=False))
    wx = place.gather_weight(mine[0], other[0])
    dt_slots = place.gather_slots(w_dt).reshape((own_rows, all_heads))
    thin = jnp.concatenate([w_bc, dt_slots, norm_gain[:, None]], axis=1)
    thin = jnp.pad(thin, ((0, 0), (0, bc_width + 128 - thin.shape[1])))
    thin = place.ordered(0, thin, swap(thin), 0).reshape((2 * own_rows, -1))
    thin = place.gather_rows(thin, True)
    wz = place.gather_weight(mine[1], other[1])
    wo = place.gather_weight(mine[2], other[2])

    rows = jnp.concatenate(
        [
            conv_x,
            conv_x_bias[None],
            gate_gain[None],
            jnp.pad(jnp.concatenate([dt_bias, a_log, d_skip])[None], ((0, 0), (0, slot_channels - 3 * slot_heads))),
            jnp.zeros((1, slot_channels), f32),
        ],
        axis=0,
    )
    rows = place.gather_slots(rows)
    own = lax.dynamic_index_in_dim(
        rows.reshape((8, slots, 2, half_channels)), core, 2, keepdims=False
    ).reshape((8, channels))
    gain_row = own[5:6]
    lane = jnp.arange(128)
    head_at = lane % 32
    global_head = (head_at // half_heads) * slot_heads + core * half_heads + head_at % half_heads
    pick = ((lane[:, None] == global_head[None, :]) & (head_at < heads)[None, :]).astype(f32)
    small = rows[6, :, : 3 * slot_heads].reshape((slots, 3, slot_heads)).transpose(1, 0, 2)
    small = jnp.pad(small.reshape((3, all_heads)), ((0, 5), (0, 128 - all_heads)))
    small = exact(small, pick)
    bias_lanes = small[0]
    rate_lanes = jnp.where(head_at < heads, -jnp.exp(small[1]), 0.0)
    to_heads = head_map(channels, f32)
    skip_row = exact(small[2:3] * (lane < 32), to_heads.T)
    cw = jnp.concatenate([own[:5], skip_row, jnp.zeros((2, channels), f32)], axis=0)

    padded = jnp.pad(segment_ids, ((0, 0), (HALO, HALO)), constant_values=-1)
    ids_own = lax.dynamic_slice(
        padded, (slot // pieces, (slot % pieces) * length), (1, length + 2 * HALO)
    )
    ids_all = jnp.concatenate([ids_own, swap(ids_own)], axis=0)
    ids = ids_all[:, HALO : HALO + length]
    before = ids_all[:, HALO - 1]

    def near(k):
        return ids_all[:, HALO + k : HALO + k + length] == ids

    flags = [near(-1), near(-2), near(-3), ids, near(1), near(2), near(3), jnp.zeros_like(ids)]
    flags = jnp.stack([v.astype(f32) for v in flags], axis=-1)

    x_rows = jnp.concatenate([along_sequence(x_in[-HALO:], pieces, True), x_in], axis=0)
    tokens_ext = x_rows.astype(f32)
    inv_ext = lax.rsqrt(jnp.mean(tokens_ext * tokens_ext, axis=-1, keepdims=True) + epsilon)
    gain = thin[:, bc_width + all_heads].astype(f32)[None, :]
    normed_own = (tokens_ext * inv_ext * gain).astype(bf16)
    normed_other = swap(normed_own)
    normed_ext = jnp.concatenate([normed_own, normed_other], axis=0)
    normed = jnp.concatenate([normed_own[HALO:], normed_other[HALO:]], axis=0)
    tokens, inv_rms = tokens_ext[HALO:], inv_ext[HALO:]
    cot = jnp.concatenate([cotangent, swap(cotangent)], axis=0)

    dt_pick = jnp.dot(thin[:, bc_width:], pick.astype(bf16), preferred_element_type=f32).astype(bf16)
    thin_proj = mm(normed_ext, jnp.concatenate([thin[:, :bc_width], dt_pick], axis=1))
    thin_proj = thin_proj.reshape((2, HALO + length, -1))
    bc_ext = thin_proj[:, :, :bc_width]
    dt_in = thin_proj[:, HALO:, bc_width:] + bias_lanes
    x_ext = mm(normed_ext, wx).reshape((2, HALO + length, channels))

    bc_pre = conv_bc_bias + conv_bc[0] * bc_ext[:, HALO:]
    for k in range(1, conv_bc.shape[0]):
        shifted = bc_ext[:, HALO - k : HALO - k + length]
        bc_pre = bc_pre + conv_bc[k] * shifted * flags[:, :, k - 1 : k]
    bc_act = jax.nn.silu(bc_pre)
    bc_turned = bc_act.astype(bf16).transpose(0, 2, 1)
    c_low = bc_act[:, :, bc_width // 2 :].astype(bf16)

    step = jax.nn.softplus(dt_in)
    log_step = (step * rate_lanes).reshape((2 * n_chunks, CH, 128))
    tri = (jnp.arange(CH)[:, None] >= jnp.arange(CH)[None, :]).astype(f32)
    running = jnp.einsum("ts,csh->cth", tri, log_step, precision=highest)
    running = running.reshape((2, n_chunks, CH, 128))
    last = running[:, :, -1:, :]
    ids_chunks = ids.reshape((2, n_chunks, CH, 1))
    chunk_end = ids_chunks[:, :, -1:, :]
    chunk_before = jnp.concatenate(
        [before[:, None, None, None], chunk_end[:, :-1]], axis=1
    )
    still = (chunk_end == chunk_before).astype(f32)
    alpha = still * jnp.exp(last)
    lead = jnp.cumsum(last, axis=1) - last
    since_piece = (ids_chunks == before[:, None, None, None]).astype(f32) * jnp.exp(running + lead)
    since_piece = since_piece.reshape((2 * length, 128))
    group_lane = lane // 32
    hv = jnp.where(
        group_lane == 0,
        running * LOG2E,
        jnp.where(
            group_lane == 1,
            step.reshape((2, n_chunks, CH, 128)),
            jnp.where(
                group_lane == 2,
                (ids_chunks == chunk_before).astype(f32) * jnp.exp(running),
                (ids_chunks == chunk_end).astype(f32) * jnp.exp(last - running),
            ),
        ),
    ).reshape((2, length, 128))
    rv = jnp.concatenate(
        [
            hv[:, :, :24].transpose(0, 2, 1),
            ids.astype(f32)[:, None, :],
            jnp.zeros((2, 7, length), f32),
        ],
        axis=1,
    )
    first_lanes = (lane < 32).astype(f32)
    al = exact((alpha * first_lanes).reshape((2 * n_chunks, 128)), to_heads.T)
    al = al.reshape((2, n_chunks, channels))
    whole_alpha = jnp.prod(al, axis=1, keepdims=True)
    al = jnp.pad(al, ((0, 0), (0, 8 - n_chunks), (0, 0)))
    wide_since = mm((since_piece * first_lanes).astype(bf16), to_heads.T.astype(bf16))
    wide_since = wide_since.reshape((2, length, channels))

    def hand_on(local, forward):
        low = local.astype(bf16)
        for _ in range(pieces - 2):
            came = along_sequence(low, pieces, forward)
            low = (local + whole_alpha * came.astype(f32)).astype(bf16)
        return along_sequence(low, pieces, forward)

    y_here, states = scan_fwd(hv, flags, rv, al, bc_act, bc_turned, x_ext, cw, CH)
    state_in = hand_on(states[:, -1], True)
    y = y_here + wide_since * lax.dot_general(
        c_low, state_in, (((2,), (1,)), ((0,), (0,))), preferred_element_type=f32
    )

    gate_in = mm(normed, wz)
    mixed_grad = mm(cot, wo)
    y = y.reshape((2 * length, channels))
    sig = jax.nn.sigmoid(gate_in)
    act = gate_in * sig
    gated = y * act
    scaled = mixed_grad * gain_row
    sums = jnp.stack([jnp.sum(gated * gated, axis=1), jnp.sum(scaled * gated, axis=1)])
    sums = sums.reshape((2, 2, length))
    sums = (sums + swap(sums)[:, ::-1]).reshape((2, 2 * length))
    gate_rms = lax.rsqrt(sums[0] / all_channels + epsilon)[:, None]
    mixed = (gated * gate_rms * gain_row).astype(bf16)
    gate_gain_part = jnp.sum(mixed_grad * gated * gate_rms, axis=0)
    gated_grad = gate_rms * scaled - gated * gate_rms**3 * (sums[1] / all_channels)[:, None]
    y_grad = (gated_grad * act).reshape((2, length, channels))
    gate_grad = (gated_grad * y * sig * (1.0 + gate_in * (1.0 - sig))).astype(bf16)

    state_grad = lax.dot_general(
        c_low, (y_grad * wide_since).astype(bf16), (((1,), (1,)), ((0,), (0,))), preferred_element_type=f32
    )
    state_grad = hand_on(state_grad, False)
    wo_part = tmm(cot, mixed).astype(bf16)
    w_out_grad = place.scatter_weight(wo_part).T
    branch = mmt(mixed, wo)
    block_out = (tokens + branch[:length] + swap(branch[length:].astype(bf16)).astype(f32)).astype(bf16)
    wz_part = tmm(normed, gate_grad).astype(bf16)
    w_z_grad = place.scatter_weight(wz_part)

    x_low, tail, head, dbc, dcol, drow, dcw = scan_bwd(
        hv, flags, rv, al, bc_act, bc_turned, x_ext, cw, y_grad, states, state_in, state_grad, CH
    )

    head = along_sequence(head, pieces, False)

    def past_end(begin, taps):
        total = jnp.zeros((begin.shape[0], HALO, begin.shape[2]), f32)
        for k in range(1, taps.shape[0]):
            moved = jnp.pad(begin[:, :k], ((0, 0), (HALO - k, 0), (0, 0)))
            total = total + taps[k] * moved * flags[: begin.shape[0], length - HALO :, 3 + k : 4 + k]
        return total

    fixed = (tail + past_end(head, own[:4])).astype(bf16)
    x_low = lax.dynamic_update_slice(x_low, fixed, (0, length - HALO, 0)).reshape((2 * length, channels))

    bc_grad = dbc[0] + swap(dbc[1])
    pre = bc_pre[0]
    sig_bc = jax.nn.sigmoid(pre)
    bc_dpre = bc_grad * (sig_bc * (1.0 + pre * (1.0 - sig_bc)))
    bc_head = along_sequence(bc_dpre[:8], pieces, False)
    bc_raw = conv_bc[0] * bc_dpre
    bc_taps = [jnp.sum(bc_dpre * bc_ext[0, HALO:], axis=0)]
    longer = jnp.concatenate([bc_dpre, bc_head], axis=0)
    for k in range(1, conv_bc.shape[0]):
        bc_raw = bc_raw + conv_bc[k] * longer[k : k + length] * flags[0, :, 3 + k : 4 + k]
        shifted = bc_ext[0, HALO - k : HALO - k + length]
        bc_taps.append(jnp.sum(bc_dpre * shifted * flags[0, :, k - 1 : k], axis=0))
    bc_low = bc_raw.astype(bf16)
    bc_small = jnp.stack(bc_taps + [jnp.sum(bc_dpre, axis=0)] + [jnp.zeros((bc_width,), f32)] * 3)
    bc_small = place.sum_chips(bc_small + swap(bc_small))
    bc_small = place.sum_slots(bc_small)

    dcum = dcol[:, :, :128] - jnp.pad(drow.transpose(0, 2, 1), ((0, 0), (0, 0), (0, 96)))
    dlog = jnp.einsum("ts,csh->cth", tri.T, dcum.reshape((2 * n_chunks, CH, 128)), precision=highest)
    dstep = dcol[:, :, 128:] + dlog.reshape((2, length, 128)) * rate_lanes
    dt_raw = (dstep * jax.nn.sigmoid(dt_in)).reshape((2 * length, 128))
    rate_part = jnp.sum(dlog * log_step, axis=(0, 1))
    place_back = (pick * first_lanes).T.astype(bf16)
    dt_low = mm(dt_raw.astype(bf16), place_back).astype(bf16)

    dcw = jnp.sum(dcw, axis=0)
    head_rows = jnp.stack([jnp.sum(dt_raw, axis=0), rate_part]) * first_lanes
    head_rows = exact(head_rows, to_heads.T)
    packed = jnp.concatenate(
        [dcw[:5], gate_gain_part[None], dcw[5:6], head_rows, jnp.zeros((7, channels), f32)], axis=0
    )
    packed = place.sum_chips(packed).reshape((16, slots, half_channels))
    packed = place.scatter_slots(packed)
    packed = place.ordered(0, packed, swap(packed), 1).reshape((16, slot_channels))
    by_head = packed[6:9].reshape((3, slot_heads, 64))

    wx_part = tmm(normed, x_low).astype(bf16)
    w_x_grad = place.scatter_weight(wx_part)
    thin_low = jnp.concatenate(
        [jnp.concatenate([bc_low, jnp.zeros_like(bc_low)], axis=0), dt_low], axis=1
    )
    thin_part = tmm(normed, thin_low).astype(bf16)
    thin_grad = place.scatter_rows(thin_part, True, low_bit=0)
    thin_grad = place.sum_slots(thin_grad)
    w_bc_grad = thin_grad[:, :bc_width]
    w_dt_grad = lax.dynamic_slice_in_dim(thin_grad, bc_width + slot * slot_heads, slot_heads, 1)

    normed_grad = mmt(x_low, wx) + mmt(gate_grad, wz) + mmt(thin_low, thin)
    normed_grad = normed_grad[:length] + swap(normed_grad[length:].astype(bf16)).astype(f32)
    gain_part = jnp.sum(normed_grad * tokens * inv_rms, axis=0)
    pushed = normed_grad * gain
    x_grad = (
        cotangent.astype(f32)
        + inv_rms * pushed
        - tokens * inv_rms**3 * jnp.mean(pushed * tokens, axis=-1, keepdims=True)
    )
    gain_rows = gain_part.reshape((features // own_rows * 2, own_rows // 2))
    gain_rows = place.scatter_rows(gain_rows, True, low_bit=0)
    norm_gain_grad = place.sum_slots(gain_rows).reshape((own_rows,))
    return (
        block_out,
        x_grad,
        norm_gain_grad,
        w_x_grad,
        w_z_grad,
        w_bc_grad,
        w_dt_grad,
        packed[:4],
        packed[4],
        bc_small[:4],
        bc_small[4],
        by_head[1, :, 0],
        by_head[2, :, 0],
        jnp.sum(by_head[0], axis=1),
        packed[5],
        w_out_grad,
    )


def tie(*values):
    return lax.optimization_barrier(values)


def on_device(*args):
    if Place().fast(args[3].shape[1] // 2):
        return on_device_fast(*args)
    return on_device_general(*args)


def on_device_fast(
    x_in,
    segment_ids,
    norm_gain,
    w_x,
    w_z,
    w_bc,
    w_dt,
    conv_x,
    conv_x_bias,
    conv_bc,
    conv_bc_bias,
    dt_bias,
    a_log,
    d_skip,
    gate_gain,
    w_out,
    cotangent,
):
    place = Place()
    core, slots, slot = place.core, place.slots, place.slot
    length, features = x_in.shape
    sequences, whole_length = segment_ids.shape
    pieces = whole_length // length
    own_rows = w_x.shape[0]
    slot_channels = w_x.shape[1]
    slot_heads = w_dt.shape[1]
    half_channels = slot_channels // 2
    half_heads = slot_heads // 2
    channels = half_channels * slots
    heads = half_heads * slots
    all_channels = 2 * channels
    all_heads = 2 * heads
    bc_width = w_bc.shape[1]
    n_chunks = length // CH
    groups = [tuple(range(0, slots, 2)), tuple(range(1, slots, 2))]
    at = place.offsets(own_rows, half_channels)

    def split(weight):
        return weight.reshape((own_rows, 2, half_channels))

    stacked = jnp.stack([split(w_x), split(w_z), split(w_out.T)])
    mine = lax.dynamic_index_in_dim(stacked, core, 2, keepdims=False)
    other = swap(lax.dynamic_index_in_dim(stacked, 1 - core, 2, keepdims=False))
    both = place.ordered(0, mine, other, 1).reshape((3, 2 * own_rows, half_channels))
    padded = jnp.pad(segment_ids, ((0, 0), (HALO, HALO)), constant_values=-1)
    ids_own = lax.dynamic_slice(
        padded, (slot // pieces, (slot % pieces) * length), (1, length + 2 * HALO)
    )
    ids_all = jnp.concatenate([ids_own, swap(ids_own)], axis=0).astype(f32)
    both, ids_all, conv_x, conv_x_bias, gate_gain, dt_bias, a_log, d_skip, w_dt, w_bc, norm_gain, x_in, cotangent = tie(
        both, ids_all, conv_x, conv_x_bias, gate_gain, dt_bias, a_log, d_skip, w_dt, w_bc, norm_gain, x_in, cotangent)

    rows = jnp.concatenate(
        [
            conv_x,
            conv_x_bias[None],
            gate_gain[None],
            jnp.pad(
                jnp.concatenate([dt_bias, a_log, d_skip])[None], ((0, 0), (0, slot_channels - 3 * slot_heads))
            ),
            jnp.zeros((1, slot_channels), f32),
            jnp.pad(w_dt.T.astype(f32), ((0, 0), (0, slot_channels - own_rows))),
        ],
        axis=0,
    )
    rows = place.gather_slots(rows)
    halo = along_sequence(x_in[-HALO:], pieces, True)
    wx_here = [both[:1]] + [around(both[:1], d) for d in range(1, slots)]
    wx_one, wx_two = {}, {}
    wx_one[0], wx_two[0] = place.unit(0, wx_here[0])
    cot_turned_own = turn(cotangent)
    rows, halo, wx_here[slots - 1], wx_one, wx_two, cot_turned_own, w_bc, norm_gain = tie(
        rows, halo, wx_here[slots - 1], wx_one, wx_two, cot_turned_own, w_bc, norm_gain)
    dt_slots = rows[8:, :, :own_rows].transpose(2, 1, 0).reshape((own_rows, all_heads)).astype(bf16)
    thin = jnp.concatenate([w_bc, dt_slots, norm_gain[:, None]], axis=1)
    thin = jnp.pad(thin, ((0, 0), (0, bc_width + 128 - thin.shape[1])))
    thin = place.ordered(0, thin, swap(thin), 0)
    low, high = place.bits
    thin = place.ordered(low, thin, across(thin, low), 0)
    odd = slots - 1
    wx_one[odd] = across(wx_here[odd], high)
    thin, wx_here[odd], wx_here[1], wx_one, cot_turned_own, cotangent = tie(
        thin, wx_here[odd], wx_here[1], wx_one, cot_turned_own, cotangent)
    thin = place.ordered(high, thin, across(thin, high), 0).reshape((features, -1))
    wx_two[odd] = across(wx_here[odd], low)
    gain = thin[:, bc_width + all_heads].astype(f32)[None, :]
    thin, gain, wx_here, wx_two, both, cot_turned_own, cotangent = tie(
        thin, gain, wx_here, wx_two, both, cot_turned_own, cotangent)
    pair_here = {0: both[1:], 1: around(both[1:], 1)}
    normed_own, normed_turned_own = norm(x_in, halo, gain)
    normed_both = [normed_own, swap(normed_own)]
    for d in range(1, slots - 1):
        wx_one[d], wx_two[d] = place.unit(d, wx_here[d])

    thin, gain, normed_both, normed_turned_own, pair_here, rows, ids_all, wx_here, wx_one, wx_two = tie(
        thin, gain, normed_both, normed_turned_own, pair_here, rows, ids_all, wx_here, wx_one, wx_two)
    normed_turned = [normed_turned_own, swap(normed_turned_own)]
    cot = [cotangent, swap(cotangent)]
    cot_turned = [cot_turned_own, swap(cot_turned_own)]

    pair_here[2] = around(pair_here[0], 2)
    one, two, both_k = {}, {}, {}
    one[0], two[0] = place.unit(0, pair_here[0])
    own = lax.dynamic_index_in_dim(
        rows[:8].reshape((8, slots, 2, half_channels)), core, 2, keepdims=False
    ).reshape((8, channels))
    gain_row = own[5:6]
    lane = jnp.arange(128)
    head_at = lane % 32
    global_head = (head_at // half_heads) * slot_heads + core * half_heads + head_at % half_heads
    pick = ((lane[:, None] == global_head[None, :]) & (head_at < heads)[None, :]).astype(f32)
    first_lanes = (lane < 32).astype(f32)
    small = rows[6, :, : 3 * slot_heads].reshape((slots, 3, slot_heads)).transpose(1, 0, 2)
    small = jnp.pad(small.reshape((3, all_heads)), ((0, 5), (0, 128 - all_heads)))
    small = exact(small, pick)
    bias_lanes = small[0]
    rate_lanes = jnp.where(head_at < heads, -jnp.exp(small[1]), 0.0)
    to_heads = head_map(channels, f32)
    skip_row = exact(small[2:3] * first_lanes, to_heads.T)
    cw = jnp.concatenate([own[:5], skip_row, jnp.zeros((2, channels), f32)], axis=0)
    lanes = jnp.concatenate([bias_lanes[None], rate_lanes[None], jnp.zeros((6, 128), f32)], axis=0)
    cbc = jnp.concatenate([conv_bc, conv_bc_bias[None], jnp.zeros((3, bc_width), f32)], axis=0)
    wide_ids = jnp.pad(ids_all, ((0, 0), (0, -ids_all.shape[1] % 128)))
    wide_ids = jnp.broadcast_to(wide_ids[:, None, :], (2, 8, wide_ids.shape[1]))
    ids_rows = jnp.broadcast_to(ids_all[:, None, HALO : HALO + length], (2, 8, length))
    tri = (jnp.arange(CH)[:, None] >= jnp.arange(CH)[None, :]).astype(f32)

    bc_ext, bc_pre, bc_act, bc_turned, c_low, dt_in, log_step, hv, rv, al, wide_since, flags = prepare(
        normed_both[0], normed_both[1], thin, pick.astype(bf16), lanes, cbc, wide_ids, ids_rows, channels)
    whole_alpha = jnp.prod(al[:, :n_chunks], axis=1, keepdims=True)
    log_step = log_step.reshape((2 * n_chunks, CH, 128))
    wx_both = {d: place.forward(d, wx_one[d]) for d in range(slots)}

    def hand_on(local, forward):
        low = local.astype(bf16)
        for _ in range(pieces - 2):
            came = along_sequence(low, pieces, forward)
            low = (local + whole_alpha * came.astype(f32)).astype(bf16)
        return along_sequence(low, pieces, forward)

    (one, two, pair_here, wx_here, wx_one, wx_two, wx_both, normed_both, hv, rv, al, bc_act, bc_turned, cw, wide_since, c_low, flags, bc_ext, bc_pre,
     dt_in, log_step) = tie(
        one, two, pair_here, wx_here, wx_one, wx_two, wx_both, normed_both, hv, rv, al, bc_act, bc_turned, cw, wide_since, c_low, flags,
        bc_ext, bc_pre, dt_in, log_step)
    wx_items = []
    for d in range(slots):
        wx_items += place.items(d, wx_here[d], wx_one[d], wx_two[d], wx_both[d])

    pair_here[3] = around(pair_here[0], 3)
    both_k[0] = place.forward(0, one[0])
    one[1], two[1] = place.unit(1, pair_here[1])
    one[2] = across(pair_here[2], place.bits[0])
    x_ext, wx = project(normed_both, 0, at, wx_items, 0, channels)
    x_ext = x_ext.reshape((2, HALO + length, channels))

    x_ext, one, two, both_k, pair_here = tie(x_ext, one, two, both_k, pair_here)
    one[3], two[3] = place.unit(3, pair_here[3])
    two[2] = across(pair_here[2], place.bits[1])
    both_k[1] = place.forward(1, one[1])
    y_here, states = scan_fwd(hv, flags, rv, al, bc_act, bc_turned, x_ext, cw, CH)

    y_here, states, one, two, both_k = tie(y_here, states, one, two, both_k)
    state_in = hand_on(states[:, -1], True)
    both_k[2], both_k[3] = place.forward(2, one[2]), place.forward(3, one[3])
    pair_items = []
    for d in range(slots):
        pair_items += place.items(d, pair_here[d], one[d], two[d], both_k[d])
    tokens = x_in.astype(f32)

    gate_in, wz = project(normed_both, HALO, at, pair_items, 0, channels)
    mixed_grad, wo = project(cot, 0, at, pair_items, 1, channels)
    flat = lambda v: v.reshape((2 * length, -1))
    y, sums = gate_sums(flat(y_here), flat(wide_since), flat(c_low), state_in, gate_in, mixed_grad, gain_row)
    mixed, gate_grad, y_grad, gain_grad, state_grad = gate_grads(
        y, flat(wide_since), flat(c_low), gate_in, mixed_grad, gain_row, sums, swap(sums), all_channels)
    y_grad = y_grad.reshape((2, length, channels))
    state_grad = hand_on(state_grad, False)
    parts = [
        weight_parts(at, [normed_turned, cot_turned], [[gate_grad], [mixed]], group, own_rows, half_channels, flip)
        for flip, group in enumerate(groups)
    ]
    parts, y_grad, mixed, gate_grad, state_grad = tie(parts, y_grad, mixed, gate_grad, state_grad)
    pair_came = [place.first_exchange(i, parts[i][1]) for i in range(2)]

    branch_other = swap(mmt(mixed[length:], wo).astype(bf16))
    branch = mmt(mixed[:length], wo)
    block_out = (tokens + branch + branch_other.astype(f32)).astype(bf16)

    def backward(piece):
        return scan_bwd(
            hv, flags, rv, al, bc_act, bc_turned, x_ext, cw, y_grad, states, state_in, state_grad, CH, piece, 1
        )

    back_other = backward(1)
    pair_came, back_other, y_grad, block_out = tie(pair_came, back_other, y_grad, block_out)
    terms = [place.second_term(parts[i][0], pair_came[i]) for i in range(2)]
    pair_last = [place.second_exchange(i, terms[i]) for i in range(2)]
    back_own = backward(0)
    dbc_other = swap(back_other[3][0])
    head_other = along_sequence(back_other[2], pieces, False)
    pair_last, back_own, dbc_other, head_other = tie(pair_last, back_own, dbc_other, head_other)

    head = jnp.concatenate([along_sequence(back_own[2], pieces, False), head_other])
    pair_sums = place.slot_parts([p[0] for p in parts], pair_came, pair_last, groups)
    pair_others = {1: around(pair_sums[1].astype(bf16), -1)}
    place_back = (pick * first_lanes).T.astype(bf16)
    bc_dpre, dt_low, bc_small, packed = small_grads(
        back_own[3], dbc_other, bc_pre, bc_ext, flags, back_own[4], back_other[4], back_own[5], back_other[5],
        log_step.reshape((2, length, 128)), dt_in, lanes, place_back, back_own[6], back_other[6], gain_grad)

    def past_end(begin, taps):
        total = jnp.zeros((begin.shape[0], HALO, begin.shape[2]), f32)
        for k in range(1, taps.shape[0]):
            moved = jnp.pad(begin[:, :k], ((0, 0), (HALO - k, 0), (0, 0)))
            total = total + taps[k] * moved * flags[: begin.shape[0], length - HALO :, 3 + k : 4 + k]
        return total

    fix = past_end(head, own[:4])
    x_low = [
        lax.dynamic_update_slice(back[0][0], (back[1][0] + fix[i]).astype(bf16), (length - HALO, 0))
        for i, back in enumerate((back_own, back_other))
    ]
    x_low, bc_dpre, dt_low, bc_small, packed = tie(x_low, bc_dpre, dt_low, bc_small, packed)
    bc_head = along_sequence(bc_dpre[:8], pieces, False)
    x_parts = [
        weight_parts(at, [normed_turned], [x_low], group, own_rows, half_channels, flip)
        for flip, group in enumerate(groups)
    ]
    x_parts, x_low, pair_others, pair_sums, bc_head, bc_dpre, dt_low = tie(
        x_parts, x_low, pair_others, pair_sums, bc_head, bc_dpre, dt_low)
    x_came = [place.first_exchange(i, x_parts[i][1]) for i in range(2)]
    for d in range(2, slots - 1):
        pair_others[d] = around(pair_sums[d].astype(bf16), -d)
    normed_grad, normed_grad_other, thin_part = normed_grads(
        bc_dpre, bc_head, flags, cbc, dt_low, normed_turned, x_low, gate_grad, wx, wz, thin)

    x_came, thin_part, pair_others, pair_sums, normed_grad, normed_grad_other, packed, bc_small = tie(
        x_came, thin_part, pair_others, pair_sums, normed_grad, normed_grad_other, packed, bc_small)
    x_terms = [place.second_term(x_parts[i][0], x_came[i]) for i in range(2)]
    x_last = [place.second_exchange(i, x_terms[i]) for i in range(2)]
    pair_others[slots - 1] = around(pair_sums[slots - 1].astype(bf16), 1)
    thin_part = place.ordered_sum(thin_part)
    x_grad, gain_part = x_grads(normed_grad, swap(normed_grad_other), x_in, cotangent, gain)
    gain_part = jnp.sum(gain_part, axis=0).reshape((-1, bc_width))
    gain_rows = gain_part.shape[0]
    bc_small = jnp.concatenate([bc_small[:5], gain_part, jnp.zeros((11 - gain_rows, bc_width), f32)], axis=0)
    bc_small = bc_small + swap(bc_small)
    packed = jnp.concatenate([packed, bc_small], axis=1)
    low, high = place.bits
    packed = packed + across(packed, low)
    thin_part = place.half_rows(thin_part, low)

    x_last, packed, thin_part, x_grad, pair_sums, pair_others = tie(
        x_last, packed, thin_part, x_grad, pair_sums, pair_others)
    x_sums = place.slot_parts([p[0] for p in x_parts], x_came, x_last, groups)
    x_others = [around(x_sums[1].astype(bf16), -1)]
    packed = packed + across(packed, high)
    thin_grad = place.half_rows(thin_part, high)
    packed, thin_grad, x_others, x_sums = tie(packed, thin_grad, x_others, x_sums)

    bc_small = packed[:, channels:]
    packed = packed[:, :channels].reshape((16, slots, half_channels))

    def block(index):
        return lax.dynamic_index_in_dim(packed, index % slots, 1, keepdims=False)

    own_sums = jnp.concatenate([block(slot), bc_small], axis=1)
    for d in range(1, slots):
        own_sums = own_sums + around(jnp.concatenate([block(slot + d), bc_small], axis=1), d)
    thin_grad = place.sum_slots(thin_grad)
    own_sums, thin_grad, x_sums, x_others = tie(own_sums, thin_grad, x_sums, x_others)
    x_others += [around(x_sums[d].astype(bf16), -d) for d in range(2, slots)]
    packed = own_sums[:, :half_channels]
    bc_small = own_sums[:, half_channels:]
    packed = place.ordered(0, packed, swap(packed), 1).reshape((16, slot_channels))
    by_head = packed[6:9].reshape((3, slot_heads, 64))
    norm_gain_grad = lax.dynamic_slice_in_dim(
        bc_small[5 : 5 + gain_rows].reshape((features,)), lax.axis_index("dp") * own_rows, own_rows, 0)
    w_z_grad, w_out_grad = place.to_owner(pair_sums[0], list(pair_others.values()))
    w_bc_grad = thin_grad[:, :bc_width]
    w_dt_grad = lax.dynamic_slice_in_dim(thin_grad, bc_width + slot * slot_heads, slot_heads, 1)
    w_x_grad = place.to_owner(x_sums[0], x_others)[0]
    return (
        block_out,
        x_grad,
        norm_gain_grad,
        w_x_grad,
        w_z_grad,
        w_bc_grad,
        w_dt_grad,
        packed[:4],
        packed[4],
        bc_small[:4],
        bc_small[4],
        by_head[1, :, 0],
        by_head[2, :, 0],
        jnp.sum(by_head[0], axis=1),
        packed[5],
        w_out_grad.T,
    )


def solution(mesh):
    rows = P(("dp", "tensor"), None)
    both = P("dp", "tensor")
    heads = P("tensor")
    in_specs = (
        rows, P("dp", None), P("dp"), both, both, P("dp", None), both, P(None, "tensor"), heads,
        P(), P(), heads, heads, heads, heads, P("tensor", "dp"), rows,
    )
    out_specs = (
        rows, rows, P("dp"), both, both, P("dp", None), both, P(None, "tensor"), heads,
        P(), P(), heads, heads, heads, heads, P("tensor", "dp"),
    )
    return jax.shard_map(
        on_device, mesh=mesh, in_specs=in_specs, out_specs=out_specs, check_vma=False
    )
```

```python
import jax
import jax.numpy as jnp
from jax import lax
from jax.experimental import pallas as pl
from jax.experimental.pallas import tpu as pltpu
from jax.sharding import PartitionSpec as P

CH = 256
HALO = 16
GROUP = 4
LOG2E = 1.4426950408889634
epsilon = 1e-05
f32 = jnp.float32
bf16 = jnp.bfloat16
highest = lax.Precision.HIGHEST


def mm(a, b):
    return lax.dot_general(a, b, (((1,), (0,)), ((), ())), preferred_element_type=f32)


def mmt(a, b):
    return lax.dot_general(a, b, (((1,), (1,)), ((), ())), preferred_element_type=f32)


def tmm(a, b):
    return lax.dot_general(a, b, (((0,), (0,)), ((), ())), preferred_element_type=f32)


def exact(a, b):
    return lax.dot_general(
        a, b, (((1,), (0,)), ((), ())), precision=highest, preferred_element_type=f32
    )


def head_map(channels, kind):
    return (jnp.arange(channels)[:, None] // 64 == jnp.arange(128)[None, :]).astype(kind)


def spread(cols, first, rows, lane_low):
    parts = []
    for pair in range(GROUP // 2):
        left = jnp.broadcast_to(cols[:, first + 2 * pair : first + 2 * pair + 1], (rows, 128))
        right = jnp.broadcast_to(cols[:, first + 2 * pair + 1 : first + 2 * pair + 2], (rows, 128))
        parts.append(jnp.where(lane_low, left, right))
    return jnp.concatenate(parts, axis=1)


def conv_pre(x_ref, cw_ref, flags, start, rows):
    pre = cw_ref[4:5, :] + cw_ref[0:1, :] * x_ref[0, HALO + start : HALO + start + rows, :]
    for k in range(1, 4):
        shifted = x_ref[0, HALO + start - k : HALO + start - k + rows, :]
        pre = pre + (cw_ref[k : k + 1, :] * shifted) * flags[:, k - 1 : k]
    return pre


def masked_scores(cb_ref, bc_ref, fl_ref, rv_ref, n_chunks, rows):
    for c in range(n_chunks):
        at = slice(c * rows, (c + 1) * rows)
        ids_col = fl_ref[0, at, 3:4]
        ids_row = rv_ref[0, 24:25, at]
        t_at = lax.broadcasted_iota(jnp.int32, (rows, rows), 0)
        s_at = lax.broadcasted_iota(jnp.int32, (rows, rows), 1)
        keep = (ids_col == ids_row) & (t_at >= s_at)
        scores = lax.dot_general(
            bc_ref[0, at, 128:], bc_ref[0, at, :128], (((1,), (1,)), ((), ())),
            precision=highest, preferred_element_type=f32,
        )
        cb_ref[c] = jnp.where(keep, scores, 0.0)


def scan_fwd_body(n_chunks, rows, hv_ref, fl_ref, rv_ref, al_ref, bc_ref, bt_ref, x_ref, cw_ref, y_ref, st_ref, cb_ref):
    group = pl.program_id(1)
    turn = lax.rem(128 - GROUP * group, 128)

    @pl.when(group == 0)
    def _():
        masked_scores(cb_ref, bc_ref, fl_ref, rv_ref, n_chunks, rows)

    lane_low = lax.broadcasted_iota(jnp.int32, (rows, 128), 1) < 64
    state = jnp.zeros((128, GROUP * 64), f32)
    for c in range(n_chunks):
        at = slice(c * rows, (c + 1) * rows)
        cols = pltpu.roll(hv_ref[0, at, :], turn, 1)
        flags = fl_ref[0, at, :]
        pre = conv_pre(x_ref, cw_ref, flags, c * rows, rows)
        act = pre * jax.nn.sigmoid(pre)
        u = act * spread(cols, 32, rows, lane_low)
        ub = u.astype(bf16)
        y = cw_ref[5:6, :] * act
        if c > 0:
            c_rows = bc_ref[0, at, 128:].astype(bf16)
            y = y + mm(c_rows, state.astype(bf16)) * spread(cols, 64, rows, lane_low)
        scores = cb_ref[c]
        parts = []
        for pair in range(GROUP // 2):
            u_pair = ub[:, 128 * pair : 128 * pair + 128]
            outs = []
            for j in (2 * pair, 2 * pair + 1):
                gap = cols[:, j : j + 1] - rv_ref[0, pl.ds(group * GROUP + j, 1), at]
                mix = (scores * jnp.exp2(jnp.minimum(gap, 0.0))).astype(bf16)
                outs.append(mm(mix, u_pair))
            parts.append(jnp.where(lane_low, outs[0], outs[1]))
        y_ref[0, at, :] = y + jnp.concatenate(parts, axis=1)
        wu = (u * spread(cols, 96, rows, lane_low)).astype(bf16)
        state = al_ref[0, c : c + 1, :] * state + mm(bt_ref[0, :128, at], wu)
        st_ref[0, c] = state


def scan_fwd(hv, fl, rv, al, bc, bt, x_ext, cw, rows, first=0, count=2):
    length = hv.shape[1]
    n_chunks = length // rows
    width = GROUP * 64
    channels = x_ext.shape[2]
    groups = channels // width
    return pl.pallas_call(
        lambda *refs: scan_fwd_body(n_chunks, rows, *refs),
        grid=(count, groups),
        in_specs=[
            pl.BlockSpec((1, length, 128), lambda s, g: (first + s, 0, 0)),
            pl.BlockSpec((1, length, 8), lambda s, g: (first + s, 0, 0)),
            pl.BlockSpec((1, 32, length), lambda s, g: (first + s, 0, 0)),
            pl.BlockSpec((1, 8, width), lambda s, g: (first + s, 0, g)),
            pl.BlockSpec((1, length, 256), lambda s, g: (first + s, 0, 0)),
            pl.BlockSpec((1, 256, length), lambda s, g: (first + s, 0, 0)),
            pl.BlockSpec((1, HALO + length, width), lambda s, g: (first + s, 0, g)),
            pl.BlockSpec((8, width), lambda s, g: (0, g)),
        ],
        out_specs=[
            pl.BlockSpec((1, length, width), lambda s, g: (s, 0, g)),
            pl.BlockSpec((1, n_chunks, 128, width), lambda s, g: (s, 0, 0, g)),
        ],
        out_shape=[
            jax.ShapeDtypeStruct((count, length, channels), f32),
            jax.ShapeDtypeStruct((count, n_chunks, 128, channels), f32),
        ],
        scratch_shapes=[pltpu.VMEM((n_chunks, rows, rows), f32)],
        cost_estimate=pl.CostEstimate(
            flops=count * groups * GROUP * length * (rows + 256) * 128 * 2,
            transcendentals=count * groups * GROUP * length * rows,
            bytes_accessed=count * length * channels * 8,
        ),
        name="scan_fwd",
    )(hv, fl, rv, al, bc, bt, x_ext, cw)


def scan_bwd_body(
    n_chunks, rows, hv_ref, fl_ref, rv_ref, al_ref, bc_ref, bt_ref, x_ref, cw_ref, dy_ref, st_ref, sr_ref, rr_ref, seg_ref,
    xl_ref, tail_ref, head_ref, dbc_ref, dcol_ref, drow_ref, dcw_ref, cb_ref, dcb_ref, dpre_ref,
):
    group = pl.program_id(1)
    turn = lax.rem(128 - GROUP * group, 128)
    length = n_chunks * rows
    width = GROUP * 64

    @pl.when(group == 0)
    def _():
        masked_scores(cb_ref, bc_ref, fl_ref, rv_ref, n_chunks, rows)
        dcb_ref[...] = jnp.zeros_like(dcb_ref)
        dbc_ref[...] = jnp.zeros_like(dbc_ref)
        dcol_ref[...] = jnp.zeros_like(dcol_ref)
        drow_ref[...] = jnp.zeros_like(drow_ref)

    lane_low = lax.broadcasted_iota(jnp.int32, (rows, 128), 1) < 64
    lane = lax.broadcasted_iota(jnp.int32, (rows, 128), 1)
    row_at = lax.broadcasted_iota(jnp.int32, (rows, width), 0)
    grad_state = rr_ref[0].astype(f32)
    recv = sr_ref[0].astype(f32)
    states = [recv]
    carry = recv
    for c in range(n_chunks - 1):
        carry = al_ref[0, c : c + 1, :] * carry
        states.append(st_ref[0, c] + carry)
    tap_sums = [jnp.zeros((1, width), f32) for _ in range(6)]
    dpre_ref[length : length + 8, :] = jnp.zeros((8, width), f32)
    for c in reversed(range(n_chunks)):
        at = slice(c * rows, (c + 1) * rows)
        cols = pltpu.roll(hv_ref[0, at, :], turn, 1)
        flags = fl_ref[0, at, :]
        pre = conv_pre(x_ref, cw_ref, flags, c * rows, rows)
        sig = jax.nn.sigmoid(pre)
        act = pre * sig
        step_wide = spread(cols, 32, rows, lane_low)
        end_wide = spread(cols, 96, rows, lane_low)
        u = act * step_wide
        ub = u.astype(bf16)
        dy = dy_ref[0, at, :]
        dyb = dy.astype(bf16)
        b_rows = bc_ref[0, at, :128].astype(bf16)
        c_rows = bc_ref[0, at, 128:].astype(bf16)
        state_b = states[c].astype(bf16)
        dye = dy * spread(cols, 64, rows, lane_low)
        dyeb = dye.astype(bf16)
        gs_b = grad_state.astype(bf16)
        wub = (u * end_wide).astype(bf16)
        dbc_ref[0, at, 128:] += mmt(dyeb, state_b)
        dbc_ref[0, at, :128] += mmt(wub, gs_b)
        du_state = mm(b_rows, gs_b) * end_wide
        u_du = u * du_state
        at_end = jnp.sum(u_du, axis=0, keepdims=True) + al_ref[0, c : c + 1, :] * jnp.sum(
            grad_state * states[c], axis=0, keepdims=True
        )
        log_grad = dye * mm(c_rows, state_b) - u_du
        log_grad = jnp.where(row_at == rows - 1, log_grad + at_end, log_grad)
        grad_state = al_ref[0, c : c + 1, :] * grad_state + mm(bt_ref[0, 128:, at], dyeb)
        scores = cb_ref[c]
        dcb = dcb_ref[c]
        parts = []
        row_sums = jnp.zeros((rows, 128), f32)
        for pair in range(GROUP // 2):
            lanes = slice(128 * pair, 128 * pair + 128)
            u_pair = ub[:, lanes]
            dy_pair = dyb[:, lanes]
            outs = []
            for j in (2 * pair, 2 * pair + 1):
                gap = cols[:, j : j + 1] - rv_ref[0, pl.ds(group * GROUP + j, 1), at]
                decay = jnp.exp2(jnp.minimum(gap, 0.0))
                mix = (scores * decay).astype(bf16)
                own = lane_low if j % 2 == 0 else jnp.logical_not(lane_low)
                prod = mmt(jnp.where(own, dy_pair, jnp.zeros_like(dy_pair)), u_pair) * decay
                dcb = dcb + prod
                full = prod * scores
                row_sums = jnp.where(
                    lane == group * GROUP + j, jnp.sum(full, axis=1, keepdims=True), row_sums
                )
                drow_ref[0, pl.ds(group * GROUP + j, 1), at] = jnp.sum(full, axis=0, keepdims=True)
                outs.append(tmm(mix, dy_pair))
            parts.append(jnp.where(lane_low, outs[0], outs[1]))
        dcb_ref[c] = dcb
        du = jnp.concatenate(parts, axis=1) + du_state
        seg = seg_ref[...]
        dcol_ref[0, at, :128] += row_sums + lax.dot_general(
            log_grad, seg, (((1,), (0,)), ((), ())), precision=highest, preferred_element_type=f32
        )
        dcol_ref[0, at, 128:] += lax.dot_general(
            du * act, seg, (((1,), (0,)), ((), ())), precision=highest, preferred_element_type=f32
        )
        dact = du * step_wide + cw_ref[5:6, :] * dy
        dpre = dact * (sig * (1.0 + pre * (1.0 - sig)))
        dpre_ref[at, :] = dpre
        tap_sums[0] += jnp.sum(dpre * x_ref[0, HALO + c * rows : HALO + (c + 1) * rows, :], axis=0, keepdims=True)
        for k in range(1, 4):
            shifted = x_ref[0, HALO + c * rows - k : HALO + (c + 1) * rows - k, :]
            tap_sums[k] += jnp.sum(dpre * flags[:, k - 1 : k] * shifted, axis=0, keepdims=True)
        tap_sums[4] += jnp.sum(dpre, axis=0, keepdims=True)
        tap_sums[5] += jnp.sum(dy * act, axis=0, keepdims=True)
        xg = cw_ref[0:1, :] * dpre
        for k in range(1, 4):
            xg = xg + (cw_ref[k : k + 1, :] * dpre_ref[c * rows + k : (c + 1) * rows + k, :]) * flags[:, 3 + k : 4 + k]
        xl_ref[0, at, :] = xg.astype(bf16)
        if c == n_chunks - 1:
            tail_ref[0] = xg[rows - 16 :, :]
        if c == 0:
            head_ref[0] = dpre[:8, :]
    dcw_ref[0] = jnp.concatenate(tap_sums + [jnp.zeros((2, width), f32)], axis=0)

    @pl.when(group == pl.num_programs(1) - 1)
    def _():
        for c in range(n_chunks):
            at = slice(c * rows, (c + 1) * rows)
            ids_col = fl_ref[0, at, 3:4]
            ids_row = rv_ref[0, 24:25, at]
            t_at = lax.broadcasted_iota(jnp.int32, (rows, rows), 0)
            s_at = lax.broadcasted_iota(jnp.int32, (rows, rows), 1)
            keep = (ids_col == ids_row) & (t_at >= s_at)
            grad = jnp.where(keep, dcb_ref[c], 0.0).astype(bf16)
            dbc_ref[0, at, 128:] += mm(grad, bc_ref[0, at, :128].astype(bf16))
            dbc_ref[0, at, :128] += tmm(grad, bc_ref[0, at, 128:].astype(bf16))


def scan_bwd(hv, fl, rv, al, bc, bt, x_ext, cw, dy, states, s_recv, r_recv, rows, first=0, count=2):
    length = hv.shape[1]
    n_chunks = length // rows
    width = GROUP * 64
    channels = x_ext.shape[2]
    groups = channels // width
    seg = head_map(channels, f32)
    return pl.pallas_call(
        lambda *refs: scan_bwd_body(n_chunks, rows, *refs),
        grid=(count, groups),
        in_specs=[
            pl.BlockSpec((1, length, 128), lambda s, g: (first + s, 0, 0)),
            pl.BlockSpec((1, length, 8), lambda s, g: (first + s, 0, 0)),
            pl.BlockSpec((1, 32, length), lambda s, g: (first + s, 0, 0)),
            pl.BlockSpec((1, 8, width), lambda s, g: (first + s, 0, g)),
            pl.BlockSpec((1, length, 256), lambda s, g: (first + s, 0, 0)),
            pl.BlockSpec((1, 256, length), lambda s, g: (first + s, 0, 0)),
            pl.BlockSpec((1, HALO + length, width), lambda s, g: (first + s, 0, g)),
            pl.BlockSpec((8, width), lambda s, g: (0, g)),
            pl.BlockSpec((1, length, width), lambda s, g: (first + s, 0, g)),
            pl.BlockSpec((1, n_chunks, 128, width), lambda s, g: (first + s, 0, 0, g)),
            pl.BlockSpec((1, 128, width), lambda s, g: (first + s, 0, g)),
            pl.BlockSpec((1, 128, width), lambda s, g: (first + s, 0, g)),
            pl.BlockSpec((width, 128), lambda s, g: (g, 0)),
        ],
        out_specs=[
            pl.BlockSpec((1, length, width), lambda s, g: (s, 0, g)),
            pl.BlockSpec((1, 16, width), lambda s, g: (s, 0, g)),
            pl.BlockSpec((1, 8, width), lambda s, g: (s, 0, g)),
            pl.BlockSpec((1, length, 256), lambda s, g: (s, 0, 0)),
            pl.BlockSpec((1, length, 256), lambda s, g: (s, 0, 0)),
            pl.BlockSpec((1, 32, length), lambda s, g: (s, 0, 0)),
            pl.BlockSpec((1, 8, width), lambda s, g: (s, 0, g)),
        ],
        out_shape=[
            jax.ShapeDtypeStruct((count, length, channels), bf16),
            jax.ShapeDtypeStruct((count, 16, channels), f32),
            jax.ShapeDtypeStruct((count, 8, channels), f32),
            jax.ShapeDtypeStruct((count, length, 256), f32),
            jax.ShapeDtypeStruct((count, length, 256), f32),
            jax.ShapeDtypeStruct((count, 32, length), f32),
            jax.ShapeDtypeStruct((count, 8, channels), f32),
        ],
        scratch_shapes=[
            pltpu.VMEM((n_chunks, rows, rows), f32),
            pltpu.VMEM((n_chunks, rows, rows), f32),
            pltpu.VMEM((length + 8, width), f32),
        ],
        cost_estimate=pl.CostEstimate(
            flops=count * groups * GROUP * length * (rows + 256) * 128 * 6,
            transcendentals=count * groups * GROUP * length * rows,
            bytes_accessed=count * length * channels * 12,
        ),
        name="scan_bwd",
    )(hv, fl, rv, al, bc, bt, x_ext, cw, dy, states, s_recv, r_recv, seg)


def project_body(places, skip, at_ref, *refs):
    left_ref, right_ref, blocks, out_ref, full_ref = refs[0], refs[1], refs[2:-2], refs[-2], refs[-1]

    @pl.when(pl.program_id(0) == 0)
    def _():
        for ref, (d, k) in zip(blocks, places):
            rows, columns = ref.shape[1:]
            row = pl.multiple_of(at_ref[k], rows)
            column = pl.multiple_of(at_ref[4 + d], columns)
            full_ref[pl.ds(row, rows), pl.ds(column, columns)] = ref[0]
        out_ref[...] = mm(left_ref[skip:, :], full_ref[...])

    @pl.when(pl.program_id(0) == 1)
    def _():
        out_ref[...] = mm(right_ref[skip:, :], full_ref[...])


def project(acts, skip, at, items, weight, channels):
    rows, features = acts[0].shape
    rows = rows - skip
    blocks = [item[0] for item in items]
    places = [item[1:] for item in items]
    return pl.pallas_call(
        lambda *refs: project_body(places, skip, *refs),
        grid_spec=pltpu.PrefetchScalarGridSpec(
            num_scalar_prefetch=1,
            grid=(2,),
            in_specs=[pl.BlockSpec(v.shape, lambda i, at: (0, 0), pipeline_mode=pl.Buffered(1)) for v in acts]
            + [
                pl.BlockSpec((1,) + b.shape[1:], lambda i, at: (weight, 0, 0), pipeline_mode=pl.Buffered(1))
                for b in blocks
            ],
            out_specs=[
                pl.BlockSpec((rows, channels), lambda i, at: (i, 0)),
                pl.BlockSpec((features, channels), lambda i, at: (0, 0), pipeline_mode=pl.Buffered(1)),
            ],
        ),
        out_shape=[
            jax.ShapeDtypeStruct((2 * rows, channels), f32),
            jax.ShapeDtypeStruct((features, channels), bf16),
        ],
        cost_estimate=pl.CostEstimate(
            flops=4 * rows * features * channels,
            transcendentals=0,
            bytes_accessed=rows * features * 4 + rows * channels * 8 + features * channels * 4,
        ),
        name="project",
    )(at, *acts, *blocks)


def turn_body(x_ref, out_ref):
    out_ref[...] = x_ref[...].T


def turn(x):
    rows, columns = x.shape
    return pl.pallas_call(
        turn_body, out_shape=jax.ShapeDtypeStruct((columns, rows), x.dtype), name="turn", cost_estimate=pl.CostEstimate(flops=1, transcendentals=0, bytes_accessed=1)
    )(x)


def norm_body(x_ref, halo_ref, gain_ref, out_ref, turned_ref):
    def normed(ref, at):
        x = ref[at, :].astype(f32)
        inv = lax.rsqrt(jnp.mean(x * x, axis=-1, keepdims=True) + epsilon)
        return (x * inv * gain_ref[...]).astype(bf16)

    out_ref[:HALO, :] = normed(halo_ref, slice(0, HALO))
    for r in range(x_ref.shape[0] // 128):
        rows = normed(x_ref, slice(128 * r, 128 * r + 128))
        out_ref[HALO + 128 * r : HALO + 128 * r + 128, :] = rows
        turned_ref[:, 128 * r : 128 * r + 128] = rows.T


def norm(x, halo, gain):
    rows, features = x.shape
    return pl.pallas_call(
        norm_body,
        out_shape=[
            jax.ShapeDtypeStruct((HALO + rows, features), bf16),
            jax.ShapeDtypeStruct((features, rows), bf16),
        ],
        cost_estimate=pl.CostEstimate(flops=1, transcendentals=0, bytes_accessed=1),
        name="norm",
    )(x, halo, gain)


def prepare_body(
    own_ref, other_ref, thin_ref, pick_ref, lanes_ref, cbc_ref, ids_ref, row_ref,
    bcx_ref, pre_ref, act_ref, turned_ref, low_ref, dt_ref, log_ref, hv_ref, rv_ref, al_ref, since_ref, flags_ref,
    scr_ref,
):
    length = act_ref.shape[1]
    n_chunks = length // CH
    width = pre_ref.shape[2]
    channels = al_ref.shape[2]
    picked = mm(thin_ref[:, width:], pick_ref[...]).astype(bf16)
    weights = jnp.concatenate([thin_ref[:, :width], picked], axis=1)

    @pl.when(pl.program_id(0) == 0)
    def _():
        scr_ref[...] = mm(own_ref[...], weights)

    @pl.when(pl.program_id(0) == 1)
    def _():
        scr_ref[...] = mm(other_ref[...], weights)

    columns = ids_ref[0].T
    at = slice(HALO, HALO + length)
    ids = columns[at, :1]
    before = columns[HALO - 1 : HALO, :1]
    eight = lax.broadcasted_iota(jnp.int32, (length, 8), 1)
    flags = jnp.where(eight == 3, ids, 0.0)
    near = {}
    for j, k in enumerate((-1, -2, -3, 0, 1, 2, 3)):
        if k != 0:
            near[k] = (columns[HALO + k : HALO + k + length, :1] == ids).astype(f32)
            flags = jnp.where(eight == j, near[k], flags)
    flags_ref[0] = flags

    bcx_ref[0] = scr_ref[:, :width]
    pre = cbc_ref[4:5, :] + cbc_ref[0:1, :] * scr_ref[at, :width]
    for k in range(1, 4):
        pre = pre + cbc_ref[k : k + 1, :] * scr_ref[HALO - k : HALO - k + length, :width] * near[-k]
    act = pre * jax.nn.sigmoid(pre)
    pre_ref[0] = pre
    act_ref[0] = act
    turned_ref[0] = act.T.astype(bf16)
    low_ref[0] = act[:, width // 2 :].astype(bf16)

    dt_in = scr_ref[at, width:] + lanes_ref[0:1, :]
    dt_ref[0] = dt_in
    step = jnp.maximum(dt_in, 0.0) + jnp.log1p(jnp.exp(-jnp.abs(dt_in)))
    log_step = step * lanes_ref[1:2, :]
    log_ref[0] = log_step
    tri = (
        lax.broadcasted_iota(jnp.int32, (CH, CH), 0) >= lax.broadcasted_iota(jnp.int32, (CH, CH), 1)
    ).astype(f32)
    quarter = lax.broadcasted_iota(jnp.int32, (CH, 128), 1) // 32
    low_lanes = lax.broadcasted_iota(jnp.int32, (CH, 128), 1) < 32
    row_at = lax.broadcasted_iota(jnp.int32, (32, CH), 0)
    to_wide = (
        lax.broadcasted_iota(jnp.int32, (128, channels), 1) // 64 == lax.broadcasted_iota(jnp.int32, (128, channels), 0)
    ).astype(f32)
    eight_rows = lax.broadcasted_iota(jnp.int32, (8, 128), 0)
    alphas = jnp.zeros((8, 128), f32)
    lead = jnp.zeros((1, 128), f32)
    chunk_before = before
    for c in range(n_chunks):
        rows = slice(c * CH, (c + 1) * CH)
        running = exact(tri, log_step[rows])
        last = running[CH - 1 : CH, :]
        ids_c = ids[rows]
        chunk_end = ids_c[CH - 1 : CH, :]
        still = (chunk_end == chunk_before).astype(f32)
        alphas = jnp.where(eight_rows == c, still * jnp.exp(last), alphas)
        since = (ids_c == before).astype(f32) * jnp.exp(running + lead)
        since = jnp.where(low_lanes, since, 0.0).astype(bf16)
        since_ref[0, rows, :] = mm(since, to_wide.astype(bf16)).astype(bf16)
        hv = jnp.where(
            quarter == 0,
            running * LOG2E,
            jnp.where(
                quarter == 1,
                step[rows],
                jnp.where(
                    quarter == 2,
                    (ids_c == chunk_before).astype(f32) * jnp.exp(running),
                    (ids_c == chunk_end).astype(f32) * jnp.exp(last - running),
                ),
            ),
        )
        hv_ref[0, rows, :] = hv
        turned = hv.T[:32, :]
        rv_ref[0, :, rows] = jnp.where(
            row_at < 24, turned, jnp.where(row_at == 24, row_ref[0, 0:1, rows], 0.0)
        )
        lead = lead + last
        chunk_before = chunk_end
    first = lax.broadcasted_iota(jnp.int32, (8, 128), 1) < 32
    al_ref[0] = exact(jnp.where(first, alphas, 0.0), to_wide)


def prepare(own, other, thin, pick, lanes, cbc, ids_all, ids_rows, channels):
    length = own.shape[0] - HALO
    width = cbc.shape[1]
    whole = lambda v: pl.BlockSpec(v.shape, lambda s: (0,) * len(v.shape), pipeline_mode=pl.Buffered(1))
    piece = lambda shape: pl.BlockSpec((1,) + shape, lambda s: (s, 0, 0))
    outs = [
        ((HALO + length, width), f32), ((length, width), f32), ((length, width), f32), ((width, length), bf16),
        ((length, width // 2), bf16), ((length, 128), f32), ((length, 128), f32), ((length, 128), f32),
        ((32, length), f32), ((8, channels), f32), ((length, channels), bf16), ((length, 8), f32),
    ]
    return pl.pallas_call(
        prepare_body,
        grid=(2,),
        in_specs=[whole(v) for v in (own, other, thin, pick, lanes, cbc)]
        + [piece(ids_all.shape[1:]), piece(ids_rows.shape[1:])],
        out_specs=[piece(shape) for shape, _ in outs],
        out_shape=[jax.ShapeDtypeStruct((2,) + shape, kind) for shape, kind in outs],
        scratch_shapes=[pltpu.VMEM((HALO + length, width + 128), f32)],
        cost_estimate=pl.CostEstimate(flops=1, transcendentals=0, bytes_accessed=1),
        name="prepare",
    )(own, other, thin, pick, lanes, cbc, ids_all, ids_rows)


def gate_sums_body(here_ref, since_ref, low_ref, state_ref, gate_ref, grad_ref, gain_ref, y_ref, sums_ref):
    y = here_ref[...] + since_ref[...].astype(f32) * mm(low_ref[...], state_ref[0])
    y_ref[...] = y
    gate = gate_ref[...]
    gated = y * (gate * jax.nn.sigmoid(gate))
    scaled = grad_ref[...] * gain_ref[...]
    lane = lax.broadcasted_iota(jnp.int32, sums_ref.shape, 1)
    sums_ref[...] = jnp.where(
        lane == 0,
        jnp.sum(gated * gated, axis=1, keepdims=True),
        jnp.where(lane == 1, jnp.sum(scaled * gated, axis=1, keepdims=True), 0.0),
    )


def gate_sums(here, since, low, state, gate, grad, gain):
    tokens, channels = here.shape
    tile = 128
    per = tokens // tile // 2
    token = lambda width: pl.BlockSpec((tile, width), lambda i: (i, 0))
    return pl.pallas_call(
        gate_sums_body,
        grid=(tokens // tile,),
        in_specs=[
            token(channels), token(channels), token(low.shape[1]),
            pl.BlockSpec((1,) + state.shape[1:], lambda i: (i // per, 0, 0)),
            token(channels), token(channels), pl.BlockSpec((1, channels), lambda i: (0, 0)),
        ],
        out_specs=[token(channels), token(128)],
        out_shape=[jax.ShapeDtypeStruct((tokens, channels), f32), jax.ShapeDtypeStruct((tokens, 128), f32)],
        cost_estimate=pl.CostEstimate(flops=1, transcendentals=0, bytes_accessed=1),
        name="gate_sums",
    )(here, since, low, state, gate, grad, gain)


def gate_grads_body(
    all_channels, per, y_ref, since_ref, low_ref, gate_ref, grad_ref, gain_ref, sums_ref, came_ref,
    mixed_ref, gate_grad_ref, y_grad_ref, gain_grad_ref, state_ref,
):
    at = pl.program_id(0)
    y = y_ref[...]
    gate = gate_ref[...]
    grad = grad_ref[...]
    sums = sums_ref[...] + came_ref[...]
    gate_rms = lax.rsqrt(sums[:, 0:1] / all_channels + epsilon)
    inner = gate_rms * gate_rms * gate_rms * (sums[:, 1:2] / all_channels)
    sig = jax.nn.sigmoid(gate)
    act = gate * sig
    gated = y * act
    hat = gated * gate_rms
    mixed_ref[...] = (hat * gain_ref[...]).astype(bf16)
    gated_grad = gate_rms * (grad * gain_ref[...]) - gated * inner
    y_grad = gated_grad * act
    y_grad_ref[...] = y_grad
    gate_grad_ref[...] = (gated_grad * y * sig * (1.0 + gate * (1.0 - sig))).astype(bf16)
    part = jnp.sum((grad * hat).reshape((y.shape[0] // 8, 8, y.shape[1])), axis=0)
    pushed = tmm(low_ref[...], (y_grad * since_ref[...].astype(f32)).astype(bf16))

    @pl.when(at == 0)
    def _():
        gain_grad_ref[...] = part

    @pl.when(at > 0)
    def _():
        gain_grad_ref[...] += part

    @pl.when(lax.rem(at, per) == 0)
    def _():
        state_ref[0] = pushed

    @pl.when(lax.rem(at, per) > 0)
    def _():
        state_ref[0] += pushed


def gate_grads(y, since, low, gate, grad, gain, sums, came, all_channels):
    tokens, channels = y.shape
    tile = 128
    count = tokens // tile
    per = count // 2
    token = lambda width: pl.BlockSpec((tile, width), lambda i: (i, 0))
    turned = pl.BlockSpec((tile, 128), lambda i: (lax.rem(i + per, count), 0))
    return pl.pallas_call(
        lambda *refs: gate_grads_body(all_channels, per, *refs),
        grid=(count,),
        in_specs=[
            token(channels), token(channels), token(low.shape[1]), token(channels), token(channels),
            pl.BlockSpec((1, channels), lambda i: (0, 0)), token(128), turned,
        ],
        out_specs=[
            token(channels), token(channels), token(channels), pl.BlockSpec((8, channels), lambda i: (0, 0)),
            pl.BlockSpec((1, low.shape[1], channels), lambda i: (i // per, 0, 0)),
        ],
        out_shape=[
            jax.ShapeDtypeStruct((tokens, channels), bf16),
            jax.ShapeDtypeStruct((tokens, channels), bf16),
            jax.ShapeDtypeStruct((tokens, channels), f32),
            jax.ShapeDtypeStruct((8, channels), f32),
            jax.ShapeDtypeStruct((2, low.shape[1], channels), f32),
        ],
        cost_estimate=pl.CostEstimate(flops=1, transcendentals=0, bytes_accessed=1),
        name="gate_grads",
    )(y, since, low, gate, grad, gain, sums, came)


def small_grads_body(
    dbc_ref, came_ref, pre_ref, bcx_ref, flags_ref, own_col_ref, other_col_ref, own_row_ref, other_row_ref,
    log_ref, dt_ref, lanes_ref, back_ref, own_sums_ref, other_sums_ref, gain_ref, dpre_ref, dt_low_ref, taps_ref,
    packed_ref,
):
    length = dpre_ref.shape[0]
    width = dpre_ref.shape[1]
    channels = packed_ref.shape[1]
    pre = pre_ref[0]
    sig = jax.nn.sigmoid(pre)
    dpre = (dbc_ref[0] + came_ref[...]) * (sig * (1.0 + pre * (1.0 - sig)))
    dpre_ref[...] = dpre
    sums = [jnp.sum(dpre * bcx_ref[0, HALO:, :], axis=0, keepdims=True)]
    for k in range(1, 4):
        shifted = bcx_ref[0, HALO - k : HALO - k + length, :]
        sums.append(jnp.sum(dpre * shifted * flags_ref[0, :, k - 1 : k], axis=0, keepdims=True))
    sums.append(jnp.sum(dpre, axis=0, keepdims=True))
    taps_ref[...] = jnp.concatenate(sums + [jnp.zeros((11, width), f32)], axis=0)

    tri = (
        lax.broadcasted_iota(jnp.int32, (CH, CH), 1) >= lax.broadcasted_iota(jnp.int32, (CH, CH), 0)
    ).astype(f32)
    raw_sum = jnp.zeros((1, 128), f32)
    rate_sum = jnp.zeros((1, 128), f32)
    for p, (col_ref, row_ref) in enumerate(((own_col_ref, own_row_ref), (other_col_ref, other_row_ref))):
        for c in range(length // CH):
            rows = slice(c * CH, (c + 1) * CH)
            by_row = jnp.concatenate([row_ref[0, :, rows], jnp.zeros((96, CH), f32)], axis=0).T
            dlog = exact(tri, col_ref[0, rows, :128] - by_row)
            dstep = col_ref[0, rows, 128:] + dlog * lanes_ref[1:2, :]
            raw = dstep * jax.nn.sigmoid(dt_ref[p, rows, :])
            rate_sum += jnp.sum(dlog * log_ref[p, rows, :], axis=0, keepdims=True)
            raw_sum += jnp.sum(raw, axis=0, keepdims=True)
            dt_low_ref[p, rows, :] = mm(raw.astype(bf16), back_ref[...]).astype(bf16)
    to_wide = (
        lax.broadcasted_iota(jnp.int32, (128, channels), 1) // 64 == lax.broadcasted_iota(jnp.int32, (128, channels), 0)
    ).astype(f32)
    both = jnp.concatenate([raw_sum, rate_sum, jnp.zeros((6, 128), f32)], axis=0)
    first = lax.broadcasted_iota(jnp.int32, (8, 128), 1) < 32
    wide = exact(jnp.where(first, both, 0.0), to_wide)
    sums = own_sums_ref[0] + other_sums_ref[0]
    gain = jnp.sum(gain_ref[...], axis=0, keepdims=True)
    packed_ref[...] = jnp.concatenate(
        [sums[:5], gain, sums[5:6], wide[:2], jnp.zeros((7, channels), f32)], axis=0
    )


def small_grads(dbc, came, pre, *rest):
    length, width = came.shape
    channels = rest[-1].shape[1]
    return pl.pallas_call(
        small_grads_body,
        out_shape=[
            jax.ShapeDtypeStruct((length, width), f32),
            jax.ShapeDtypeStruct((2, length, 128), bf16),
            jax.ShapeDtypeStruct((16, width), f32),
            jax.ShapeDtypeStruct((16, channels), f32),
        ],
        cost_estimate=pl.CostEstimate(flops=1, transcendentals=0, bytes_accessed=1),
        name="small_grads",
    )(dbc, came, pre, *rest)


def normed_grads_body(
    dpre_ref, head_ref, flags_ref, cbc_ref, dt_low_ref, own_turned_ref, other_turned_ref, own_ref, other_ref, gate_ref,
    wx_ref, wz_ref, thin_ref, own_out_ref, other_out_ref, part_ref, low_ref, scr_ref,
):
    length, width = dpre_ref.shape

    @pl.when((pl.program_id(0) == 0) & (pl.program_id(1) == 0))
    def _():
        scr_ref[:length, :] = dpre_ref[...]
        scr_ref[length:, :] = head_ref[...]
        raw = cbc_ref[0:1, :] * dpre_ref[...]
        for k in range(1, 4):
            raw = raw + cbc_ref[k : k + 1, :] * scr_ref[k : k + length, :] * flags_ref[0, :, 3 + k : 4 + k]
        own = jnp.concatenate([raw.astype(bf16), dt_low_ref[0]], axis=1)
        other = jnp.concatenate([jnp.zeros((length, width), bf16), dt_low_ref[1]], axis=1)
        low_ref[:length, :] = own
        low_ref[length:, :] = other
        part_ref[...] = (mm(own_turned_ref[...], own) + mm(other_turned_ref[...], other)).astype(bf16)

    def total(ref, rows):
        return (
            mmt(ref[...], wx_ref[...]) + mmt(gate_ref[rows, :], wz_ref[...]) + mmt(low_ref[rows, :], thin_ref[...])
        )

    @pl.when(pl.program_id(0) == 0)
    def _():
        other_out_ref[...] = total(other_ref, slice(length, 2 * length)).astype(bf16)

    @pl.when(pl.program_id(0) == 1)
    def _():
        own_out_ref[...] = total(own_ref, slice(0, length))


def normed_grads(dpre, head, flags, cbc, dt_low, turned, x_low, gate_grad, wx, wz, thin):
    length, width = dpre.shape
    features = wx.shape[0]
    tile = features // 3
    last = features // tile - 1
    whole = lambda v: pl.BlockSpec(v.shape, lambda p, j: (0,) * len(v.shape), pipeline_mode=pl.Buffered(1))
    weight = lambda v: pl.BlockSpec((tile, v.shape[1]), lambda p, j: (j, 0))
    return pl.pallas_call(
        normed_grads_body,
        grid=(2, features // tile),
        in_specs=[whole(v) for v in (dpre, head, flags, cbc, dt_low, *turned, *x_low, gate_grad)]
        + [weight(v) for v in (wx, wz, thin)],
        out_specs=[
            pl.BlockSpec((length, tile), lambda p, j: (0, j * p)),
            pl.BlockSpec((length, tile), lambda p, j: (0, j * (1 - p) + last * p)),
            pl.BlockSpec((features, width + 128), lambda p, j: (0, 0), pipeline_mode=pl.Buffered(1)),
        ],
        out_shape=[
            jax.ShapeDtypeStruct((length, features), f32),
            jax.ShapeDtypeStruct((length, features), bf16),
            jax.ShapeDtypeStruct((features, width + 128), bf16),
        ],
        scratch_shapes=[pltpu.VMEM((2 * length, width + 128), bf16), pltpu.VMEM((length + 8, width), f32)],
        cost_estimate=pl.CostEstimate(
            flops=8 * length * features * features, transcendentals=0, bytes_accessed=8 * features * features
        ),
        name="normed_grads",
    )(dpre, head, flags, cbc, dt_low, *turned, *x_low, gate_grad, wx, wz, thin)


def branch_body(mixed_ref, weight_ref, own_ref, other_ref):
    part = mmt(mixed_ref[...], weight_ref[...])

    @pl.when(pl.program_id(0) == 0)
    def _():
        other_ref[...] = part.astype(bf16)

    @pl.when(pl.program_id(0) == 1)
    def _():
        own_ref[...] = part


def branch_parts(mixed, weight):
    tokens, channels = mixed.shape
    features = weight.shape[0]
    half = pl.BlockSpec((tokens // 2, features), lambda p: (0, 0))
    return pl.pallas_call(
        branch_body,
        grid=(2,),
        in_specs=[
            pl.BlockSpec((tokens // 2, channels), lambda p: (1 - p, 0)),
            pl.BlockSpec(weight.shape, lambda p: (0, 0), pipeline_mode=pl.Buffered(1)),
        ],
        out_specs=[half, half],
        out_shape=[
            jax.ShapeDtypeStruct((tokens // 2, features), f32),
            jax.ShapeDtypeStruct((tokens // 2, features), bf16),
        ],
        cost_estimate=pl.CostEstimate(
            flops=2 * tokens * channels * features, transcendentals=0, bytes_accessed=4 * features * channels
        ),
        name="branch_parts",
    )(mixed, weight)


def x_grads_body(own_ref, came_ref, x_ref, cot_ref, gain_ref, out_ref, gain_grad_ref):
    grad = own_ref[...] + came_ref[...].astype(f32)
    x = x_ref[...].astype(f32)
    inv = lax.rsqrt(jnp.mean(x * x, axis=-1, keepdims=True) + epsilon)
    hat = x * inv
    part = jnp.sum((grad * hat).reshape((x.shape[0] // 8, 8, x.shape[1])), axis=0)
    pushed = grad * gain_ref[...]
    inner = jnp.mean(pushed * x, axis=-1, keepdims=True)
    out_ref[...] = cot_ref[...].astype(f32) + inv * pushed - hat * (inv * inv * inner)

    @pl.when(pl.program_id(0) == 0)
    def _():
        gain_grad_ref[...] = part

    @pl.when(pl.program_id(0) > 0)
    def _():
        gain_grad_ref[...] += part


def x_grads(own, came, x, cot, gain):
    tokens, features = own.shape
    tile = 128
    token = pl.BlockSpec((tile, features), lambda i: (i, 0))
    return pl.pallas_call(
        x_grads_body,
        grid=(tokens // tile,),
        in_specs=[token] * 4 + [pl.BlockSpec((1, features), lambda i: (0, 0))],
        out_specs=[token, pl.BlockSpec((8, features), lambda i: (0, 0))],
        out_shape=[jax.ShapeDtypeStruct((tokens, features), f32), jax.ShapeDtypeStruct((8, features), f32)],
        cost_estimate=pl.CostEstimate(flops=1, transcendentals=0, bytes_accessed=1),
        name="x_grads",
    )(own, came, x, cot, gain)


def weight_parts_body(count, group, flip, at_ref, *refs):
    keep_ref, give_ref = refs[-2:]
    rows, columns = keep_ref.shape[3:]
    rights_per = (len(refs) - 2) // count - 2
    for w in range(count):
        lefts = refs[2 * w : 2 * w + 2]
        rights = refs[2 * count + w * rights_per : 2 * count + (w + 1) * rights_per]
        tokens = lefts[0].shape[1]

        @pl.when(pl.program_id(0) == w)
        def _():
            def right(i):
                ref, start = (rights[0], i * tokens) if rights_per == 1 else (rights[i], 0)
                return jnp.concatenate(
                    [
                        ref[start : start + tokens, pl.ds(pl.multiple_of(at_ref[4 + d], columns), columns)]
                        for d in group
                    ],
                    axis=1,
                )

            values = [right(0), right(1)]
            for k in range(4):
                left = pl.ds(pl.multiple_of(at_ref[k], rows), rows)
                part = mm(lefts[0][left, :], values[0]) + mm(lefts[1][left, :], values[1])
                part = part.astype(bf16)
                away, place = (k // 2, k % 2) if flip == 0 else (k % 2, k // 2)
                target = give_ref if away else keep_ref
                for i in range(len(group)):
                    target[0, i, place] = part[:, i * columns : (i + 1) * columns]


def weight_parts(at, lefts, rights, group, own_rows, columns, flip):
    count = len(lefts)
    tokens = 2 * lefts[0][0].shape[1]
    lefts = [piece for left in lefts for piece in left]
    rights = [piece for right in rights for piece in right]
    shape = (count, len(group), 2, 2 * own_rows, columns)
    whole = lambda v: pl.BlockSpec(v.shape, lambda w, at: (0, 0), pipeline_mode=pl.Buffered(1))
    return pl.pallas_call(
        lambda *refs: weight_parts_body(count, group, flip, *refs),
        grid_spec=pltpu.PrefetchScalarGridSpec(
            num_scalar_prefetch=1,
            grid=(count,),
            in_specs=[whole(v) for v in lefts] + [whole(v) for v in rights],
            out_specs=[pl.BlockSpec((1,) + shape[1:], lambda w, at: (w, 0, 0, 0, 0))] * 2,
        ),
        out_shape=[jax.ShapeDtypeStruct(shape, bf16)] * 2,
        cost_estimate=pl.CostEstimate(
            flops=2 * count * tokens * 8 * own_rows * columns * len(group),
            transcendentals=0,
            bytes_accessed=count * tokens * (8 * own_rows + columns * len(group)) * 2,
        ),
        name="weight_parts",
    )(at, *lefts, *rights)


def swap(value):
    size = lax.axis_size("dp")
    return lax.ppermute(value, "dp", [(i, i ^ 1) for i in range(size)])


def across(value, bit):
    size = lax.axis_size("dp")
    return lax.ppermute(value, "dp", [(i, i ^ (1 << bit)) for i in range(size)])


def around(value, by):
    size = lax.axis_size("tensor")
    by = by % size
    return lax.ppermute(value, "tensor", [(i, (i + by) % size) for i in range(size)])


def along_sequence(value, pieces, forward):
    size = lax.axis_size("tensor")
    pairs = [(i, i + 1) for i in range(size - 1) if (i + 1) % pieces]
    if not forward:
        pairs = [(b, a) for a, b in pairs]
    return lax.ppermute(value, "tensor", pairs)


class Place:
    def __init__(self):
        dp = lax.axis_index("dp")
        self.core = dp % 2
        self.slots = lax.axis_size("tensor")
        self.slot = lax.axis_index("tensor")
        self.bits = [b for b in range(1, lax.axis_size("dp").bit_length() - 1)]
        self.side = {b: (dp >> b) % 2 for b in range(lax.axis_size("dp").bit_length() - 1)}

    def gather_slots(self, block):
        blocks = [block] + [around(block, d) for d in range(1, self.slots)]
        shape = (block.shape[0], self.slots, block.shape[1])
        index = lax.broadcasted_iota(jnp.int32, shape, 1)
        out = jnp.broadcast_to(block[:, None, :], shape)
        for d in range(1, self.slots):
            from_slot = (self.slot - d) % self.slots
            out = jnp.where(index == from_slot, blocks[d][:, None, :], out)
        return out

    def scatter_slots(self, blocks):
        def block(at):
            return lax.dynamic_index_in_dim(blocks, at % self.slots, 1, keepdims=False)

        total = block(self.slot).astype(f32)
        for d in range(1, self.slots):
            total = total + around(block(self.slot + d), d).astype(f32)
        return total

    def ordered(self, bit, mine, other, axis):
        mine, other = jnp.expand_dims(mine, axis), jnp.expand_dims(other, axis)
        low = self.side[bit] == 0
        return jnp.where(
            low,
            jnp.concatenate([mine, other], axis=axis),
            jnp.concatenate([other, mine], axis=axis),
        )

    def gather_rows(self, block, upward):
        done = block
        for bit in self.bits if upward else self.bits[::-1]:
            axis = 0 if upward else len(done.shape) - 2
            done = self.ordered(bit, done, across(done, bit), axis)
        return done.reshape((-1, block.shape[1]))

    def scatter_rows(self, whole, upward, low_bit=1):
        bits = [b for b in self.bits if b >= low_bit]
        if low_bit == 0:
            bits = [0] + bits
        count = len(bits)
        rows = whole.shape[0] >> count
        left = sorted(bits, reverse=True)
        now = whole.reshape((2,) * count + (rows, whole.shape[1]))
        for bit in bits if upward else bits[::-1]:
            axis = left.index(bit)
            left.remove(bit)
            side = self.side[bit]
            keep = lax.dynamic_index_in_dim(now, side, axis, keepdims=False)
            give = lax.dynamic_index_in_dim(now, 1 - side, axis, keepdims=False)
            now = (keep.astype(f32) + across(give, bit).astype(f32)).astype(whole.dtype)
        return now

    def half_rows(self, whole, bit):
        keep = lax.dynamic_index_in_dim(whole, self.side[bit], whole.ndim - 3, keepdims=False)
        give = lax.dynamic_index_in_dim(whole, 1 - self.side[bit], whole.ndim - 3, keepdims=False)
        return (keep.astype(f32) + across(give, bit).astype(f32)).astype(whole.dtype)

    def ordered_sum(self, part):
        return self.half_rows(part.reshape((2, 2, 2, -1, part.shape[1])), 0)

    def gather_weight(self, mine, other):
        both = self.ordered(0, mine, other, 0).reshape((-1, mine.shape[1]))
        blocks = self.gather_slots(both)
        half = self.slots // 2
        first = blocks[:, :half].reshape((both.shape[0], -1))
        second = blocks[:, half:].reshape((both.shape[0], -1))
        return jnp.concatenate(
            [self.gather_rows(first, True), self.gather_rows(second, False)], axis=1
        )

    def scatter_weight(self, part):
        columns = part.shape[1] // 2
        half = self.slots // 2
        first = self.scatter_rows(part[:, :columns], False)
        second = self.scatter_rows(part[:, columns:], True)
        rows = first.shape[0]
        blocks = jnp.concatenate(
            [first.reshape((rows, half, -1)), second.reshape((rows, half, -1))], axis=1
        )
        mine = self.scatter_slots(blocks).reshape((2, rows // 2, -1))
        keep = lax.dynamic_index_in_dim(mine, self.core, 0, keepdims=False)
        give = lax.dynamic_index_in_dim(mine, 1 - self.core, 0, keepdims=False)
        out = self.ordered(0, keep, swap(give), 1)
        return out.reshape((rows // 2, -1))

    def fast(self, half_channels):
        return len(self.bits) == 2 and self.slots == 4 and half_channels % 128 == 0

    def offsets(self, own_rows, half_channels):
        chip = lax.axis_index("dp") // 2
        rows = [(chip ^ k) * 2 * own_rows for k in range(4)]
        columns = [(self.slot - d) % self.slots * half_channels for d in range(self.slots)]
        return jnp.stack(rows + columns).astype(jnp.int32)

    def unit(self, d, block):
        first, second = self.bits if d % 2 == 0 else self.bits[::-1]
        return across(block, first), across(block, second)

    def forward(self, d, one):
        return across(one, self.bits[1] if d % 2 == 0 else self.bits[0])

    def items(self, d, here, one, two, both):
        order = (here, one, two, both) if d % 2 == 0 else (here, two, one, both)
        return [(block, d, k) for k, block in enumerate(order)]

    def first_exchange(self, at, give):
        return across(give, self.bits[1 - at])

    def second_term(self, keep, came):
        return (keep[:, :, 1].astype(f32) + came[:, :, 1].astype(f32)).astype(bf16)

    def second_exchange(self, at, term):
        return across(term, self.bits[at])

    def slot_parts(self, keeps, cames, lasts, groups):
        own = {}
        for group, keep, came, last in zip(groups, keeps, cames, lasts):
            total = keep[:, :, 0].astype(f32) + came[:, :, 0].astype(f32) + last.astype(f32)
            for i, d in enumerate(group):
                own[d] = total[:, i]
        return own

    def slot_sum(self, keeps, cames, lasts, groups):
        own = self.slot_parts(keeps, cames, lasts, groups)
        return own[0], [around(own[d].astype(bf16), -d) for d in range(1, self.slots)]

    def to_owner(self, own, others):
        total = own
        for other in others:
            total = total + other.astype(f32)
        weights, rows, columns = total.shape
        total = total.reshape((weights, 2, rows // 2, columns))
        keep = lax.dynamic_index_in_dim(total, self.core, 1, keepdims=False)
        give = lax.dynamic_index_in_dim(total, 1 - self.core, 1, keepdims=False)
        out = self.ordered(0, keep, swap(give), 2)
        return out.reshape((weights, rows // 2, 2 * columns))

    def sum_chips(self, value):
        for bit in self.bits:
            value = value + across(value, bit)
        return value

    def sum_slots(self, value):
        total = value.astype(f32)
        for d in range(1, self.slots):
            total = total + around(value, d).astype(f32)
        return total


def on_device_general(
    x_in,
    segment_ids,
    norm_gain,
    w_x,
    w_z,
    w_bc,
    w_dt,
    conv_x,
    conv_x_bias,
    conv_bc,
    conv_bc_bias,
    dt_bias,
    a_log,
    d_skip,
    gate_gain,
    w_out,
    cotangent,
):
    place = Place()
    core, slots, slot = place.core, place.slots, place.slot
    length, features = x_in.shape
    sequences, whole_length = segment_ids.shape
    pieces = whole_length // length
    own_rows = w_x.shape[0]
    slot_channels = w_x.shape[1]
    slot_heads = w_dt.shape[1]
    half_channels = slot_channels // 2
    half_heads = slot_heads // 2
    channels = half_channels * slots
    heads = half_heads * slots
    all_channels = 2 * channels
    all_heads = 2 * heads
    bc_width = w_bc.shape[1]
    n_chunks = length // CH

    def split(weight):
        return weight.reshape((own_rows, 2, half_channels))

    stacked = jnp.stack([split(w_x), split(w_z), split(w_out.T)])
    mine = lax.dynamic_index_in_dim(stacked, core, 2, keepdims=False)
    other = swap(lax.dynamic_index_in_dim(stacked, 1 - core, 2, keepdims=False))
    wx = place.gather_weight(mine[0], other[0])
    dt_slots = place.gather_slots(w_dt).reshape((own_rows, all_heads))
    thin = jnp.concatenate([w_bc, dt_slots, norm_gain[:, None]], axis=1)
    thin = jnp.pad(thin, ((0, 0), (0, bc_width + 128 - thin.shape[1])))
    thin = place.ordered(0, thin, swap(thin), 0).reshape((2 * own_rows, -1))
    thin = place.gather_rows(thin, True)
    wz = place.gather_weight(mine[1], other[1])
    wo = place.gather_weight(mine[2], other[2])

    rows = jnp.concatenate(
        [
            conv_x,
            conv_x_bias[None],
            gate_gain[None],
            jnp.pad(jnp.concatenate([dt_bias, a_log, d_skip])[None], ((0, 0), (0, slot_channels - 3 * slot_heads))),
            jnp.zeros((1, slot_channels), f32),
        ],
        axis=0,
    )
    rows = place.gather_slots(rows)
    own = lax.dynamic_index_in_dim(
        rows.reshape((8, slots, 2, half_channels)), core, 2, keepdims=False
    ).reshape((8, channels))
    gain_row = own[5:6]
    lane = jnp.arange(128)
    head_at = lane % 32
    global_head = (head_at // half_heads) * slot_heads + core * half_heads + head_at % half_heads
    pick = ((lane[:, None] == global_head[None, :]) & (head_at < heads)[None, :]).astype(f32)
    small = rows[6, :, : 3 * slot_heads].reshape((slots, 3, slot_heads)).transpose(1, 0, 2)
    small = jnp.pad(small.reshape((3, all_heads)), ((0, 5), (0, 128 - all_heads)))
    small = exact(small, pick)
    bias_lanes = small[0]
    rate_lanes = jnp.where(head_at < heads, -jnp.exp(small[1]), 0.0)
    to_heads = head_map(channels, f32)
    skip_row = exact(small[2:3] * (lane < 32), to_heads.T)
    cw = jnp.concatenate([own[:5], skip_row, jnp.zeros((2, channels), f32)], axis=0)

    padded = jnp.pad(segment_ids, ((0, 0), (HALO, HALO)), constant_values=-1)
    ids_own = lax.dynamic_slice(
        padded, (slot // pieces, (slot % pieces) * length), (1, length + 2 * HALO)
    )
    ids_all = jnp.concatenate([ids_own, swap(ids_own)], axis=0)
    ids = ids_all[:, HALO : HALO + length]
    before = ids_all[:, HALO - 1]

    def near(k):
        return ids_all[:, HALO + k : HALO + k + length] == ids

    flags = [near(-1), near(-2), near(-3), ids, near(1), near(2), near(3), jnp.zeros_like(ids)]
    flags = jnp.stack([v.astype(f32) for v in flags], axis=-1)

    x_rows = jnp.concatenate([along_sequence(x_in[-HALO:], pieces, True), x_in], axis=0)
    tokens_ext = x_rows.astype(f32)
    inv_ext = lax.rsqrt(jnp.mean(tokens_ext * tokens_ext, axis=-1, keepdims=True) + epsilon)
    gain = thin[:, bc_width + all_heads].astype(f32)[None, :]
    normed_own = (tokens_ext * inv_ext * gain).astype(bf16)
    normed_other = swap(normed_own)
    normed_ext = jnp.concatenate([normed_own, normed_other], axis=0)
    normed = jnp.concatenate([normed_own[HALO:], normed_other[HALO:]], axis=0)
    tokens, inv_rms = tokens_ext[HALO:], inv_ext[HALO:]
    cot = jnp.concatenate([cotangent, swap(cotangent)], axis=0)

    dt_pick = jnp.dot(thin[:, bc_width:], pick.astype(bf16), preferred_element_type=f32).astype(bf16)
    thin_proj = mm(normed_ext, jnp.concatenate([thin[:, :bc_width], dt_pick], axis=1))
    thin_proj = thin_proj.reshape((2, HALO + length, -1))
    bc_ext = thin_proj[:, :, :bc_width]
    dt_in = thin_proj[:, HALO:, bc_width:] + bias_lanes
    x_ext = mm(normed_ext, wx).reshape((2, HALO + length, channels))

    bc_pre = conv_bc_bias + conv_bc[0] * bc_ext[:, HALO:]
    for k in range(1, conv_bc.shape[0]):
        shifted = bc_ext[:, HALO - k : HALO - k + length]
        bc_pre = bc_pre + conv_bc[k] * shifted * flags[:, :, k - 1 : k]
    bc_act = jax.nn.silu(bc_pre)
    bc_turned = bc_act.astype(bf16).transpose(0, 2, 1)
    c_low = bc_act[:, :, bc_width // 2 :].astype(bf16)

    step = jax.nn.softplus(dt_in)
    log_step = (step * rate_lanes).reshape((2 * n_chunks, CH, 128))
    tri = (jnp.arange(CH)[:, None] >= jnp.arange(CH)[None, :]).astype(f32)
    running = jnp.einsum("ts,csh->cth", tri, log_step, precision=highest)
    running = running.reshape((2, n_chunks, CH, 128))
    last = running[:, :, -1:, :]
    ids_chunks = ids.reshape((2, n_chunks, CH, 1))
    chunk_end = ids_chunks[:, :, -1:, :]
    chunk_before = jnp.concatenate(
        [before[:, None, None, None], chunk_end[:, :-1]], axis=1
    )
    still = (chunk_end == chunk_before).astype(f32)
    alpha = still * jnp.exp(last)
    lead = jnp.cumsum(last, axis=1) - last
    since_piece = (ids_chunks == before[:, None, None, None]).astype(f32) * jnp.exp(running + lead)
    since_piece = since_piece.reshape((2 * length, 128))
    group_lane = lane // 32
    hv = jnp.where(
        group_lane == 0,
        running * LOG2E,
        jnp.where(
            group_lane == 1,
            step.reshape((2, n_chunks, CH, 128)),
            jnp.where(
                group_lane == 2,
                (ids_chunks == chunk_before).astype(f32) * jnp.exp(running),
                (ids_chunks == chunk_end).astype(f32) * jnp.exp(last - running),
            ),
        ),
    ).reshape((2, length, 128))
    rv = jnp.concatenate(
        [
            hv[:, :, :24].transpose(0, 2, 1),
            ids.astype(f32)[:, None, :],
            jnp.zeros((2, 7, length), f32),
        ],
        axis=1,
    )
    first_lanes = (lane < 32).astype(f32)
    al = exact((alpha * first_lanes).reshape((2 * n_chunks, 128)), to_heads.T)
    al = al.reshape((2, n_chunks, channels))
    whole_alpha = jnp.prod(al, axis=1, keepdims=True)
    al = jnp.pad(al, ((0, 0), (0, 8 - n_chunks), (0, 0)))
    wide_since = mm((since_piece * first_lanes).astype(bf16), to_heads.T.astype(bf16))
    wide_since = wide_since.reshape((2, length, channels))

    def hand_on(local, forward):
        low = local.astype(bf16)
        for _ in range(pieces - 2):
            came = along_sequence(low, pieces, forward)
            low = (local + whole_alpha * came.astype(f32)).astype(bf16)
        return along_sequence(low, pieces, forward)

    y_here, states = scan_fwd(hv, flags, rv, al, bc_act, bc_turned, x_ext, cw, CH)
    state_in = hand_on(states[:, -1], True)
    y = y_here + wide_since * lax.dot_general(
        c_low, state_in, (((2,), (1,)), ((0,), (0,))), preferred_element_type=f32
    )

    gate_in = mm(normed, wz)
    mixed_grad = mm(cot, wo)
    y = y.reshape((2 * length, channels))
    sig = jax.nn.sigmoid(gate_in)
    act = gate_in * sig
    gated = y * act
    scaled = mixed_grad * gain_row
    sums = jnp.stack([jnp.sum(gated * gated, axis=1), jnp.sum(scaled * gated, axis=1)])
    sums = sums.reshape((2, 2, length))
    sums = (sums + swap(sums)[:, ::-1]).reshape((2, 2 * length))
    gate_rms = lax.rsqrt(sums[0] / all_channels + epsilon)[:, None]
    mixed = (gated * gate_rms * gain_row).astype(bf16)
    gate_gain_part = jnp.sum(mixed_grad * gated * gate_rms, axis=0)
    gated_grad = gate_rms * scaled - gated * gate_rms**3 * (sums[1] / all_channels)[:, None]
    y_grad = (gated_grad * act).reshape((2, length, channels))
    gate_grad = (gated_grad * y * sig * (1.0 + gate_in * (1.0 - sig))).astype(bf16)

    state_grad = lax.dot_general(
        c_low, (y_grad * wide_since).astype(bf16), (((1,), (1,)), ((0,), (0,))), preferred_element_type=f32
    )
    state_grad = hand_on(state_grad, False)
    wo_part = tmm(cot, mixed).astype(bf16)
    w_out_grad = place.scatter_weight(wo_part).T
    branch = mmt(mixed, wo)
    block_out = (tokens + branch[:length] + swap(branch[length:].astype(bf16)).astype(f32)).astype(bf16)
    wz_part = tmm(normed, gate_grad).astype(bf16)
    w_z_grad = place.scatter_weight(wz_part)

    x_low, tail, head, dbc, dcol, drow, dcw = scan_bwd(
        hv, flags, rv, al, bc_act, bc_turned, x_ext, cw, y_grad, states, state_in, state_grad, CH
    )

    head = along_sequence(head, pieces, False)

    def past_end(begin, taps):
        total = jnp.zeros((begin.shape[0], HALO, begin.shape[2]), f32)
        for k in range(1, taps.shape[0]):
            moved = jnp.pad(begin[:, :k], ((0, 0), (HALO - k, 0), (0, 0)))
            total = total + taps[k] * moved * flags[: begin.shape[0], length - HALO :, 3 + k : 4 + k]
        return total

    fixed = (tail + past_end(head, own[:4])).astype(bf16)
    x_low = lax.dynamic_update_slice(x_low, fixed, (0, length - HALO, 0)).reshape((2 * length, channels))

    bc_grad = dbc[0] + swap(dbc[1])
    pre = bc_pre[0]
    sig_bc = jax.nn.sigmoid(pre)
    bc_dpre = bc_grad * (sig_bc * (1.0 + pre * (1.0 - sig_bc)))
    bc_head = along_sequence(bc_dpre[:8], pieces, False)
    bc_raw = conv_bc[0] * bc_dpre
    bc_taps = [jnp.sum(bc_dpre * bc_ext[0, HALO:], axis=0)]
    longer = jnp.concatenate([bc_dpre, bc_head], axis=0)
    for k in range(1, conv_bc.shape[0]):
        bc_raw = bc_raw + conv_bc[k] * longer[k : k + length] * flags[0, :, 3 + k : 4 + k]
        shifted = bc_ext[0, HALO - k : HALO - k + length]
        bc_taps.append(jnp.sum(bc_dpre * shifted * flags[0, :, k - 1 : k], axis=0))
    bc_low = bc_raw.astype(bf16)
    bc_small = jnp.stack(bc_taps + [jnp.sum(bc_dpre, axis=0)] + [jnp.zeros((bc_width,), f32)] * 3)
    bc_small = place.sum_chips(bc_small + swap(bc_small))
    bc_small = place.sum_slots(bc_small)

    dcum = dcol[:, :, :128] - jnp.pad(drow.transpose(0, 2, 1), ((0, 0), (0, 0), (0, 96)))
    dlog = jnp.einsum("ts,csh->cth", tri.T, dcum.reshape((2 * n_chunks, CH, 128)), precision=highest)
    dstep = dcol[:, :, 128:] + dlog.reshape((2, length, 128)) * rate_lanes
    dt_raw = (dstep * jax.nn.sigmoid(dt_in)).reshape((2 * length, 128))
    rate_part = jnp.sum(dlog * log_step, axis=(0, 1))
    place_back = (pick * first_lanes).T.astype(bf16)
    dt_low = mm(dt_raw.astype(bf16), place_back).astype(bf16)

    dcw = jnp.sum(dcw, axis=0)
    head_rows = jnp.stack([jnp.sum(dt_raw, axis=0), rate_part]) * first_lanes
    head_rows = exact(head_rows, to_heads.T)
    packed = jnp.concatenate(
        [dcw[:5], gate_gain_part[None], dcw[5:6], head_rows, jnp.zeros((7, channels), f32)], axis=0
    )
    packed = place.sum_chips(packed).reshape((16, slots, half_channels))
    packed = place.scatter_slots(packed)
    packed = place.ordered(0, packed, swap(packed), 1).reshape((16, slot_channels))
    by_head = packed[6:9].reshape((3, slot_heads, 64))

    wx_part = tmm(normed, x_low).astype(bf16)
    w_x_grad = place.scatter_weight(wx_part)
    thin_low = jnp.concatenate(
        [jnp.concatenate([bc_low, jnp.zeros_like(bc_low)], axis=0), dt_low], axis=1
    )
    thin_part = tmm(normed, thin_low).astype(bf16)
    thin_grad = place.scatter_rows(thin_part, True, low_bit=0)
    thin_grad = place.sum_slots(thin_grad)
    w_bc_grad = thin_grad[:, :bc_width]
    w_dt_grad = lax.dynamic_slice_in_dim(thin_grad, bc_width + slot * slot_heads, slot_heads, 1)

    normed_grad = mmt(x_low, wx) + mmt(gate_grad, wz) + mmt(thin_low, thin)
    normed_grad = normed_grad[:length] + swap(normed_grad[length:].astype(bf16)).astype(f32)
    gain_part = jnp.sum(normed_grad * tokens * inv_rms, axis=0)
    pushed = normed_grad * gain
    x_grad = (
        cotangent.astype(f32)
        + inv_rms * pushed
        - tokens * inv_rms**3 * jnp.mean(pushed * tokens, axis=-1, keepdims=True)
    )
    gain_rows = gain_part.reshape((features // own_rows * 2, own_rows // 2))
    gain_rows = place.scatter_rows(gain_rows, True, low_bit=0)
    norm_gain_grad = place.sum_slots(gain_rows).reshape((own_rows,))
    return (
        block_out,
        x_grad,
        norm_gain_grad,
        w_x_grad,
        w_z_grad,
        w_bc_grad,
        w_dt_grad,
        packed[:4],
        packed[4],
        bc_small[:4],
        bc_small[4],
        by_head[1, :, 0],
        by_head[2, :, 0],
        jnp.sum(by_head[0], axis=1),
        packed[5],
        w_out_grad,
    )


def tie(*values):
    return lax.optimization_barrier(values)


def on_device(*args):
    if Place().fast(args[3].shape[1] // 2):
        return on_device_fast(*args)
    return on_device_general(*args)


def on_device_fast(
    x_in,
    segment_ids,
    norm_gain,
    w_x,
    w_z,
    w_bc,
    w_dt,
    conv_x,
    conv_x_bias,
    conv_bc,
    conv_bc_bias,
    dt_bias,
    a_log,
    d_skip,
    gate_gain,
    w_out,
    cotangent,
):
    place = Place()
    core, slots, slot = place.core, place.slots, place.slot
    length, features = x_in.shape
    sequences, whole_length = segment_ids.shape
    pieces = whole_length // length
    own_rows = w_x.shape[0]
    slot_channels = w_x.shape[1]
    slot_heads = w_dt.shape[1]
    half_channels = slot_channels // 2
    half_heads = slot_heads // 2
    channels = half_channels * slots
    heads = half_heads * slots
    all_channels = 2 * channels
    all_heads = 2 * heads
    bc_width = w_bc.shape[1]
    n_chunks = length // CH
    groups = [tuple(range(0, slots, 2)), tuple(range(1, slots, 2))]
    at = place.offsets(own_rows, half_channels)

    def split(weight):
        return weight.reshape((own_rows, 2, half_channels))

    stacked = jnp.stack([split(w_x), split(w_z), split(w_out.T)])
    mine = lax.dynamic_index_in_dim(stacked, core, 2, keepdims=False)
    other = swap(lax.dynamic_index_in_dim(stacked, 1 - core, 2, keepdims=False))
    both = place.ordered(0, mine, other, 1).reshape((3, 2 * own_rows, half_channels))
    padded = jnp.pad(segment_ids, ((0, 0), (HALO, HALO)), constant_values=-1)
    ids_own = lax.dynamic_slice(
        padded, (slot // pieces, (slot % pieces) * length), (1, length + 2 * HALO)
    )
    ids_all = jnp.concatenate([ids_own, swap(ids_own)], axis=0).astype(f32)
    both, ids_all, conv_x, conv_x_bias, gate_gain, dt_bias, a_log, d_skip, w_dt, w_bc, norm_gain, x_in, cotangent = tie(
        both, ids_all, conv_x, conv_x_bias, gate_gain, dt_bias, a_log, d_skip, w_dt, w_bc, norm_gain, x_in, cotangent)

    rows = jnp.concatenate(
        [
            conv_x,
            conv_x_bias[None],
            gate_gain[None],
            jnp.pad(
                jnp.concatenate([dt_bias, a_log, d_skip])[None], ((0, 0), (0, slot_channels - 3 * slot_heads))
            ),
            jnp.zeros((1, slot_channels), f32),
            jnp.pad(w_dt.T.astype(f32), ((0, 0), (0, slot_channels - own_rows))),
        ],
        axis=0,
    )
    rows = place.gather_slots(rows)
    halo = along_sequence(x_in[-HALO:], pieces, True)
    wx_here = [both[:1]] + [around(both[:1], d) for d in range(1, slots)]
    wx_one, wx_two = {}, {}
    wx_one[0], wx_two[0] = place.unit(0, wx_here[0])
    cot_turned_own = turn(cotangent)
    rows, halo, wx_here[slots - 1], wx_one, wx_two, cot_turned_own, w_bc, norm_gain = tie(
        rows, halo, wx_here[slots - 1], wx_one, wx_two, cot_turned_own, w_bc, norm_gain)
    dt_slots = rows[8:, :, :own_rows].transpose(2, 1, 0).reshape((own_rows, all_heads)).astype(bf16)
    thin = jnp.concatenate([w_bc, dt_slots, norm_gain[:, None]], axis=1)
    thin = jnp.pad(thin, ((0, 0), (0, bc_width + 128 - thin.shape[1])))
    thin = place.ordered(0, thin, swap(thin), 0)
    low, high = place.bits
    thin = place.ordered(low, thin, across(thin, low), 0)
    odd = slots - 1
    wx_one[odd] = across(wx_here[odd], high)
    thin, wx_here[odd], wx_here[1], wx_one, cot_turned_own, cotangent = tie(
        thin, wx_here[odd], wx_here[1], wx_one, cot_turned_own, cotangent)
    thin = place.ordered(high, thin, across(thin, high), 0).reshape((features, -1))
    wx_two[odd] = across(wx_here[odd], low)
    gain = thin[:, bc_width + all_heads].astype(f32)[None, :]
    thin, gain, wx_here, wx_two, both, cot_turned_own, cotangent = tie(
        thin, gain, wx_here, wx_two, both, cot_turned_own, cotangent)
    pair_here = {0: both[1:], 1: around(both[1:], 1)}
    normed_own, normed_turned_own = norm(x_in, halo, gain)
    normed_both = [normed_own, swap(normed_own)]
    for d in range(1, slots - 1):
        wx_one[d], wx_two[d] = place.unit(d, wx_here[d])

    thin, gain, normed_both, normed_turned_own, pair_here, rows, ids_all, wx_here, wx_one, wx_two = tie(
        thin, gain, normed_both, normed_turned_own, pair_here, rows, ids_all, wx_here, wx_one, wx_two)
    normed_turned = [normed_turned_own, swap(normed_turned_own)]
    cot = [cotangent, swap(cotangent)]
    cot_turned = [cot_turned_own, swap(cot_turned_own)]

    pair_here[2] = around(pair_here[0], 2)
    one, two, both_k = {}, {}, {}
    one[0], two[0] = place.unit(0, pair_here[0])
    own = lax.dynamic_index_in_dim(
        rows[:8].reshape((8, slots, 2, half_channels)), core, 2, keepdims=False
    ).reshape((8, channels))
    gain_row = own[5:6]
    lane = jnp.arange(128)
    head_at = lane % 32
    global_head = (head_at // half_heads) * slot_heads + core * half_heads + head_at % half_heads
    pick = ((lane[:, None] == global_head[None, :]) & (head_at < heads)[None, :]).astype(f32)
    first_lanes = (lane < 32).astype(f32)
    small = rows[6, :, : 3 * slot_heads].reshape((slots, 3, slot_heads)).transpose(1, 0, 2)
    small = jnp.pad(small.reshape((3, all_heads)), ((0, 5), (0, 128 - all_heads)))
    small = exact(small, pick)
    bias_lanes = small[0]
    rate_lanes = jnp.where(head_at < heads, -jnp.exp(small[1]), 0.0)
    to_heads = head_map(channels, f32)
    skip_row = exact(small[2:3] * first_lanes, to_heads.T)
    cw = jnp.concatenate([own[:5], skip_row, jnp.zeros((2, channels), f32)], axis=0)
    lanes = jnp.concatenate([bias_lanes[None], rate_lanes[None], jnp.zeros((6, 128), f32)], axis=0)
    cbc = jnp.concatenate([conv_bc, conv_bc_bias[None], jnp.zeros((3, bc_width), f32)], axis=0)
    wide_ids = jnp.pad(ids_all, ((0, 0), (0, -ids_all.shape[1] % 128)))
    wide_ids = jnp.broadcast_to(wide_ids[:, None, :], (2, 8, wide_ids.shape[1]))
    ids_rows = jnp.broadcast_to(ids_all[:, None, HALO : HALO + length], (2, 8, length))
    tri = (jnp.arange(CH)[:, None] >= jnp.arange(CH)[None, :]).astype(f32)

    bc_ext, bc_pre, bc_act, bc_turned, c_low, dt_in, log_step, hv, rv, al, wide_since, flags = prepare(
        normed_both[0], normed_both[1], thin, pick.astype(bf16), lanes, cbc, wide_ids, ids_rows, channels)
    whole_alpha = jnp.prod(al[:, :n_chunks], axis=1, keepdims=True)
    log_step = log_step.reshape((2 * n_chunks, CH, 128))
    wx_both = {d: place.forward(d, wx_one[d]) for d in range(slots)}

    def hand_on(local, forward):
        low = local.astype(bf16)
        for _ in range(pieces - 2):
            came = along_sequence(low, pieces, forward)
            low = (local + whole_alpha * came.astype(f32)).astype(bf16)
        return along_sequence(low, pieces, forward)

    (one, two, pair_here, wx_here, wx_one, wx_two, wx_both, normed_both, hv, rv, al, bc_act, bc_turned, cw, wide_since, c_low, flags, bc_ext, bc_pre,
     dt_in, log_step) = tie(
        one, two, pair_here, wx_here, wx_one, wx_two, wx_both, normed_both, hv, rv, al, bc_act, bc_turned, cw, wide_since, c_low, flags,
        bc_ext, bc_pre, dt_in, log_step)
    wx_items = []
    for d in range(slots):
        wx_items += place.items(d, wx_here[d], wx_one[d], wx_two[d], wx_both[d])

    pair_here[3] = around(pair_here[0], 3)
    both_k[0] = place.forward(0, one[0])
    one[1], two[1] = place.unit(1, pair_here[1])
    one[2] = across(pair_here[2], place.bits[0])
    x_ext, wx = project(normed_both, 0, at, wx_items, 0, channels)
    x_ext = x_ext.reshape((2, HALO + length, channels))

    x_ext, one, two, both_k, pair_here = tie(x_ext, one, two, both_k, pair_here)
    one[3], two[3] = place.unit(3, pair_here[3])
    two[2] = across(pair_here[2], place.bits[1])
    both_k[1] = place.forward(1, one[1])
    y_here, states = scan_fwd(hv, flags, rv, al, bc_act, bc_turned, x_ext, cw, CH)

    y_here, states, one, two, both_k = tie(y_here, states, one, two, both_k)
    state_in = hand_on(states[:, -1], True)
    both_k[2], both_k[3] = place.forward(2, one[2]), place.forward(3, one[3])
    pair_items = []
    for d in range(slots):
        pair_items += place.items(d, pair_here[d], one[d], two[d], both_k[d])
    tokens = x_in.astype(f32)

    gate_in, wz = project(normed_both, HALO, at, pair_items, 0, channels)
    mixed_grad, wo = project(cot, 0, at, pair_items, 1, channels)
    flat = lambda v: v.reshape((2 * length, -1))
    y, sums = gate_sums(flat(y_here), flat(wide_since), flat(c_low), state_in, gate_in, mixed_grad, gain_row)
    mixed, gate_grad, y_grad, gain_grad, state_grad = gate_grads(
        y, flat(wide_since), flat(c_low), gate_in, mixed_grad, gain_row, sums, swap(sums), all_channels)
    y_grad = y_grad.reshape((2, length, channels))
    state_grad = hand_on(state_grad, False)
    parts = [
        weight_parts(at, [normed_turned, cot_turned], [[gate_grad], [mixed]], group, own_rows, half_channels, flip)
        for flip, group in enumerate(groups)
    ]
    parts, y_grad, mixed, gate_grad, state_grad = tie(parts, y_grad, mixed, gate_grad, state_grad)
    pair_came = [place.first_exchange(i, parts[i][1]) for i in range(2)]


    def backward(piece):
        return scan_bwd(
            hv, flags, rv, al, bc_act, bc_turned, x_ext, cw, y_grad, states, state_in, state_grad, CH, piece, 1
        )

    back_other = backward(1)
    dbc_other = swap(back_other[3][0])
    head_other = along_sequence(back_other[2], pieces, False)
    back_other, y_grad = tie(back_other, y_grad)
    back_own = backward(0)
    pair_came, back_own, dbc_other, head_other = tie(pair_came, back_own, dbc_other, head_other)
    terms = [place.second_term(parts[i][0], pair_came[i]) for i in range(2)]
    pair_last = [place.second_exchange(i, terms[i]) for i in range(2)]

    head = jnp.concatenate([along_sequence(back_own[2], pieces, False), head_other])
    place_back = (pick * first_lanes).T.astype(bf16)
    bc_dpre, dt_low, bc_small, packed = small_grads(
        back_own[3], dbc_other, bc_pre, bc_ext, flags, back_own[4], back_other[4], back_own[5], back_other[5],
        log_step.reshape((2, length, 128)), dt_in, lanes, place_back, back_own[6], back_other[6], gain_grad)

    def past_end(begin, taps):
        total = jnp.zeros((begin.shape[0], HALO, begin.shape[2]), f32)
        for k in range(1, taps.shape[0]):
            moved = jnp.pad(begin[:, :k], ((0, 0), (HALO - k, 0), (0, 0)))
            total = total + taps[k] * moved * flags[: begin.shape[0], length - HALO :, 3 + k : 4 + k]
        return total

    fix = past_end(head, own[:4])
    x_low = [
        lax.dynamic_update_slice(back[0][0], (back[1][0] + fix[i]).astype(bf16), (length - HALO, 0))
        for i, back in enumerate((back_own, back_other))
    ]
    x_low, bc_dpre, dt_low, bc_small, packed = tie(x_low, bc_dpre, dt_low, bc_small, packed)
    bc_head = along_sequence(bc_dpre[:8], pieces, False)
    x_parts = [
        weight_parts(at, [normed_turned], [x_low], group, own_rows, half_channels, flip)
        for flip, group in enumerate(groups)
    ]
    x_parts, x_low, pair_last, bc_head, bc_dpre, dt_low = tie(x_parts, x_low, pair_last, bc_head, bc_dpre, dt_low)
    x_came = [place.first_exchange(i, x_parts[i][1]) for i in range(2)]
    pair_sums = place.slot_parts([p[0] for p in parts], pair_came, pair_last, groups)
    pair_others = {d: around(pair_sums[d].astype(bf16), -d) for d in range(1, slots - 1)}
    normed_grad, normed_grad_other, thin_part = normed_grads(
        bc_dpre, bc_head, flags, cbc, dt_low, normed_turned, x_low, gate_grad, wx, wz, thin)

    x_came, thin_part, pair_others, pair_sums, normed_grad, normed_grad_other, packed, bc_small = tie(
        x_came, thin_part, pair_others, pair_sums, normed_grad, normed_grad_other, packed, bc_small)
    x_terms = [place.second_term(x_parts[i][0], x_came[i]) for i in range(2)]
    x_last = [place.second_exchange(i, x_terms[i]) for i in range(2)]
    pair_others[slots - 1] = around(pair_sums[slots - 1].astype(bf16), 1)
    thin_part = place.ordered_sum(thin_part)
    x_grad, gain_part = x_grads(normed_grad, swap(normed_grad_other), x_in, cotangent, gain)
    gain_part = jnp.sum(gain_part, axis=0).reshape((-1, bc_width))
    gain_rows = gain_part.shape[0]
    bc_small = jnp.concatenate([bc_small[:5], gain_part, jnp.zeros((11 - gain_rows, bc_width), f32)], axis=0)
    bc_small = bc_small + swap(bc_small)
    packed = jnp.concatenate([packed, bc_small], axis=1)
    low, high = place.bits
    packed = packed + across(packed, low)
    thin_part = place.half_rows(thin_part, low)

    x_last, packed, thin_part, x_grad, pair_sums, pair_others = tie(
        x_last, packed, thin_part, x_grad, pair_sums, pair_others)
    x_sums = place.slot_parts([p[0] for p in x_parts], x_came, x_last, groups)
    x_others = [around(x_sums[1].astype(bf16), -1)]
    packed = packed + across(packed, high)
    thin_grad = place.half_rows(thin_part, high)
    packed, thin_grad, x_others, x_sums, pair_sums, pair_others, mixed = tie(
        packed, thin_grad, x_others, x_sums, pair_sums, pair_others, mixed)

    bc_small = packed[:, channels:]
    packed = packed[:, :channels].reshape((16, slots, half_channels))

    def block(index):
        return lax.dynamic_index_in_dim(packed, index % slots, 1, keepdims=False)

    own_sums = jnp.concatenate([block(slot), bc_small], axis=1)
    for d in range(1, slots):
        own_sums = own_sums + around(jnp.concatenate([block(slot + d), bc_small], axis=1), d)
    branch, branch_other = branch_parts(mixed, wo)
    x_others += [around(x_sums[d].astype(bf16), -d) for d in range(2, slots)]
    branch, branch_other, x_others, own_sums, thin_grad = tie(branch, branch_other, x_others, own_sums, thin_grad)
    thin_grad = place.sum_slots(thin_grad)
    pair_grads = place.to_owner(pair_sums[0], list(pair_others.values()))
    block_out = (tokens + branch + swap(branch_other).astype(f32)).astype(bf16)
    packed = own_sums[:, :half_channels]
    bc_small = own_sums[:, half_channels:]
    packed = place.ordered(0, packed, swap(packed), 1).reshape((16, slot_channels))
    by_head = packed[6:9].reshape((3, slot_heads, 64))
    norm_gain_grad = lax.dynamic_slice_in_dim(
        bc_small[5 : 5 + gain_rows].reshape((features,)), lax.axis_index("dp") * own_rows, own_rows, 0)
    w_z_grad, w_out_grad = pair_grads
    w_bc_grad = thin_grad[:, :bc_width]
    w_dt_grad = lax.dynamic_slice_in_dim(thin_grad, bc_width + slot * slot_heads, slot_heads, 1)
    w_x_grad = place.to_owner(x_sums[0], x_others)[0]
    return (
        block_out,
        x_grad,
        norm_gain_grad,
        w_x_grad,
        w_z_grad,
        w_bc_grad,
        w_dt_grad,
        packed[:4],
        packed[4],
        bc_small[:4],
        bc_small[4],
        by_head[1, :, 0],
        by_head[2, :, 0],
        jnp.sum(by_head[0], axis=1),
        packed[5],
        w_out_grad.T,
    )


def solution(mesh):
    rows = P(("dp", "tensor"), None)
    both = P("dp", "tensor")
    heads = P("tensor")
    in_specs = (
        rows, P("dp", None), P("dp"), both, both, P("dp", None), both, P(None, "tensor"), heads,
        P(), P(), heads, heads, heads, heads, P("tensor", "dp"), rows,
    )
    out_specs = (
        rows, rows, P("dp"), both, both, P("dp", None), both, P(None, "tensor"), heads,
        P(), P(), heads, heads, heads, heads, P("tensor", "dp"),
    )
    return jax.shard_map(
        on_device, mesh=mesh, in_specs=in_specs, out_specs=out_specs, check_vma=False
    )
```

```python
import jax
import jax.numpy as jnp
from jax import lax
from jax.experimental import pallas as pl
from jax.experimental.pallas import tpu as pltpu
from jax.sharding import PartitionSpec as P

CH = 256
HALO = 16
GROUP = 4
LOG2E = 1.4426950408889634
epsilon = 1e-05
f32 = jnp.float32
bf16 = jnp.bfloat16
highest = lax.Precision.HIGHEST


def mm(a, b):
    return lax.dot_general(a, b, (((1,), (0,)), ((), ())), preferred_element_type=f32)


def mmt(a, b):
    return lax.dot_general(a, b, (((1,), (1,)), ((), ())), preferred_element_type=f32)


def tmm(a, b):
    return lax.dot_general(a, b, (((0,), (0,)), ((), ())), preferred_element_type=f32)


def exact(a, b):
    return lax.dot_general(
        a, b, (((1,), (0,)), ((), ())), precision=highest, preferred_element_type=f32
    )


def head_map(channels, kind):
    return (jnp.arange(channels)[:, None] // 64 == jnp.arange(128)[None, :]).astype(kind)


def spread(cols, first, rows, lane_low):
    parts = []
    for pair in range(GROUP // 2):
        left = jnp.broadcast_to(cols[:, first + 2 * pair : first + 2 * pair + 1], (rows, 128))
        right = jnp.broadcast_to(cols[:, first + 2 * pair + 1 : first + 2 * pair + 2], (rows, 128))
        parts.append(jnp.where(lane_low, left, right))
    return jnp.concatenate(parts, axis=1)


def conv_pre(x_ref, cw_ref, flags, start, rows):
    pre = cw_ref[4:5, :] + cw_ref[0:1, :] * x_ref[0, HALO + start : HALO + start + rows, :]
    for k in range(1, 4):
        shifted = x_ref[0, HALO + start - k : HALO + start - k + rows, :]
        pre = pre + (cw_ref[k : k + 1, :] * shifted) * flags[:, k - 1 : k]
    return pre


def masked_scores(cb_ref, bc_ref, fl_ref, rv_ref, n_chunks, rows):
    for c in range(n_chunks):
        at = slice(c * rows, (c + 1) * rows)
        ids_col = fl_ref[0, at, 3:4]
        ids_row = rv_ref[0, 24:25, at]
        t_at = lax.broadcasted_iota(jnp.int32, (rows, rows), 0)
        s_at = lax.broadcasted_iota(jnp.int32, (rows, rows), 1)
        keep = (ids_col == ids_row) & (t_at >= s_at)
        scores = lax.dot_general(
            bc_ref[0, at, 128:], bc_ref[0, at, :128], (((1,), (1,)), ((), ())),
            precision=highest, preferred_element_type=f32,
        )
        cb_ref[c] = jnp.where(keep, scores, 0.0)


def scan_fwd_body(n_chunks, rows, hv_ref, fl_ref, rv_ref, al_ref, bc_ref, bt_ref, x_ref, cw_ref, y_ref, st_ref, cb_ref):
    group = pl.program_id(1)
    turn = lax.rem(128 - GROUP * group, 128)

    @pl.when(group == 0)
    def _():
        masked_scores(cb_ref, bc_ref, fl_ref, rv_ref, n_chunks, rows)

    lane_low = lax.broadcasted_iota(jnp.int32, (rows, 128), 1) < 64
    state = jnp.zeros((128, GROUP * 64), f32)
    for c in range(n_chunks):
        at = slice(c * rows, (c + 1) * rows)
        cols = pltpu.roll(hv_ref[0, at, :], turn, 1)
        flags = fl_ref[0, at, :]
        pre = conv_pre(x_ref, cw_ref, flags, c * rows, rows)
        act = pre * jax.nn.sigmoid(pre)
        u = act * spread(cols, 32, rows, lane_low)
        ub = u.astype(bf16)
        y = cw_ref[5:6, :] * act
        if c > 0:
            c_rows = bc_ref[0, at, 128:].astype(bf16)
            y = y + mm(c_rows, state.astype(bf16)) * spread(cols, 64, rows, lane_low)
        scores = cb_ref[c]
        parts = []
        for pair in range(GROUP // 2):
            u_pair = ub[:, 128 * pair : 128 * pair + 128]
            outs = []
            for j in (2 * pair, 2 * pair + 1):
                gap = cols[:, j : j + 1] - rv_ref[0, pl.ds(group * GROUP + j, 1), at]
                mix = (scores * jnp.exp2(jnp.minimum(gap, 0.0))).astype(bf16)
                outs.append(mm(mix, u_pair))
            parts.append(jnp.where(lane_low, outs[0], outs[1]))
        y_ref[0, at, :] = y + jnp.concatenate(parts, axis=1)
        wu = (u * spread(cols, 96, rows, lane_low)).astype(bf16)
        state = al_ref[0, c : c + 1, :] * state + mm(bt_ref[0, :128, at], wu)
        st_ref[0, c] = state


def scan_fwd(hv, fl, rv, al, bc, bt, x_ext, cw, rows, first=0, count=2):
    length = hv.shape[1]
    n_chunks = length // rows
    width = GROUP * 64
    channels = x_ext.shape[2]
    groups = channels // width
    return pl.pallas_call(
        lambda *refs: scan_fwd_body(n_chunks, rows, *refs),
        grid=(count, groups),
        in_specs=[
            pl.BlockSpec((1, length, 128), lambda s, g: (first + s, 0, 0)),
            pl.BlockSpec((1, length, 8), lambda s, g: (first + s, 0, 0)),
            pl.BlockSpec((1, 32, length), lambda s, g: (first + s, 0, 0)),
            pl.BlockSpec((1, 8, width), lambda s, g: (first + s, 0, g)),
            pl.BlockSpec((1, length, 256), lambda s, g: (first + s, 0, 0)),
            pl.BlockSpec((1, 256, length), lambda s, g: (first + s, 0, 0)),
            pl.BlockSpec((1, HALO + length, width), lambda s, g: (first + s, 0, g)),
            pl.BlockSpec((8, width), lambda s, g: (0, g)),
        ],
        out_specs=[
            pl.BlockSpec((1, length, width), lambda s, g: (s, 0, g)),
            pl.BlockSpec((1, n_chunks, 128, width), lambda s, g: (s, 0, 0, g)),
        ],
        out_shape=[
            jax.ShapeDtypeStruct((count, length, channels), f32),
            jax.ShapeDtypeStruct((count, n_chunks, 128, channels), f32),
        ],
        scratch_shapes=[pltpu.VMEM((n_chunks, rows, rows), f32)],
        cost_estimate=pl.CostEstimate(
            flops=count * groups * GROUP * length * (rows + 256) * 128 * 2,
            transcendentals=count * groups * GROUP * length * rows,
            bytes_accessed=count * length * channels * 8,
        ),
        name="scan_fwd",
    )(hv, fl, rv, al, bc, bt, x_ext, cw)


def scan_bwd_body(
    n_chunks, rows, hv_ref, fl_ref, rv_ref, al_ref, bc_ref, bt_ref, x_ref, cw_ref, dy_ref, st_ref, sr_ref, rr_ref, seg_ref,
    xl_ref, tail_ref, head_ref, dbc_ref, dcol_ref, drow_ref, dcw_ref, cb_ref, dcb_ref, dpre_ref,
):
    group = pl.program_id(1)
    turn = lax.rem(128 - GROUP * group, 128)
    length = n_chunks * rows
    width = GROUP * 64

    @pl.when(group == 0)
    def _():
        masked_scores(cb_ref, bc_ref, fl_ref, rv_ref, n_chunks, rows)
        dcb_ref[...] = jnp.zeros_like(dcb_ref)
        dbc_ref[...] = jnp.zeros_like(dbc_ref)
        dcol_ref[...] = jnp.zeros_like(dcol_ref)
        drow_ref[...] = jnp.zeros_like(drow_ref)

    lane_low = lax.broadcasted_iota(jnp.int32, (rows, 128), 1) < 64
    lane = lax.broadcasted_iota(jnp.int32, (rows, 128), 1)
    row_at = lax.broadcasted_iota(jnp.int32, (rows, width), 0)
    grad_state = rr_ref[0].astype(f32)
    recv = sr_ref[0].astype(f32)
    states = [recv]
    carry = recv
    for c in range(n_chunks - 1):
        carry = al_ref[0, c : c + 1, :] * carry
        states.append(st_ref[0, c] + carry)
    tap_sums = [jnp.zeros((1, width), f32) for _ in range(6)]
    dpre_ref[length : length + 8, :] = jnp.zeros((8, width), f32)
    for c in reversed(range(n_chunks)):
        at = slice(c * rows, (c + 1) * rows)
        cols = pltpu.roll(hv_ref[0, at, :], turn, 1)
        flags = fl_ref[0, at, :]
        pre = conv_pre(x_ref, cw_ref, flags, c * rows, rows)
        sig = jax.nn.sigmoid(pre)
        act = pre * sig
        step_wide = spread(cols, 32, rows, lane_low)
        end_wide = spread(cols, 96, rows, lane_low)
        u = act * step_wide
        ub = u.astype(bf16)
        dy = dy_ref[0, at, :]
        dyb = dy.astype(bf16)
        b_rows = bc_ref[0, at, :128].astype(bf16)
        c_rows = bc_ref[0, at, 128:].astype(bf16)
        state_b = states[c].astype(bf16)
        dye = dy * spread(cols, 64, rows, lane_low)
        dyeb = dye.astype(bf16)
        gs_b = grad_state.astype(bf16)
        wub = (u * end_wide).astype(bf16)
        dbc_ref[0, at, 128:] += mmt(dyeb, state_b)
        dbc_ref[0, at, :128] += mmt(wub, gs_b)
        du_state = mm(b_rows, gs_b) * end_wide
        u_du = u * du_state
        at_end = jnp.sum(u_du, axis=0, keepdims=True) + al_ref[0, c : c + 1, :] * jnp.sum(
            grad_state * states[c], axis=0, keepdims=True
        )
        log_grad = dye * mm(c_rows, state_b) - u_du
        log_grad = jnp.where(row_at == rows - 1, log_grad + at_end, log_grad)
        grad_state = al_ref[0, c : c + 1, :] * grad_state + mm(bt_ref[0, 128:, at], dyeb)
        scores = cb_ref[c]
        dcb = dcb_ref[c]
        parts = []
        row_sums = jnp.zeros((rows, 128), f32)
        for pair in range(GROUP // 2):
            lanes = slice(128 * pair, 128 * pair + 128)
            u_pair = ub[:, lanes]
            dy_pair = dyb[:, lanes]
            outs = []
            for j in (2 * pair, 2 * pair + 1):
                gap = cols[:, j : j + 1] - rv_ref[0, pl.ds(group * GROUP + j, 1), at]
                decay = jnp.exp2(jnp.minimum(gap, 0.0))
                mix = (scores * decay).astype(bf16)
                own = lane_low if j % 2 == 0 else jnp.logical_not(lane_low)
                prod = mmt(jnp.where(own, dy_pair, jnp.zeros_like(dy_pair)), u_pair) * decay
                dcb = dcb + prod
                full = prod * scores
                row_sums = jnp.where(
                    lane == group * GROUP + j, jnp.sum(full, axis=1, keepdims=True), row_sums
                )
                drow_ref[0, pl.ds(group * GROUP + j, 1), at] = jnp.sum(full, axis=0, keepdims=True)
                outs.append(tmm(mix, dy_pair))
            parts.append(jnp.where(lane_low, outs[0], outs[1]))
        dcb_ref[c] = dcb
        du = jnp.concatenate(parts, axis=1) + du_state
        seg = seg_ref[...]
        dcol_ref[0, at, :128] += row_sums + lax.dot_general(
            log_grad, seg, (((1,), (0,)), ((), ())), precision=highest, preferred_element_type=f32
        )
        dcol_ref[0, at, 128:] += lax.dot_general(
            du * act, seg, (((1,), (0,)), ((), ())), precision=highest, preferred_element_type=f32
        )
        dact = du * step_wide + cw_ref[5:6, :] * dy
        dpre = dact * (sig * (1.0 + pre * (1.0 - sig)))
        dpre_ref[at, :] = dpre
        tap_sums[0] += jnp.sum(dpre * x_ref[0, HALO + c * rows : HALO + (c + 1) * rows, :], axis=0, keepdims=True)
        for k in range(1, 4):
            shifted = x_ref[0, HALO + c * rows - k : HALO + (c + 1) * rows - k, :]
            tap_sums[k] += jnp.sum(dpre * flags[:, k - 1 : k] * shifted, axis=0, keepdims=True)
        tap_sums[4] += jnp.sum(dpre, axis=0, keepdims=True)
        tap_sums[5] += jnp.sum(dy * act, axis=0, keepdims=True)
        xg = cw_ref[0:1, :] * dpre
        for k in range(1, 4):
            xg = xg + (cw_ref[k : k + 1, :] * dpre_ref[c * rows + k : (c + 1) * rows + k, :]) * flags[:, 3 + k : 4 + k]
        xl_ref[0, at, :] = xg.astype(bf16)
        if c == n_chunks - 1:
            tail_ref[0] = xg[rows - 16 :, :]
        if c == 0:
            head_ref[0] = dpre[:8, :]
    dcw_ref[0] = jnp.concatenate(tap_sums + [jnp.zeros((2, width), f32)], axis=0)

    @pl.when(group == pl.num_programs(1) - 1)
    def _():
        for c in range(n_chunks):
            at = slice(c * rows, (c + 1) * rows)
            ids_col = fl_ref[0, at, 3:4]
            ids_row = rv_ref[0, 24:25, at]
            t_at = lax.broadcasted_iota(jnp.int32, (rows, rows), 0)
            s_at = lax.broadcasted_iota(jnp.int32, (rows, rows), 1)
            keep = (ids_col == ids_row) & (t_at >= s_at)
            grad = jnp.where(keep, dcb_ref[c], 0.0).astype(bf16)
            dbc_ref[0, at, 128:] += mm(grad, bc_ref[0, at, :128].astype(bf16))
            dbc_ref[0, at, :128] += tmm(grad, bc_ref[0, at, 128:].astype(bf16))


def scan_bwd(hv, fl, rv, al, bc, bt, x_ext, cw, dy, states, s_recv, r_recv, rows, first=0, count=2):
    length = hv.shape[1]
    n_chunks = length // rows
    width = GROUP * 64
    channels = x_ext.shape[2]
    groups = channels // width
    seg = head_map(channels, f32)
    return pl.pallas_call(
        lambda *refs: scan_bwd_body(n_chunks, rows, *refs),
        grid=(count, groups),
        in_specs=[
            pl.BlockSpec((1, length, 128), lambda s, g: (first + s, 0, 0)),
            pl.BlockSpec((1, length, 8), lambda s, g: (first + s, 0, 0)),
            pl.BlockSpec((1, 32, length), lambda s, g: (first + s, 0, 0)),
            pl.BlockSpec((1, 8, width), lambda s, g: (first + s, 0, g)),
            pl.BlockSpec((1, length, 256), lambda s, g: (first + s, 0, 0)),
            pl.BlockSpec((1, 256, length), lambda s, g: (first + s, 0, 0)),
            pl.BlockSpec((1, HALO + length, width), lambda s, g: (first + s, 0, g)),
            pl.BlockSpec((8, width), lambda s, g: (0, g)),
            pl.BlockSpec((1, length, width), lambda s, g: (first + s, 0, g)),
            pl.BlockSpec((1, n_chunks, 128, width), lambda s, g: (first + s, 0, 0, g)),
            pl.BlockSpec((1, 128, width), lambda s, g: (first + s, 0, g)),
            pl.BlockSpec((1, 128, width), lambda s, g: (first + s, 0, g)),
            pl.BlockSpec((width, 128), lambda s, g: (g, 0)),
        ],
        out_specs=[
            pl.BlockSpec((1, length, width), lambda s, g: (s, 0, g)),
            pl.BlockSpec((1, 16, width), lambda s, g: (s, 0, g)),
            pl.BlockSpec((1, 8, width), lambda s, g: (s, 0, g)),
            pl.BlockSpec((1, length, 256), lambda s, g: (s, 0, 0)),
            pl.BlockSpec((1, length, 256), lambda s, g: (s, 0, 0)),
            pl.BlockSpec((1, 32, length), lambda s, g: (s, 0, 0)),
            pl.BlockSpec((1, 8, width), lambda s, g: (s, 0, g)),
        ],
        out_shape=[
            jax.ShapeDtypeStruct((count, length, channels), bf16),
            jax.ShapeDtypeStruct((count, 16, channels), f32),
            jax.ShapeDtypeStruct((count, 8, channels), f32),
            jax.ShapeDtypeStruct((count, length, 256), f32),
            jax.ShapeDtypeStruct((count, length, 256), f32),
            jax.ShapeDtypeStruct((count, 32, length), f32),
            jax.ShapeDtypeStruct((count, 8, channels), f32),
        ],
        scratch_shapes=[
            pltpu.VMEM((n_chunks, rows, rows), f32),
            pltpu.VMEM((n_chunks, rows, rows), f32),
            pltpu.VMEM((length + 8, width), f32),
        ],
        cost_estimate=pl.CostEstimate(
            flops=count * groups * GROUP * length * (rows + 256) * 128 * 6,
            transcendentals=count * groups * GROUP * length * rows,
            bytes_accessed=count * length * channels * 12,
        ),
        name="scan_bwd",
    )(hv, fl, rv, al, bc, bt, x_ext, cw, dy, states, s_recv, r_recv, seg)


def project_body(places, skip, at_ref, *refs):
    left_ref, right_ref, blocks, out_ref, full_ref = refs[0], refs[1], refs[2:-2], refs[-2], refs[-1]

    @pl.when(pl.program_id(0) == 0)
    def _():
        for ref, (d, k) in zip(blocks, places):
            rows, columns = ref.shape[1:]
            row = pl.multiple_of(at_ref[k], rows)
            column = pl.multiple_of(at_ref[4 + d], columns)
            full_ref[pl.ds(row, rows), pl.ds(column, columns)] = ref[0]
        out_ref[...] = mm(left_ref[skip:, :], full_ref[...])

    @pl.when(pl.program_id(0) == 1)
    def _():
        out_ref[...] = mm(right_ref[skip:, :], full_ref[...])


def project(acts, skip, at, items, weight, channels):
    rows, features = acts[0].shape
    rows = rows - skip
    blocks = [item[0] for item in items]
    places = [item[1:] for item in items]
    return pl.pallas_call(
        lambda *refs: project_body(places, skip, *refs),
        grid_spec=pltpu.PrefetchScalarGridSpec(
            num_scalar_prefetch=1,
            grid=(2,),
            in_specs=[pl.BlockSpec(v.shape, lambda i, at: (0, 0), pipeline_mode=pl.Buffered(1)) for v in acts]
            + [
                pl.BlockSpec((1,) + b.shape[1:], lambda i, at: (weight, 0, 0), pipeline_mode=pl.Buffered(1))
                for b in blocks
            ],
            out_specs=[
                pl.BlockSpec((rows, channels), lambda i, at: (i, 0)),
                pl.BlockSpec((features, channels), lambda i, at: (0, 0), pipeline_mode=pl.Buffered(1)),
            ],
        ),
        out_shape=[
            jax.ShapeDtypeStruct((2 * rows, channels), f32),
            jax.ShapeDtypeStruct((features, channels), bf16),
        ],
        cost_estimate=pl.CostEstimate(
            flops=4 * rows * features * channels,
            transcendentals=0,
            bytes_accessed=rows * features * 4 + rows * channels * 8 + features * channels * 4,
        ),
        name="project",
    )(at, *acts, *blocks)


def turn_body(x_ref, out_ref):
    out_ref[...] = x_ref[...].T


def turn(x):
    rows, columns = x.shape
    return pl.pallas_call(
        turn_body, out_shape=jax.ShapeDtypeStruct((columns, rows), x.dtype), name="turn", cost_estimate=pl.CostEstimate(flops=1, transcendentals=0, bytes_accessed=1)
    )(x)


def norm_body(x_ref, halo_ref, gain_ref, out_ref, turned_ref):
    def normed(ref, at):
        x = ref[at, :].astype(f32)
        inv = lax.rsqrt(jnp.mean(x * x, axis=-1, keepdims=True) + epsilon)
        return (x * inv * gain_ref[...]).astype(bf16)

    out_ref[:HALO, :] = normed(halo_ref, slice(0, HALO))
    for r in range(x_ref.shape[0] // 128):
        rows = normed(x_ref, slice(128 * r, 128 * r + 128))
        out_ref[HALO + 128 * r : HALO + 128 * r + 128, :] = rows
        turned_ref[:, 128 * r : 128 * r + 128] = rows.T


def norm(x, halo, gain):
    rows, features = x.shape
    return pl.pallas_call(
        norm_body,
        out_shape=[
            jax.ShapeDtypeStruct((HALO + rows, features), bf16),
            jax.ShapeDtypeStruct((features, rows), bf16),
        ],
        cost_estimate=pl.CostEstimate(flops=1, transcendentals=0, bytes_accessed=1),
        name="norm",
    )(x, halo, gain)


def prepare_body(
    own_ref, other_ref, thin_ref, pick_ref, lanes_ref, cbc_ref, ids_ref, row_ref,
    bcx_ref, pre_ref, act_ref, turned_ref, low_ref, dt_ref, log_ref, hv_ref, rv_ref, al_ref, since_ref, flags_ref,
    scr_ref,
):
    length = act_ref.shape[1]
    n_chunks = length // CH
    width = pre_ref.shape[2]
    channels = al_ref.shape[2]
    picked = mm(thin_ref[:, width:], pick_ref[...]).astype(bf16)
    weights = jnp.concatenate([thin_ref[:, :width], picked], axis=1)

    @pl.when(pl.program_id(0) == 0)
    def _():
        scr_ref[...] = mm(own_ref[...], weights)

    @pl.when(pl.program_id(0) == 1)
    def _():
        scr_ref[...] = mm(other_ref[...], weights)

    columns = ids_ref[0].T
    at = slice(HALO, HALO + length)
    ids = columns[at, :1]
    before = columns[HALO - 1 : HALO, :1]
    eight = lax.broadcasted_iota(jnp.int32, (length, 8), 1)
    flags = jnp.where(eight == 3, ids, 0.0)
    near = {}
    for j, k in enumerate((-1, -2, -3, 0, 1, 2, 3)):
        if k != 0:
            near[k] = (columns[HALO + k : HALO + k + length, :1] == ids).astype(f32)
            flags = jnp.where(eight == j, near[k], flags)
    flags_ref[0] = flags

    bcx_ref[0] = scr_ref[:, :width]
    pre = cbc_ref[4:5, :] + cbc_ref[0:1, :] * scr_ref[at, :width]
    for k in range(1, 4):
        pre = pre + cbc_ref[k : k + 1, :] * scr_ref[HALO - k : HALO - k + length, :width] * near[-k]
    act = pre * jax.nn.sigmoid(pre)
    pre_ref[0] = pre
    act_ref[0] = act
    turned_ref[0] = act.T.astype(bf16)
    low_ref[0] = act[:, width // 2 :].astype(bf16)

    dt_in = scr_ref[at, width:] + lanes_ref[0:1, :]
    dt_ref[0] = dt_in
    step = jnp.maximum(dt_in, 0.0) + jnp.log1p(jnp.exp(-jnp.abs(dt_in)))
    log_step = step * lanes_ref[1:2, :]
    log_ref[0] = log_step
    tri = (
        lax.broadcasted_iota(jnp.int32, (CH, CH), 0) >= lax.broadcasted_iota(jnp.int32, (CH, CH), 1)
    ).astype(f32)
    quarter = lax.broadcasted_iota(jnp.int32, (CH, 128), 1) // 32
    low_lanes = lax.broadcasted_iota(jnp.int32, (CH, 128), 1) < 32
    row_at = lax.broadcasted_iota(jnp.int32, (32, CH), 0)
    to_wide = (
        lax.broadcasted_iota(jnp.int32, (128, channels), 1) // 64 == lax.broadcasted_iota(jnp.int32, (128, channels), 0)
    ).astype(f32)
    eight_rows = lax.broadcasted_iota(jnp.int32, (8, 128), 0)
    alphas = jnp.zeros((8, 128), f32)
    lead = jnp.zeros((1, 128), f32)
    chunk_before = before
    for c in range(n_chunks):
        rows = slice(c * CH, (c + 1) * CH)
        running = exact(tri, log_step[rows])
        last = running[CH - 1 : CH, :]
        ids_c = ids[rows]
        chunk_end = ids_c[CH - 1 : CH, :]
        still = (chunk_end == chunk_before).astype(f32)
        alphas = jnp.where(eight_rows == c, still * jnp.exp(last), alphas)
        since = (ids_c == before).astype(f32) * jnp.exp(running + lead)
        since = jnp.where(low_lanes, since, 0.0).astype(bf16)
        since_ref[0, rows, :] = mm(since, to_wide.astype(bf16)).astype(bf16)
        hv = jnp.where(
            quarter == 0,
            running * LOG2E,
            jnp.where(
                quarter == 1,
                step[rows],
                jnp.where(
                    quarter == 2,
                    (ids_c == chunk_before).astype(f32) * jnp.exp(running),
                    (ids_c == chunk_end).astype(f32) * jnp.exp(last - running),
                ),
            ),
        )
        hv_ref[0, rows, :] = hv
        turned = hv.T[:32, :]
        rv_ref[0, :, rows] = jnp.where(
            row_at < 24, turned, jnp.where(row_at == 24, row_ref[0, 0:1, rows], 0.0)
        )
        lead = lead + last
        chunk_before = chunk_end
    first = lax.broadcasted_iota(jnp.int32, (8, 128), 1) < 32
    al_ref[0] = exact(jnp.where(first, alphas, 0.0), to_wide)


def prepare(own, other, thin, pick, lanes, cbc, ids_all, ids_rows, channels):
    length = own.shape[0] - HALO
    width = cbc.shape[1]
    whole = lambda v: pl.BlockSpec(v.shape, lambda s: (0,) * len(v.shape), pipeline_mode=pl.Buffered(1))
    piece = lambda shape: pl.BlockSpec((1,) + shape, lambda s: (s, 0, 0))
    outs = [
        ((HALO + length, width), f32), ((length, width), f32), ((length, width), f32), ((width, length), bf16),
        ((length, width // 2), bf16), ((length, 128), f32), ((length, 128), f32), ((length, 128), f32),
        ((32, length), f32), ((8, channels), f32), ((length, channels), bf16), ((length, 8), f32),
    ]
    return pl.pallas_call(
        prepare_body,
        grid=(2,),
        in_specs=[whole(v) for v in (own, other, thin, pick, lanes, cbc)]
        + [piece(ids_all.shape[1:]), piece(ids_rows.shape[1:])],
        out_specs=[piece(shape) for shape, _ in outs],
        out_shape=[jax.ShapeDtypeStruct((2,) + shape, kind) for shape, kind in outs],
        scratch_shapes=[pltpu.VMEM((HALO + length, width + 128), f32)],
        cost_estimate=pl.CostEstimate(flops=1, transcendentals=0, bytes_accessed=1),
        name="prepare",
    )(own, other, thin, pick, lanes, cbc, ids_all, ids_rows)


def gate_sums_body(here_ref, since_ref, low_ref, state_ref, gate_ref, grad_ref, gain_ref, y_ref, sums_ref):
    y = here_ref[...] + since_ref[...].astype(f32) * mm(low_ref[...], state_ref[0])
    y_ref[...] = y
    gate = gate_ref[...]
    gated = y * (gate * jax.nn.sigmoid(gate))
    scaled = grad_ref[...] * gain_ref[...]
    lane = lax.broadcasted_iota(jnp.int32, sums_ref.shape, 1)
    sums_ref[...] = jnp.where(
        lane == 0,
        jnp.sum(gated * gated, axis=1, keepdims=True),
        jnp.where(lane == 1, jnp.sum(scaled * gated, axis=1, keepdims=True), 0.0),
    )


def gate_sums(here, since, low, state, gate, grad, gain):
    tokens, channels = here.shape
    tile = 128
    per = tokens // tile // 2
    token = lambda width: pl.BlockSpec((tile, width), lambda i: (i, 0))
    return pl.pallas_call(
        gate_sums_body,
        grid=(tokens // tile,),
        in_specs=[
            token(channels), token(channels), token(low.shape[1]),
            pl.BlockSpec((1,) + state.shape[1:], lambda i: (i // per, 0, 0)),
            token(channels), token(channels), pl.BlockSpec((1, channels), lambda i: (0, 0)),
        ],
        out_specs=[token(channels), token(128)],
        out_shape=[jax.ShapeDtypeStruct((tokens, channels), f32), jax.ShapeDtypeStruct((tokens, 128), f32)],
        cost_estimate=pl.CostEstimate(flops=1, transcendentals=0, bytes_accessed=1),
        name="gate_sums",
    )(here, since, low, state, gate, grad, gain)


def gate_grads_body(
    all_channels, per, y_ref, since_ref, low_ref, gate_ref, grad_ref, gain_ref, sums_ref, came_ref,
    mixed_ref, gate_grad_ref, y_grad_ref, gain_grad_ref, state_ref,
):
    at = pl.program_id(0)
    y = y_ref[...]
    gate = gate_ref[...]
    grad = grad_ref[...]
    sums = sums_ref[...] + came_ref[...]
    gate_rms = lax.rsqrt(sums[:, 0:1] / all_channels + epsilon)
    inner = gate_rms * gate_rms * gate_rms * (sums[:, 1:2] / all_channels)
    sig = jax.nn.sigmoid(gate)
    act = gate * sig
    gated = y * act
    hat = gated * gate_rms
    mixed_ref[...] = (hat * gain_ref[...]).astype(bf16)
    gated_grad = gate_rms * (grad * gain_ref[...]) - gated * inner
    y_grad = gated_grad * act
    y_grad_ref[...] = y_grad
    gate_grad_ref[...] = (gated_grad * y * sig * (1.0 + gate * (1.0 - sig))).astype(bf16)
    part = jnp.sum((grad * hat).reshape((y.shape[0] // 8, 8, y.shape[1])), axis=0)
    pushed = tmm(low_ref[...], (y_grad * since_ref[...].astype(f32)).astype(bf16))

    @pl.when(at == 0)
    def _():
        gain_grad_ref[...] = part

    @pl.when(at > 0)
    def _():
        gain_grad_ref[...] += part

    @pl.when(lax.rem(at, per) == 0)
    def _():
        state_ref[0] = pushed

    @pl.when(lax.rem(at, per) > 0)
    def _():
        state_ref[0] += pushed


def gate_grads(y, since, low, gate, grad, gain, sums, came, all_channels):
    tokens, channels = y.shape
    tile = 128
    count = tokens // tile
    per = count // 2
    token = lambda width: pl.BlockSpec((tile, width), lambda i: (i, 0))
    turned = pl.BlockSpec((tile, 128), lambda i: (lax.rem(i + per, count), 0))
    return pl.pallas_call(
        lambda *refs: gate_grads_body(all_channels, per, *refs),
        grid=(count,),
        in_specs=[
            token(channels), token(channels), token(low.shape[1]), token(channels), token(channels),
            pl.BlockSpec((1, channels), lambda i: (0, 0)), token(128), turned,
        ],
        out_specs=[
            token(channels), token(channels), token(channels), pl.BlockSpec((8, channels), lambda i: (0, 0)),
            pl.BlockSpec((1, low.shape[1], channels), lambda i: (i // per, 0, 0)),
        ],
        out_shape=[
            jax.ShapeDtypeStruct((tokens, channels), bf16),
            jax.ShapeDtypeStruct((tokens, channels), bf16),
            jax.ShapeDtypeStruct((tokens, channels), f32),
            jax.ShapeDtypeStruct((8, channels), f32),
            jax.ShapeDtypeStruct((2, low.shape[1], channels), f32),
        ],
        cost_estimate=pl.CostEstimate(flops=1, transcendentals=0, bytes_accessed=1),
        name="gate_grads",
    )(y, since, low, gate, grad, gain, sums, came)


def small_grads_body(
    dbc_ref, came_ref, pre_ref, bcx_ref, flags_ref, own_col_ref, other_col_ref, own_row_ref, other_row_ref,
    log_ref, dt_ref, lanes_ref, back_ref, own_sums_ref, other_sums_ref, gain_ref, dpre_ref, dt_low_ref, taps_ref,
    packed_ref,
):
    length = dpre_ref.shape[0]
    width = dpre_ref.shape[1]
    channels = packed_ref.shape[1]
    pre = pre_ref[0]
    sig = jax.nn.sigmoid(pre)
    dpre = (dbc_ref[0] + came_ref[...]) * (sig * (1.0 + pre * (1.0 - sig)))
    dpre_ref[...] = dpre
    sums = [jnp.sum(dpre * bcx_ref[0, HALO:, :], axis=0, keepdims=True)]
    for k in range(1, 4):
        shifted = bcx_ref[0, HALO - k : HALO - k + length, :]
        sums.append(jnp.sum(dpre * shifted * flags_ref[0, :, k - 1 : k], axis=0, keepdims=True))
    sums.append(jnp.sum(dpre, axis=0, keepdims=True))
    taps_ref[...] = jnp.concatenate(sums + [jnp.zeros((11, width), f32)], axis=0)

    tri = (
        lax.broadcasted_iota(jnp.int32, (CH, CH), 1) >= lax.broadcasted_iota(jnp.int32, (CH, CH), 0)
    ).astype(f32)
    raw_sum = jnp.zeros((1, 128), f32)
    rate_sum = jnp.zeros((1, 128), f32)
    for p, (col_ref, row_ref) in enumerate(((own_col_ref, own_row_ref), (other_col_ref, other_row_ref))):
        for c in range(length // CH):
            rows = slice(c * CH, (c + 1) * CH)
            by_row = jnp.concatenate([row_ref[0, :, rows], jnp.zeros((96, CH), f32)], axis=0).T
            dlog = exact(tri, col_ref[0, rows, :128] - by_row)
            dstep = col_ref[0, rows, 128:] + dlog * lanes_ref[1:2, :]
            raw = dstep * jax.nn.sigmoid(dt_ref[p, rows, :])
            rate_sum += jnp.sum(dlog * log_ref[p, rows, :], axis=0, keepdims=True)
            raw_sum += jnp.sum(raw, axis=0, keepdims=True)
            dt_low_ref[p, rows, :] = mm(raw.astype(bf16), back_ref[...]).astype(bf16)
    to_wide = (
        lax.broadcasted_iota(jnp.int32, (128, channels), 1) // 64 == lax.broadcasted_iota(jnp.int32, (128, channels), 0)
    ).astype(f32)
    both = jnp.concatenate([raw_sum, rate_sum, jnp.zeros((6, 128), f32)], axis=0)
    first = lax.broadcasted_iota(jnp.int32, (8, 128), 1) < 32
    wide = exact(jnp.where(first, both, 0.0), to_wide)
    sums = own_sums_ref[0] + other_sums_ref[0]
    gain = jnp.sum(gain_ref[...], axis=0, keepdims=True)
    packed_ref[...] = jnp.concatenate(
        [sums[:5], gain, sums[5:6], wide[:2], jnp.zeros((7, channels), f32)], axis=0
    )


def small_grads(dbc, came, pre, *rest):
    length, width = came.shape
    channels = rest[-1].shape[1]
    return pl.pallas_call(
        small_grads_body,
        out_shape=[
            jax.ShapeDtypeStruct((length, width), f32),
            jax.ShapeDtypeStruct((2, length, 128), bf16),
            jax.ShapeDtypeStruct((16, width), f32),
            jax.ShapeDtypeStruct((16, channels), f32),
        ],
        cost_estimate=pl.CostEstimate(flops=1, transcendentals=0, bytes_accessed=1),
        name="small_grads",
    )(dbc, came, pre, *rest)


def normed_grads_body(
    dpre_ref, head_ref, flags_ref, cbc_ref, dt_low_ref, own_turned_ref, other_turned_ref, own_ref, other_ref, gate_ref,
    wx_ref, wz_ref, thin_ref, own_out_ref, other_out_ref, part_ref, low_ref, scr_ref,
):
    length, width = dpre_ref.shape

    @pl.when((pl.program_id(0) == 0) & (pl.program_id(1) == 0))
    def _():
        scr_ref[:length, :] = dpre_ref[...]
        scr_ref[length:, :] = head_ref[...]
        raw = cbc_ref[0:1, :] * dpre_ref[...]
        for k in range(1, 4):
            raw = raw + cbc_ref[k : k + 1, :] * scr_ref[k : k + length, :] * flags_ref[0, :, 3 + k : 4 + k]
        own = jnp.concatenate([raw.astype(bf16), dt_low_ref[0]], axis=1)
        other = jnp.concatenate([jnp.zeros((length, width), bf16), dt_low_ref[1]], axis=1)
        low_ref[:length, :] = own
        low_ref[length:, :] = other
        part_ref[...] = (mm(own_turned_ref[...], own) + mm(other_turned_ref[...], other)).astype(bf16)

    def total(ref, rows):
        return (
            mmt(ref[...], wx_ref[...]) + mmt(gate_ref[rows, :], wz_ref[...]) + mmt(low_ref[rows, :], thin_ref[...])
        )

    @pl.when(pl.program_id(0) == 0)
    def _():
        other_out_ref[...] = total(other_ref, slice(length, 2 * length)).astype(bf16)

    @pl.when(pl.program_id(0) == 1)
    def _():
        own_out_ref[...] = total(own_ref, slice(0, length))


def normed_grads(dpre, head, flags, cbc, dt_low, turned, x_low, gate_grad, wx, wz, thin):
    length, width = dpre.shape
    features = wx.shape[0]
    tile = features // 3
    last = features // tile - 1
    whole = lambda v: pl.BlockSpec(v.shape, lambda p, j: (0,) * len(v.shape), pipeline_mode=pl.Buffered(1))
    weight = lambda v: pl.BlockSpec((tile, v.shape[1]), lambda p, j: (j, 0))
    return pl.pallas_call(
        normed_grads_body,
        grid=(2, features // tile),
        in_specs=[whole(v) for v in (dpre, head, flags, cbc, dt_low, *turned, *x_low, gate_grad)]
        + [weight(v) for v in (wx, wz, thin)],
        out_specs=[
            pl.BlockSpec((length, tile), lambda p, j: (0, j * p)),
            pl.BlockSpec((length, tile), lambda p, j: (0, j * (1 - p) + last * p)),
            pl.BlockSpec((features, width + 128), lambda p, j: (0, 0), pipeline_mode=pl.Buffered(1)),
        ],
        out_shape=[
            jax.ShapeDtypeStruct((length, features), f32),
            jax.ShapeDtypeStruct((length, features), bf16),
            jax.ShapeDtypeStruct((features, width + 128), bf16),
        ],
        scratch_shapes=[pltpu.VMEM((2 * length, width + 128), bf16), pltpu.VMEM((length + 8, width), f32)],
        cost_estimate=pl.CostEstimate(
            flops=8 * length * features * features, transcendentals=0, bytes_accessed=8 * features * features
        ),
        name="normed_grads",
    )(dpre, head, flags, cbc, dt_low, *turned, *x_low, gate_grad, wx, wz, thin)


def branch_body(mixed_ref, weight_ref, own_ref, other_ref):
    part = mmt(mixed_ref[...], weight_ref[...])

    @pl.when(pl.program_id(0) == 0)
    def _():
        other_ref[...] = part.astype(bf16)

    @pl.when(pl.program_id(0) == 1)
    def _():
        own_ref[...] = part


def branch_parts(mixed, weight):
    tokens, channels = mixed.shape
    features = weight.shape[0]
    half = pl.BlockSpec((tokens // 2, features), lambda p: (0, 0))
    return pl.pallas_call(
        branch_body,
        grid=(2,),
        in_specs=[
            pl.BlockSpec((tokens // 2, channels), lambda p: (1 - p, 0)),
            pl.BlockSpec(weight.shape, lambda p: (0, 0), pipeline_mode=pl.Buffered(1)),
        ],
        out_specs=[half, half],
        out_shape=[
            jax.ShapeDtypeStruct((tokens // 2, features), f32),
            jax.ShapeDtypeStruct((tokens // 2, features), bf16),
        ],
        cost_estimate=pl.CostEstimate(
            flops=2 * tokens * channels * features, transcendentals=0, bytes_accessed=4 * features * channels
        ),
        name="branch_parts",
    )(mixed, weight)


def x_grads_body(own_ref, came_ref, x_ref, cot_ref, gain_ref, out_ref, gain_grad_ref):
    grad = own_ref[...] + came_ref[...].astype(f32)
    x = x_ref[...].astype(f32)
    inv = lax.rsqrt(jnp.mean(x * x, axis=-1, keepdims=True) + epsilon)
    hat = x * inv
    part = jnp.sum((grad * hat).reshape((x.shape[0] // 8, 8, x.shape[1])), axis=0)
    pushed = grad * gain_ref[...]
    inner = jnp.mean(pushed * x, axis=-1, keepdims=True)
    out_ref[...] = cot_ref[...].astype(f32) + inv * pushed - hat * (inv * inv * inner)

    @pl.when(pl.program_id(0) == 0)
    def _():
        gain_grad_ref[...] = part

    @pl.when(pl.program_id(0) > 0)
    def _():
        gain_grad_ref[...] += part


def x_grads(own, came, x, cot, gain):
    tokens, features = own.shape
    tile = 128
    token = pl.BlockSpec((tile, features), lambda i: (i, 0))
    return pl.pallas_call(
        x_grads_body,
        grid=(tokens // tile,),
        in_specs=[token] * 4 + [pl.BlockSpec((1, features), lambda i: (0, 0))],
        out_specs=[token, pl.BlockSpec((8, features), lambda i: (0, 0))],
        out_shape=[jax.ShapeDtypeStruct((tokens, features), f32), jax.ShapeDtypeStruct((8, features), f32)],
        cost_estimate=pl.CostEstimate(flops=1, transcendentals=0, bytes_accessed=1),
        name="x_grads",
    )(own, came, x, cot, gain)


def weight_parts_body(count, group, flip, at_ref, *refs):
    keep_ref, give_ref = refs[-2:]
    rows, columns = keep_ref.shape[3:]
    rights_per = (len(refs) - 2) // count - 2
    for w in range(count):
        lefts = refs[2 * w : 2 * w + 2]
        rights = refs[2 * count + w * rights_per : 2 * count + (w + 1) * rights_per]
        tokens = lefts[0].shape[1]

        @pl.when(pl.program_id(0) == w)
        def _():
            def right(i):
                ref, start = (rights[0], i * tokens) if rights_per == 1 else (rights[i], 0)
                return jnp.concatenate(
                    [
                        ref[start : start + tokens, pl.ds(pl.multiple_of(at_ref[4 + d], columns), columns)]
                        for d in group
                    ],
                    axis=1,
                )

            values = [right(0), right(1)]
            for k in range(4):
                left = pl.ds(pl.multiple_of(at_ref[k], rows), rows)
                part = mm(lefts[0][left, :], values[0]) + mm(lefts[1][left, :], values[1])
                part = part.astype(bf16)
                away, place = (k // 2, k % 2) if flip == 0 else (k % 2, k // 2)
                target = give_ref if away else keep_ref
                for i in range(len(group)):
                    target[0, i, place] = part[:, i * columns : (i + 1) * columns]


def weight_parts(at, lefts, rights, group, own_rows, columns, flip):
    count = len(lefts)
    tokens = 2 * lefts[0][0].shape[1]
    lefts = [piece for left in lefts for piece in left]
    rights = [piece for right in rights for piece in right]
    shape = (count, len(group), 2, 2 * own_rows, columns)
    whole = lambda v: pl.BlockSpec(v.shape, lambda w, at: (0, 0), pipeline_mode=pl.Buffered(1))
    return pl.pallas_call(
        lambda *refs: weight_parts_body(count, group, flip, *refs),
        grid_spec=pltpu.PrefetchScalarGridSpec(
            num_scalar_prefetch=1,
            grid=(count,),
            in_specs=[whole(v) for v in lefts] + [whole(v) for v in rights],
            out_specs=[pl.BlockSpec((1,) + shape[1:], lambda w, at: (w, 0, 0, 0, 0))] * 2,
        ),
        out_shape=[jax.ShapeDtypeStruct(shape, bf16)] * 2,
        cost_estimate=pl.CostEstimate(
            flops=2 * count * tokens * 8 * own_rows * columns * len(group),
            transcendentals=0,
            bytes_accessed=count * tokens * (8 * own_rows + columns * len(group)) * 2,
        ),
        name="weight_parts",
    )(at, *lefts, *rights)


def swap(value):
    size = lax.axis_size("dp")
    return lax.ppermute(value, "dp", [(i, i ^ 1) for i in range(size)])


def across(value, bit):
    size = lax.axis_size("dp")
    return lax.ppermute(value, "dp", [(i, i ^ (1 << bit)) for i in range(size)])


def around(value, by):
    size = lax.axis_size("tensor")
    by = by % size
    return lax.ppermute(value, "tensor", [(i, (i + by) % size) for i in range(size)])


def along_sequence(value, pieces, forward):
    size = lax.axis_size("tensor")
    pairs = [(i, i + 1) for i in range(size - 1) if (i + 1) % pieces]
    if not forward:
        pairs = [(b, a) for a, b in pairs]
    return lax.ppermute(value, "tensor", pairs)


class Place:
    def __init__(self):
        dp = lax.axis_index("dp")
        self.core = dp % 2
        self.slots = lax.axis_size("tensor")
        self.slot = lax.axis_index("tensor")
        self.bits = [b for b in range(1, lax.axis_size("dp").bit_length() - 1)]
        self.side = {b: (dp >> b) % 2 for b in range(lax.axis_size("dp").bit_length() - 1)}

    def gather_slots(self, block):
        blocks = [block] + [around(block, d) for d in range(1, self.slots)]
        shape = (block.shape[0], self.slots, block.shape[1])
        index = lax.broadcasted_iota(jnp.int32, shape, 1)
        out = jnp.broadcast_to(block[:, None, :], shape)
        for d in range(1, self.slots):
            from_slot = (self.slot - d) % self.slots
            out = jnp.where(index == from_slot, blocks[d][:, None, :], out)
        return out

    def scatter_slots(self, blocks):
        def block(at):
            return lax.dynamic_index_in_dim(blocks, at % self.slots, 1, keepdims=False)

        total = block(self.slot).astype(f32)
        for d in range(1, self.slots):
            total = total + around(block(self.slot + d), d).astype(f32)
        return total

    def ordered(self, bit, mine, other, axis):
        mine, other = jnp.expand_dims(mine, axis), jnp.expand_dims(other, axis)
        low = self.side[bit] == 0
        return jnp.where(
            low,
            jnp.concatenate([mine, other], axis=axis),
            jnp.concatenate([other, mine], axis=axis),
        )

    def gather_rows(self, block, upward):
        done = block
        for bit in self.bits if upward else self.bits[::-1]:
            axis = 0 if upward else len(done.shape) - 2
            done = self.ordered(bit, done, across(done, bit), axis)
        return done.reshape((-1, block.shape[1]))

    def scatter_rows(self, whole, upward, low_bit=1):
        bits = [b for b in self.bits if b >= low_bit]
        if low_bit == 0:
            bits = [0] + bits
        count = len(bits)
        rows = whole.shape[0] >> count
        left = sorted(bits, reverse=True)
        now = whole.reshape((2,) * count + (rows, whole.shape[1]))
        for bit in bits if upward else bits[::-1]:
            axis = left.index(bit)
            left.remove(bit)
            side = self.side[bit]
            keep = lax.dynamic_index_in_dim(now, side, axis, keepdims=False)
            give = lax.dynamic_index_in_dim(now, 1 - side, axis, keepdims=False)
            now = (keep.astype(f32) + across(give, bit).astype(f32)).astype(whole.dtype)
        return now

    def half_rows(self, whole, bit):
        keep = lax.dynamic_index_in_dim(whole, self.side[bit], whole.ndim - 3, keepdims=False)
        give = lax.dynamic_index_in_dim(whole, 1 - self.side[bit], whole.ndim - 3, keepdims=False)
        return (keep.astype(f32) + across(give, bit).astype(f32)).astype(whole.dtype)

    def ordered_sum(self, part):
        return self.half_rows(part.reshape((2, 2, 2, -1, part.shape[1])), 0)

    def gather_weight(self, mine, other):
        both = self.ordered(0, mine, other, 0).reshape((-1, mine.shape[1]))
        blocks = self.gather_slots(both)
        half = self.slots // 2
        first = blocks[:, :half].reshape((both.shape[0], -1))
        second = blocks[:, half:].reshape((both.shape[0], -1))
        return jnp.concatenate(
            [self.gather_rows(first, True), self.gather_rows(second, False)], axis=1
        )

    def scatter_weight(self, part):
        columns = part.shape[1] // 2
        half = self.slots // 2
        first = self.scatter_rows(part[:, :columns], False)
        second = self.scatter_rows(part[:, columns:], True)
        rows = first.shape[0]
        blocks = jnp.concatenate(
            [first.reshape((rows, half, -1)), second.reshape((rows, half, -1))], axis=1
        )
        mine = self.scatter_slots(blocks).reshape((2, rows // 2, -1))
        keep = lax.dynamic_index_in_dim(mine, self.core, 0, keepdims=False)
        give = lax.dynamic_index_in_dim(mine, 1 - self.core, 0, keepdims=False)
        out = self.ordered(0, keep, swap(give), 1)
        return out.reshape((rows // 2, -1))

    def fast(self, half_channels):
        return len(self.bits) == 2 and self.slots == 4 and half_channels % 128 == 0

    def offsets(self, own_rows, half_channels):
        chip = lax.axis_index("dp") // 2
        rows = [(chip ^ k) * 2 * own_rows for k in range(4)]
        columns = [(self.slot - d) % self.slots * half_channels for d in range(self.slots)]
        return jnp.stack(rows + columns).astype(jnp.int32)

    def unit(self, d, block):
        first, second = self.bits if d % 2 == 0 else self.bits[::-1]
        return across(block, first), across(block, second)

    def forward(self, d, one):
        return across(one, self.bits[1] if d % 2 == 0 else self.bits[0])

    def items(self, d, here, one, two, both):
        order = (here, one, two, both) if d % 2 == 0 else (here, two, one, both)
        return [(block, d, k) for k, block in enumerate(order)]

    def first_exchange(self, at, give):
        return across(give, self.bits[1 - at])

    def second_term(self, keep, came):
        return (keep[:, :, 1].astype(f32) + came[:, :, 1].astype(f32)).astype(bf16)

    def second_exchange(self, at, term):
        return across(term, self.bits[at])

    def slot_parts(self, keeps, cames, lasts, groups):
        own = {}
        for group, keep, came, last in zip(groups, keeps, cames, lasts):
            total = keep[:, :, 0].astype(f32) + came[:, :, 0].astype(f32) + last.astype(f32)
            for i, d in enumerate(group):
                own[d] = total[:, i]
        return own

    def slot_sum(self, keeps, cames, lasts, groups):
        own = self.slot_parts(keeps, cames, lasts, groups)
        return own[0], [around(own[d].astype(bf16), -d) for d in range(1, self.slots)]

    def to_owner(self, own, others):
        total = own
        for other in others:
            total = total + other.astype(f32)
        weights, rows, columns = total.shape
        total = total.reshape((weights, 2, rows // 2, columns))
        keep = lax.dynamic_index_in_dim(total, self.core, 1, keepdims=False)
        give = lax.dynamic_index_in_dim(total, 1 - self.core, 1, keepdims=False)
        out = self.ordered(0, keep, swap(give), 2)
        return out.reshape((weights, rows // 2, 2 * columns))

    def sum_chips(self, value):
        for bit in self.bits:
            value = value + across(value, bit)
        return value

    def sum_slots(self, value):
        total = value.astype(f32)
        for d in range(1, self.slots):
            total = total + around(value, d).astype(f32)
        return total


def on_device_general(
    x_in,
    segment_ids,
    norm_gain,
    w_x,
    w_z,
    w_bc,
    w_dt,
    conv_x,
    conv_x_bias,
    conv_bc,
    conv_bc_bias,
    dt_bias,
    a_log,
    d_skip,
    gate_gain,
    w_out,
    cotangent,
):
    place = Place()
    core, slots, slot = place.core, place.slots, place.slot
    length, features = x_in.shape
    sequences, whole_length = segment_ids.shape
    pieces = whole_length // length
    own_rows = w_x.shape[0]
    slot_channels = w_x.shape[1]
    slot_heads = w_dt.shape[1]
    half_channels = slot_channels // 2
    half_heads = slot_heads // 2
    channels = half_channels * slots
    heads = half_heads * slots
    all_channels = 2 * channels
    all_heads = 2 * heads
    bc_width = w_bc.shape[1]
    n_chunks = length // CH

    def split(weight):
        return weight.reshape((own_rows, 2, half_channels))

    stacked = jnp.stack([split(w_x), split(w_z), split(w_out.T)])
    mine = lax.dynamic_index_in_dim(stacked, core, 2, keepdims=False)
    other = swap(lax.dynamic_index_in_dim(stacked, 1 - core, 2, keepdims=False))
    wx = place.gather_weight(mine[0], other[0])
    dt_slots = place.gather_slots(w_dt).reshape((own_rows, all_heads))
    thin = jnp.concatenate([w_bc, dt_slots, norm_gain[:, None]], axis=1)
    thin = jnp.pad(thin, ((0, 0), (0, bc_width + 128 - thin.shape[1])))
    thin = place.ordered(0, thin, swap(thin), 0).reshape((2 * own_rows, -1))
    thin = place.gather_rows(thin, True)
    wz = place.gather_weight(mine[1], other[1])
    wo = place.gather_weight(mine[2], other[2])

    rows = jnp.concatenate(
        [
            conv_x,
            conv_x_bias[None],
            gate_gain[None],
            jnp.pad(jnp.concatenate([dt_bias, a_log, d_skip])[None], ((0, 0), (0, slot_channels - 3 * slot_heads))),
            jnp.zeros((1, slot_channels), f32),
        ],
        axis=0,
    )
    rows = place.gather_slots(rows)
    own = lax.dynamic_index_in_dim(
        rows.reshape((8, slots, 2, half_channels)), core, 2, keepdims=False
    ).reshape((8, channels))
    gain_row = own[5:6]
    lane = jnp.arange(128)
    head_at = lane % 32
    global_head = (head_at // half_heads) * slot_heads + core * half_heads + head_at % half_heads
    pick = ((lane[:, None] == global_head[None, :]) & (head_at < heads)[None, :]).astype(f32)
    small = rows[6, :, : 3 * slot_heads].reshape((slots, 3, slot_heads)).transpose(1, 0, 2)
    small = jnp.pad(small.reshape((3, all_heads)), ((0, 5), (0, 128 - all_heads)))
    small = exact(small, pick)
    bias_lanes = small[0]
    rate_lanes = jnp.where(head_at < heads, -jnp.exp(small[1]), 0.0)
    to_heads = head_map(channels, f32)
    skip_row = exact(small[2:3] * (lane < 32), to_heads.T)
    cw = jnp.concatenate([own[:5], skip_row, jnp.zeros((2, channels), f32)], axis=0)

    padded = jnp.pad(segment_ids, ((0, 0), (HALO, HALO)), constant_values=-1)
    ids_own = lax.dynamic_slice(
        padded, (slot // pieces, (slot % pieces) * length), (1, length + 2 * HALO)
    )
    ids_all = jnp.concatenate([ids_own, swap(ids_own)], axis=0)
    ids = ids_all[:, HALO : HALO + length]
    before = ids_all[:, HALO - 1]

    def near(k):
        return ids_all[:, HALO + k : HALO + k + length] == ids

    flags = [near(-1), near(-2), near(-3), ids, near(1), near(2), near(3), jnp.zeros_like(ids)]
    flags = jnp.stack([v.astype(f32) for v in flags], axis=-1)

    x_rows = jnp.concatenate([along_sequence(x_in[-HALO:], pieces, True), x_in], axis=0)
    tokens_ext = x_rows.astype(f32)
    inv_ext = lax.rsqrt(jnp.mean(tokens_ext * tokens_ext, axis=-1, keepdims=True) + epsilon)
    gain = thin[:, bc_width + all_heads].astype(f32)[None, :]
    normed_own = (tokens_ext * inv_ext * gain).astype(bf16)
    normed_other = swap(normed_own)
    normed_ext = jnp.concatenate([normed_own, normed_other], axis=0)
    normed = jnp.concatenate([normed_own[HALO:], normed_other[HALO:]], axis=0)
    tokens, inv_rms = tokens_ext[HALO:], inv_ext[HALO:]
    cot = jnp.concatenate([cotangent, swap(cotangent)], axis=0)

    dt_pick = jnp.dot(thin[:, bc_width:], pick.astype(bf16), preferred_element_type=f32).astype(bf16)
    thin_proj = mm(normed_ext, jnp.concatenate([thin[:, :bc_width], dt_pick], axis=1))
    thin_proj = thin_proj.reshape((2, HALO + length, -1))
    bc_ext = thin_proj[:, :, :bc_width]
    dt_in = thin_proj[:, HALO:, bc_width:] + bias_lanes
    x_ext = mm(normed_ext, wx).reshape((2, HALO + length, channels))

    bc_pre = conv_bc_bias + conv_bc[0] * bc_ext[:, HALO:]
    for k in range(1, conv_bc.shape[0]):
        shifted = bc_ext[:, HALO - k : HALO - k + length]
        bc_pre = bc_pre + conv_bc[k] * shifted * flags[:, :, k - 1 : k]
    bc_act = jax.nn.silu(bc_pre)
    bc_turned = bc_act.astype(bf16).transpose(0, 2, 1)
    c_low = bc_act[:, :, bc_width // 2 :].astype(bf16)

    step = jax.nn.softplus(dt_in)
    log_step = (step * rate_lanes).reshape((2 * n_chunks, CH, 128))
    tri = (jnp.arange(CH)[:, None] >= jnp.arange(CH)[None, :]).astype(f32)
    running = jnp.einsum("ts,csh->cth", tri, log_step, precision=highest)
    running = running.reshape((2, n_chunks, CH, 128))
    last = running[:, :, -1:, :]
    ids_chunks = ids.reshape((2, n_chunks, CH, 1))
    chunk_end = ids_chunks[:, :, -1:, :]
    chunk_before = jnp.concatenate(
        [before[:, None, None, None], chunk_end[:, :-1]], axis=1
    )
    still = (chunk_end == chunk_before).astype(f32)
    alpha = still * jnp.exp(last)
    lead = jnp.cumsum(last, axis=1) - last
    since_piece = (ids_chunks == before[:, None, None, None]).astype(f32) * jnp.exp(running + lead)
    since_piece = since_piece.reshape((2 * length, 128))
    group_lane = lane // 32
    hv = jnp.where(
        group_lane == 0,
        running * LOG2E,
        jnp.where(
            group_lane == 1,
            step.reshape((2, n_chunks, CH, 128)),
            jnp.where(
                group_lane == 2,
                (ids_chunks == chunk_before).astype(f32) * jnp.exp(running),
                (ids_chunks == chunk_end).astype(f32) * jnp.exp(last - running),
            ),
        ),
    ).reshape((2, length, 128))
    rv = jnp.concatenate(
        [
            hv[:, :, :24].transpose(0, 2, 1),
            ids.astype(f32)[:, None, :],
            jnp.zeros((2, 7, length), f32),
        ],
        axis=1,
    )
    first_lanes = (lane < 32).astype(f32)
    al = exact((alpha * first_lanes).reshape((2 * n_chunks, 128)), to_heads.T)
    al = al.reshape((2, n_chunks, channels))
    whole_alpha = jnp.prod(al, axis=1, keepdims=True)
    al = jnp.pad(al, ((0, 0), (0, 8 - n_chunks), (0, 0)))
    wide_since = mm((since_piece * first_lanes).astype(bf16), to_heads.T.astype(bf16))
    wide_since = wide_since.reshape((2, length, channels))

    def hand_on(local, forward):
        low = local.astype(bf16)
        for _ in range(pieces - 2):
            came = along_sequence(low, pieces, forward)
            low = (local + whole_alpha * came.astype(f32)).astype(bf16)
        return along_sequence(low, pieces, forward)

    y_here, states = scan_fwd(hv, flags, rv, al, bc_act, bc_turned, x_ext, cw, CH)
    state_in = hand_on(states[:, -1], True)
    y = y_here + wide_since * lax.dot_general(
        c_low, state_in, (((2,), (1,)), ((0,), (0,))), preferred_element_type=f32
    )

    gate_in = mm(normed, wz)
    mixed_grad = mm(cot, wo)
    y = y.reshape((2 * length, channels))
    sig = jax.nn.sigmoid(gate_in)
    act = gate_in * sig
    gated = y * act
    scaled = mixed_grad * gain_row
    sums = jnp.stack([jnp.sum(gated * gated, axis=1), jnp.sum(scaled * gated, axis=1)])
    sums = sums.reshape((2, 2, length))
    sums = (sums + swap(sums)[:, ::-1]).reshape((2, 2 * length))
    gate_rms = lax.rsqrt(sums[0] / all_channels + epsilon)[:, None]
    mixed = (gated * gate_rms * gain_row).astype(bf16)
    gate_gain_part = jnp.sum(mixed_grad * gated * gate_rms, axis=0)
    gated_grad = gate_rms * scaled - gated * gate_rms**3 * (sums[1] / all_channels)[:, None]
    y_grad = (gated_grad * act).reshape((2, length, channels))
    gate_grad = (gated_grad * y * sig * (1.0 + gate_in * (1.0 - sig))).astype(bf16)

    state_grad = lax.dot_general(
        c_low, (y_grad * wide_since).astype(bf16), (((1,), (1,)), ((0,), (0,))), preferred_element_type=f32
    )
    state_grad = hand_on(state_grad, False)
    wo_part = tmm(cot, mixed).astype(bf16)
    w_out_grad = place.scatter_weight(wo_part).T
    branch = mmt(mixed, wo)
    block_out = (tokens + branch[:length] + swap(branch[length:].astype(bf16)).astype(f32)).astype(bf16)
    wz_part = tmm(normed, gate_grad).astype(bf16)
    w_z_grad = place.scatter_weight(wz_part)

    x_low, tail, head, dbc, dcol, drow, dcw = scan_bwd(
        hv, flags, rv, al, bc_act, bc_turned, x_ext, cw, y_grad, states, state_in, state_grad, CH
    )

    head = along_sequence(head, pieces, False)

    def past_end(begin, taps):
        total = jnp.zeros((begin.shape[0], HALO, begin.shape[2]), f32)
        for k in range(1, taps.shape[0]):
            moved = jnp.pad(begin[:, :k], ((0, 0), (HALO - k, 0), (0, 0)))
            total = total + taps[k] * moved * flags[: begin.shape[0], length - HALO :, 3 + k : 4 + k]
        return total

    fixed = (tail + past_end(head, own[:4])).astype(bf16)
    x_low = lax.dynamic_update_slice(x_low, fixed, (0, length - HALO, 0)).reshape((2 * length, channels))

    bc_grad = dbc[0] + swap(dbc[1])
    pre = bc_pre[0]
    sig_bc = jax.nn.sigmoid(pre)
    bc_dpre = bc_grad * (sig_bc * (1.0 + pre * (1.0 - sig_bc)))
    bc_head = along_sequence(bc_dpre[:8], pieces, False)
    bc_raw = conv_bc[0] * bc_dpre
    bc_taps = [jnp.sum(bc_dpre * bc_ext[0, HALO:], axis=0)]
    longer = jnp.concatenate([bc_dpre, bc_head], axis=0)
    for k in range(1, conv_bc.shape[0]):
        bc_raw = bc_raw + conv_bc[k] * longer[k : k + length] * flags[0, :, 3 + k : 4 + k]
        shifted = bc_ext[0, HALO - k : HALO - k + length]
        bc_taps.append(jnp.sum(bc_dpre * shifted * flags[0, :, k - 1 : k], axis=0))
    bc_low = bc_raw.astype(bf16)
    bc_small = jnp.stack(bc_taps + [jnp.sum(bc_dpre, axis=0)] + [jnp.zeros((bc_width,), f32)] * 3)
    bc_small = place.sum_chips(bc_small + swap(bc_small))
    bc_small = place.sum_slots(bc_small)

    dcum = dcol[:, :, :128] - jnp.pad(drow.transpose(0, 2, 1), ((0, 0), (0, 0), (0, 96)))
    dlog = jnp.einsum("ts,csh->cth", tri.T, dcum.reshape((2 * n_chunks, CH, 128)), precision=highest)
    dstep = dcol[:, :, 128:] + dlog.reshape((2, length, 128)) * rate_lanes
    dt_raw = (dstep * jax.nn.sigmoid(dt_in)).reshape((2 * length, 128))
    rate_part = jnp.sum(dlog * log_step, axis=(0, 1))
    place_back = (pick * first_lanes).T.astype(bf16)
    dt_low = mm(dt_raw.astype(bf16), place_back).astype(bf16)

    dcw = jnp.sum(dcw, axis=0)
    head_rows = jnp.stack([jnp.sum(dt_raw, axis=0), rate_part]) * first_lanes
    head_rows = exact(head_rows, to_heads.T)
    packed = jnp.concatenate(
        [dcw[:5], gate_gain_part[None], dcw[5:6], head_rows, jnp.zeros((7, channels), f32)], axis=0
    )
    packed = place.sum_chips(packed).reshape((16, slots, half_channels))
    packed = place.scatter_slots(packed)
    packed = place.ordered(0, packed, swap(packed), 1).reshape((16, slot_channels))
    by_head = packed[6:9].reshape((3, slot_heads, 64))

    wx_part = tmm(normed, x_low).astype(bf16)
    w_x_grad = place.scatter_weight(wx_part)
    thin_low = jnp.concatenate(
        [jnp.concatenate([bc_low, jnp.zeros_like(bc_low)], axis=0), dt_low], axis=1
    )
    thin_part = tmm(normed, thin_low).astype(bf16)
    thin_grad = place.scatter_rows(thin_part, True, low_bit=0)
    thin_grad = place.sum_slots(thin_grad)
    w_bc_grad = thin_grad[:, :bc_width]
    w_dt_grad = lax.dynamic_slice_in_dim(thin_grad, bc_width + slot * slot_heads, slot_heads, 1)

    normed_grad = mmt(x_low, wx) + mmt(gate_grad, wz) + mmt(thin_low, thin)
    normed_grad = normed_grad[:length] + swap(normed_grad[length:].astype(bf16)).astype(f32)
    gain_part = jnp.sum(normed_grad * tokens * inv_rms, axis=0)
    pushed = normed_grad * gain
    x_grad = (
        cotangent.astype(f32)
        + inv_rms * pushed
        - tokens * inv_rms**3 * jnp.mean(pushed * tokens, axis=-1, keepdims=True)
    )
    gain_rows = gain_part.reshape((features // own_rows * 2, own_rows // 2))
    gain_rows = place.scatter_rows(gain_rows, True, low_bit=0)
    norm_gain_grad = place.sum_slots(gain_rows).reshape((own_rows,))
    return (
        block_out,
        x_grad,
        norm_gain_grad,
        w_x_grad,
        w_z_grad,
        w_bc_grad,
        w_dt_grad,
        packed[:4],
        packed[4],
        bc_small[:4],
        bc_small[4],
        by_head[1, :, 0],
        by_head[2, :, 0],
        jnp.sum(by_head[0], axis=1),
        packed[5],
        w_out_grad,
    )


def tie(*values):
    return lax.optimization_barrier(values)


def on_device(*args):
    if Place().fast(args[3].shape[1] // 2):
        return on_device_fast(*args)
    return on_device_general(*args)


def on_device_fast(
    x_in,
    segment_ids,
    norm_gain,
    w_x,
    w_z,
    w_bc,
    w_dt,
    conv_x,
    conv_x_bias,
    conv_bc,
    conv_bc_bias,
    dt_bias,
    a_log,
    d_skip,
    gate_gain,
    w_out,
    cotangent,
):
    place = Place()
    core, slots, slot = place.core, place.slots, place.slot
    length, features = x_in.shape
    sequences, whole_length = segment_ids.shape
    pieces = whole_length // length
    own_rows = w_x.shape[0]
    slot_channels = w_x.shape[1]
    slot_heads = w_dt.shape[1]
    half_channels = slot_channels // 2
    half_heads = slot_heads // 2
    channels = half_channels * slots
    heads = half_heads * slots
    all_channels = 2 * channels
    all_heads = 2 * heads
    bc_width = w_bc.shape[1]
    n_chunks = length // CH
    groups = [tuple(range(0, slots, 2)), tuple(range(1, slots, 2))]
    at = place.offsets(own_rows, half_channels)

    def split(weight):
        return weight.reshape((own_rows, 2, half_channels))

    stacked = jnp.stack([split(w_x), split(w_z), split(w_out.T)])
    mine = lax.dynamic_index_in_dim(stacked, core, 2, keepdims=False)
    other = swap(lax.dynamic_index_in_dim(stacked, 1 - core, 2, keepdims=False))
    both = place.ordered(0, mine, other, 1).reshape((3, 2 * own_rows, half_channels))
    padded = jnp.pad(segment_ids, ((0, 0), (HALO, HALO)), constant_values=-1)
    ids_own = lax.dynamic_slice(
        padded, (slot // pieces, (slot % pieces) * length), (1, length + 2 * HALO)
    )
    ids_all = jnp.concatenate([ids_own, swap(ids_own)], axis=0).astype(f32)
    both, ids_all, conv_x, conv_x_bias, gate_gain, dt_bias, a_log, d_skip, w_dt, w_bc, norm_gain, x_in, cotangent = tie(
        both, ids_all, conv_x, conv_x_bias, gate_gain, dt_bias, a_log, d_skip, w_dt, w_bc, norm_gain, x_in, cotangent)

    rows = jnp.concatenate(
        [
            conv_x,
            conv_x_bias[None],
            gate_gain[None],
            jnp.pad(
                jnp.concatenate([dt_bias, a_log, d_skip])[None], ((0, 0), (0, slot_channels - 3 * slot_heads))
            ),
            jnp.zeros((1, slot_channels), f32),
            jnp.pad(w_dt.T.astype(f32), ((0, 0), (0, slot_channels - own_rows))),
        ],
        axis=0,
    )
    rows = place.gather_slots(rows)
    halo = along_sequence(x_in[-HALO:], pieces, True)
    wx_here = [both[:1]] + [around(both[:1], d) for d in range(1, slots)]
    wx_one, wx_two = {}, {}
    wx_one[0], wx_two[0] = place.unit(0, wx_here[0])
    cot_turned_own = turn(cotangent)
    rows, halo, wx_here[slots - 1], wx_one, wx_two, cot_turned_own, w_bc, norm_gain = tie(
        rows, halo, wx_here[slots - 1], wx_one, wx_two, cot_turned_own, w_bc, norm_gain)
    dt_slots = rows[8:, :, :own_rows].transpose(2, 1, 0).reshape((own_rows, all_heads)).astype(bf16)
    thin = jnp.concatenate([w_bc, dt_slots, norm_gain[:, None]], axis=1)
    thin = jnp.pad(thin, ((0, 0), (0, bc_width + 128 - thin.shape[1])))
    thin = place.ordered(0, thin, swap(thin), 0)
    low, high = place.bits
    thin = place.ordered(low, thin, across(thin, low), 0)
    odd = slots - 1
    wx_one[odd] = across(wx_here[odd], high)
    thin, wx_here[odd], wx_here[1], wx_one, cot_turned_own, cotangent = tie(
        thin, wx_here[odd], wx_here[1], wx_one, cot_turned_own, cotangent)
    thin = place.ordered(high, thin, across(thin, high), 0).reshape((features, -1))
    wx_two[odd] = across(wx_here[odd], low)
    gain = thin[:, bc_width + all_heads].astype(f32)[None, :]
    thin, gain, wx_here, wx_two, both, cot_turned_own, cotangent = tie(
        thin, gain, wx_here, wx_two, both, cot_turned_own, cotangent)
    pair_here = {0: both[1:], 1: around(both[1:], 1)}
    normed_own, normed_turned_own = norm(x_in, halo, gain)
    normed_both = [normed_own, swap(normed_own)]
    for d in range(1, slots - 1):
        wx_one[d], wx_two[d] = place.unit(d, wx_here[d])

    thin, gain, normed_both, normed_turned_own, pair_here, rows, ids_all, wx_here, wx_one, wx_two = tie(
        thin, gain, normed_both, normed_turned_own, pair_here, rows, ids_all, wx_here, wx_one, wx_two)
    normed_turned = [normed_turned_own, swap(normed_turned_own)]
    cot = [cotangent, swap(cotangent)]
    cot_turned = [cot_turned_own, swap(cot_turned_own)]

    pair_here[2] = around(pair_here[0], 2)
    one, two, both_k = {}, {}, {}
    one[0], two[0] = place.unit(0, pair_here[0])
    own = lax.dynamic_index_in_dim(
        rows[:8].reshape((8, slots, 2, half_channels)), core, 2, keepdims=False
    ).reshape((8, channels))
    gain_row = own[5:6]
    lane = jnp.arange(128)
    head_at = lane % 32
    global_head = (head_at // half_heads) * slot_heads + core * half_heads + head_at % half_heads
    pick = ((lane[:, None] == global_head[None, :]) & (head_at < heads)[None, :]).astype(f32)
    first_lanes = (lane < 32).astype(f32)
    small = rows[6, :, : 3 * slot_heads].reshape((slots, 3, slot_heads)).transpose(1, 0, 2)
    small = jnp.pad(small.reshape((3, all_heads)), ((0, 5), (0, 128 - all_heads)))
    small = exact(small, pick)
    bias_lanes = small[0]
    rate_lanes = jnp.where(head_at < heads, -jnp.exp(small[1]), 0.0)
    to_heads = head_map(channels, f32)
    skip_row = exact(small[2:3] * first_lanes, to_heads.T)
    cw = jnp.concatenate([own[:5], skip_row, jnp.zeros((2, channels), f32)], axis=0)
    lanes = jnp.concatenate([bias_lanes[None], rate_lanes[None], jnp.zeros((6, 128), f32)], axis=0)
    cbc = jnp.concatenate([conv_bc, conv_bc_bias[None], jnp.zeros((3, bc_width), f32)], axis=0)
    wide_ids = jnp.pad(ids_all, ((0, 0), (0, -ids_all.shape[1] % 128)))
    wide_ids = jnp.broadcast_to(wide_ids[:, None, :], (2, 8, wide_ids.shape[1]))
    ids_rows = jnp.broadcast_to(ids_all[:, None, HALO : HALO + length], (2, 8, length))
    tri = (jnp.arange(CH)[:, None] >= jnp.arange(CH)[None, :]).astype(f32)

    bc_ext, bc_pre, bc_act, bc_turned, c_low, dt_in, log_step, hv, rv, al, wide_since, flags = prepare(
        normed_both[0], normed_both[1], thin, pick.astype(bf16), lanes, cbc, wide_ids, ids_rows, channels)
    whole_alpha = jnp.prod(al[:, :n_chunks], axis=1, keepdims=True)
    log_step = log_step.reshape((2 * n_chunks, CH, 128))
    wx_both = {d: place.forward(d, wx_one[d]) for d in range(slots)}

    def hand_on(local, forward):
        low = local.astype(bf16)
        for _ in range(pieces - 2):
            came = along_sequence(low, pieces, forward)
            low = (local + whole_alpha * came.astype(f32)).astype(bf16)
        return along_sequence(low, pieces, forward)

    (one, two, pair_here, wx_here, wx_one, wx_two, wx_both, normed_both, hv, rv, al, bc_act, bc_turned, cw, wide_since, c_low, flags, bc_ext, bc_pre,
     dt_in, log_step) = tie(
        one, two, pair_here, wx_here, wx_one, wx_two, wx_both, normed_both, hv, rv, al, bc_act, bc_turned, cw, wide_since, c_low, flags,
        bc_ext, bc_pre, dt_in, log_step)
    wx_items = []
    for d in range(slots):
        wx_items += place.items(d, wx_here[d], wx_one[d], wx_two[d], wx_both[d])

    pair_here[3] = around(pair_here[0], 3)
    both_k[0] = place.forward(0, one[0])
    one[1], two[1] = place.unit(1, pair_here[1])
    one[2] = across(pair_here[2], place.bits[0])
    x_ext, wx = project(normed_both, 0, at, wx_items, 0, channels)
    x_ext = x_ext.reshape((2, HALO + length, channels))

    x_ext, one, two, both_k, pair_here = tie(x_ext, one, two, both_k, pair_here)
    one[3], two[3] = place.unit(3, pair_here[3])
    two[2] = across(pair_here[2], place.bits[1])
    both_k[1] = place.forward(1, one[1])
    y_here, states = scan_fwd(hv, flags, rv, al, bc_act, bc_turned, x_ext, cw, CH)

    y_here, states, one, two, both_k = tie(y_here, states, one, two, both_k)
    state_in = hand_on(states[:, -1], True)
    both_k[2], both_k[3] = place.forward(2, one[2]), place.forward(3, one[3])
    pair_items = []
    for d in range(slots):
        pair_items += place.items(d, pair_here[d], one[d], two[d], both_k[d])
    tokens = x_in.astype(f32)

    gate_in, wz = project(normed_both, HALO, at, pair_items, 0, channels)
    mixed_grad, wo = project(cot, 0, at, pair_items, 1, channels)
    flat = lambda v: v.reshape((2 * length, -1))
    y, sums = gate_sums(flat(y_here), flat(wide_since), flat(c_low), state_in, gate_in, mixed_grad, gain_row)
    mixed, gate_grad, y_grad, gain_grad, state_grad = gate_grads(
        y, flat(wide_since), flat(c_low), gate_in, mixed_grad, gain_row, sums, swap(sums), all_channels)
    y_grad = y_grad.reshape((2, length, channels))
    state_grad = hand_on(state_grad, False)
    parts = [
        weight_parts(at, [normed_turned, cot_turned], [[gate_grad], [mixed]], group, own_rows, half_channels, flip)
        for flip, group in enumerate(groups)
    ]
    parts, y_grad, mixed, gate_grad, state_grad = tie(parts, y_grad, mixed, gate_grad, state_grad)
    pair_came = [place.first_exchange(i, parts[i][1]) for i in range(2)]


    def backward(piece):
        return scan_bwd(
            hv, flags, rv, al, bc_act, bc_turned, x_ext, cw, y_grad, states, state_in, state_grad, CH, piece, 1
        )

    back_other = backward(1)
    dbc_other = swap(back_other[3][0])
    head_other = along_sequence(back_other[2], pieces, False)
    back_other, y_grad = tie(back_other, y_grad)
    back_own = backward(0)
    pair_came, back_own, dbc_other, head_other = tie(pair_came, back_own, dbc_other, head_other)
    terms = [place.second_term(parts[i][0], pair_came[i]) for i in range(2)]
    pair_last = [place.second_exchange(i, terms[i]) for i in range(2)]

    head = jnp.concatenate([along_sequence(back_own[2], pieces, False), head_other])
    place_back = (pick * first_lanes).T.astype(bf16)
    bc_dpre, dt_low, bc_small, packed = small_grads(
        back_own[3], dbc_other, bc_pre, bc_ext, flags, back_own[4], back_other[4], back_own[5], back_other[5],
        log_step.reshape((2, length, 128)), dt_in, lanes, place_back, back_own[6], back_other[6], gain_grad)

    def past_end(begin, taps):
        total = jnp.zeros((begin.shape[0], HALO, begin.shape[2]), f32)
        for k in range(1, taps.shape[0]):
            moved = jnp.pad(begin[:, :k], ((0, 0), (HALO - k, 0), (0, 0)))
            total = total + taps[k] * moved * flags[: begin.shape[0], length - HALO :, 3 + k : 4 + k]
        return total

    fix = past_end(head, own[:4])
    x_low = [
        lax.dynamic_update_slice(back[0][0], (back[1][0] + fix[i]).astype(bf16), (length - HALO, 0))
        for i, back in enumerate((back_own, back_other))
    ]
    x_low, bc_dpre, dt_low, bc_small, packed = tie(x_low, bc_dpre, dt_low, bc_small, packed)
    bc_head = along_sequence(bc_dpre[:8], pieces, False)
    x_parts = [
        weight_parts(at, [normed_turned], [x_low], group, own_rows, half_channels, flip)
        for flip, group in enumerate(groups)
    ]
    x_parts, x_low, pair_last, bc_head, bc_dpre, dt_low = tie(x_parts, x_low, pair_last, bc_head, bc_dpre, dt_low)
    x_came = [place.first_exchange(i, x_parts[i][1]) for i in range(2)]
    pair_sums = place.slot_parts([p[0] for p in parts], pair_came, pair_last, groups)
    pair_others = {d: around(pair_sums[d].astype(bf16), -d) for d in range(1, slots - 1)}
    normed_grad, normed_grad_other, thin_part = normed_grads(
        bc_dpre, bc_head, flags, cbc, dt_low, normed_turned, x_low, gate_grad, wx, wz, thin)

    x_came, thin_part, pair_others, pair_sums, normed_grad, normed_grad_other, packed, bc_small = tie(
        x_came, thin_part, pair_others, pair_sums, normed_grad, normed_grad_other, packed, bc_small)
    x_terms = [place.second_term(x_parts[i][0], x_came[i]) for i in range(2)]
    x_last = [place.second_exchange(i, x_terms[i]) for i in range(2)]
    pair_others[slots - 1] = around(pair_sums[slots - 1].astype(bf16), 1)
    thin_part = place.ordered_sum(thin_part)
    x_grad, gain_part = x_grads(normed_grad, swap(normed_grad_other), x_in, cotangent, gain)
    gain_part = jnp.sum(gain_part, axis=0).reshape((-1, bc_width))
    gain_rows = gain_part.shape[0]
    bc_small = jnp.concatenate([bc_small[:5], gain_part, jnp.zeros((11 - gain_rows, bc_width), f32)], axis=0)
    bc_small = bc_small + swap(bc_small)
    packed = jnp.concatenate([packed, bc_small], axis=1)
    low, high = place.bits
    packed = packed + across(packed, low)
    thin_part = place.half_rows(thin_part, low)

    x_sums = place.slot_parts([p[0] for p in x_parts], x_came, x_last, groups)
    x_others = [around(x_sums[1].astype(bf16), -1)]
    x_sums, x_others, packed, thin_part, x_grad, pair_sums, pair_others = tie(
        x_sums, x_others, packed, thin_part, x_grad, pair_sums, pair_others)
    x_others.append(around(x_sums[2].astype(bf16), -2))
    pair_grads = place.to_owner(pair_sums[0], list(pair_others.values()))
    packed = packed + across(packed, high)
    thin_grad = place.half_rows(thin_part, high)
    packed, thin_grad, x_others, x_sums, pair_grads, mixed = tie(
        packed, thin_grad, x_others, x_sums, pair_grads, mixed)

    bc_small = packed[:, channels:]
    packed = packed[:, :channels].reshape((16, slots, half_channels))

    def block(index):
        return lax.dynamic_index_in_dim(packed, index % slots, 1, keepdims=False)

    own_sums = jnp.concatenate([block(slot), bc_small], axis=1)
    for d in range(1, slots):
        own_sums = own_sums + around(jnp.concatenate([block(slot + d), bc_small], axis=1), d)
    branch, branch_other = branch_parts(mixed, wo)
    x_others += [around(x_sums[d].astype(bf16), -d) for d in range(3, slots)]
    branch, branch_other, x_others, own_sums, thin_grad = tie(branch, branch_other, x_others, own_sums, thin_grad)
    thin_grad = place.sum_slots(thin_grad)
    block_out = (tokens + branch + swap(branch_other).astype(f32)).astype(bf16)
    packed = own_sums[:, :half_channels]
    bc_small = own_sums[:, half_channels:]
    packed = place.ordered(0, packed, swap(packed), 1).reshape((16, slot_channels))
    by_head = packed[6:9].reshape((3, slot_heads, 64))
    norm_gain_grad = lax.dynamic_slice_in_dim(
        bc_small[5 : 5 + gain_rows].reshape((features,)), lax.axis_index("dp") * own_rows, own_rows, 0)
    w_z_grad, w_out_grad = pair_grads
    w_bc_grad = thin_grad[:, :bc_width]
    w_dt_grad = lax.dynamic_slice_in_dim(thin_grad, bc_width + slot * slot_heads, slot_heads, 1)
    w_x_grad = place.to_owner(x_sums[0], x_others)[0]
    return (
        block_out,
        x_grad,
        norm_gain_grad,
        w_x_grad,
        w_z_grad,
        w_bc_grad,
        w_dt_grad,
        packed[:4],
        packed[4],
        bc_small[:4],
        bc_small[4],
        by_head[1, :, 0],
        by_head[2, :, 0],
        jnp.sum(by_head[0], axis=1),
        packed[5],
        w_out_grad.T,
    )


def solution(mesh):
    rows = P(("dp", "tensor"), None)
    both = P("dp", "tensor")
    heads = P("tensor")
    in_specs = (
        rows, P("dp", None), P("dp"), both, both, P("dp", None), both, P(None, "tensor"), heads,
        P(), P(), heads, heads, heads, heads, P("tensor", "dp"), rows,
    )
    out_specs = (
        rows, rows, P("dp"), both, both, P("dp", None), both, P(None, "tensor"), heads,
        P(), P(), heads, heads, heads, heads, P("tensor", "dp"),
    )
    return jax.shard_map(
        on_device, mesh=mesh, in_specs=in_specs, out_specs=out_specs, check_vma=False
    )
```
